32 devices in a mesh: expert: 8 (over y, x, core), shard: 4 (over z).
Axes of the slice: x: 2, y: 2, z: 4, core: 2. Of those that a mesh axis runs over, the one named last changes fastest.
Arguments:
- embedded: bfloat16 [8192, 1024], P(('expert', 'shard')), may hold values from -1 to 1
- document_numbers: int32 [32, 256], P(('expert', 'shard')), may hold values from 0 to 4, as said below
- expert_ids: int32 [8192, 8], P(('expert', 'shard')), may hold values from 0 to 31, all different within a row; in each aligned block of 256 rows (0 to 255, 256 to 511, ...) at most 128 rows name the same one
- attn_gain: float32 [1024], P(('expert', 'shard')), may hold values from 0.5 to 1.5
- ffn_gain: float32 [1024], P(('expert', 'shard')), may hold values from 0.5 to 1.5
- w_query: float32 [1024, 1024], P(('expert', 'shard')), may hold values from -0.75 to 0.75
- key_projection: float32 [1024, 512], P(('expert', 'shard')), may hold values from -0.75 to 0.75
- value_projection: float32 [1024, 512], P(('expert', 'shard')), may hold values from -0.1875 to 0.1875
- w_out: float32 [1024, 1024], P(('expert', 'shard')), may hold values from -3 to 3
- w_router: float32 [1024, 32], P(('expert', 'shard')), may hold values from -0.09375 to 0.09375
- expert_in: bfloat16 [32, 1024, 1024], P('expert', 'shard'), may hold values from -0.1875 to 0.1875
- expert_out: bfloat16 [32, 512, 1024], P('expert', 'shard'), may hold values from -4 to 4
- cotangent: bfloat16 [8192, 1024], P(('expert', 'shard')), may hold values from -6 to 6
Outputs:
- output: bfloat16 [8192, 1024], P(('expert', 'shard'))
- grad_embedded: bfloat16 [8192, 1024], P(('expert', 'shard'))
- grad_attn_gain: float32 [1024], P(('expert', 'shard'))
- grad_ffn_gain: float32 [1024], P(('expert', 'shard'))
- grad_w_query: float32 [1024, 1024], P(('expert', 'shard'))
- grad_w_key: float32 [1024, 512], P(('expert', 'shard'))
- grad_w_value: float32 [1024, 512], P(('expert', 'shard'))
- grad_w_out: float32 [1024, 1024], P(('expert', 'shard'))
- grad_w_router: float32 [1024, 32], P(('expert', 'shard'))
- grad_expert_in: float32 [32, 1024, 1024], P('expert', 'shard')
- grad_expert_out: float32 [32, 512, 1024], P('expert', 'shard')
The draws below stay inside these ranges and needn't reach their ends.
Inputs may be any that keep to these rules, and one draw needn't show every extreme that they name: `expert_ids`: each row names 8 different experts. In the rows of one device (aligned blocks of 256 rows) no expert is named by more than 128 rows, and in every draw some expert is named by exactly 128 rows of some device. `document_numbers`: within each sequence the document numbers start at 0 and rise by one at each new document; every document has 32 to 128 positions, and each sequence has one document of exactly 128 positions.
All inputs are finite; a program needn't handle non-finite values.
Results may differ from the reference program's by a relative error of at most 0.015.
The reference program's roundings to bfloat16 on the way count: a program that leaves them out, or rounds other values in their place, can miss the bound.
Values may be sent and summed in bfloat16 or wider, within the bound.
No kernel may reach another device: no remote copies, remote signals or barrier semaphores. Data moves between devices by JAX's collectives and lax.ppermute only.
A program may use at most 192 MiB of HBM per device.

```python
import math
from functools import partial
import jax
import jax.numpy as jnp
import numpy as np
from jax import lax

MODEL_WIDTH = 1024
QUERY_HEADS = 16
KEY_VALUE_HEADS = 8
HEAD_SIZE = 64
FF = 512
EXPERTS = 32
TOPK = 8
TOK_DEV = 256
SEQ = 256
SEQS = 32
TOKENS = 8192
CAP = 128


def one_packing(key):
    key_count, key_cuts, key_place = jax.random.split(key, 3)
    half_len = SEQ // 2
    least_len = SEQ // 8
    pieces = jax.random.randint(key_count, (), 1, 5).astype(jnp.int32)
    spare = (half_len - pieces * least_len).astype(jnp.int32)
    slot_index = jnp.arange(3, dtype=jnp.int32)
    cuts = jax.random.randint(key_cuts, (3,), 0, spare + 1).astype(jnp.int32)
    cuts = jnp.where(slot_index < pieces - 1, cuts, spare)
    cuts = jnp.sort(cuts)
    bounds = jnp.concatenate([jnp.zeros((1,), jnp.int32), cuts, spare[None]])
    extras = bounds[1:] - bounds[:-1]
    four_index = jnp.arange(4, dtype=jnp.int32)
    small_lens = jnp.where(four_index < pieces, least_len + extras, 0).astype(jnp.int32)
    place = jax.random.randint(key_place, (), 0, pieces + 1).astype(jnp.int32)
    five_index = jnp.arange(5, dtype=jnp.int32)
    below = small_lens[jnp.clip(five_index, 0, 3)]
    above = small_lens[jnp.clip(five_index - 1, 0, 3)]
    lens = jnp.where(five_index < place, below, jnp.where(five_index == place, half_len, above)).astype(jnp.int32)
    ends = jnp.cumsum(lens).astype(jnp.int32)
    positions = jnp.arange(SEQ, dtype=jnp.int32)
    return jnp.sum((positions[:, None] >= ends[None, :4]).astype(jnp.int32), axis=1).astype(jnp.int32)


def draw_document_numbers(key, part):
    base = jax.random.fold_in(key, 7)
    row_keys = jax.random.split(base, SEQS)
    return jax.vmap(one_packing)(row_keys)


def with_spikes(values, key, source, target, blocks, factor):
    owner, partner = [(jnp.arange(values.shape[axis_at]) // (values.shape[axis_at] // blocks)).reshape([-1 if axis == axis_at else 1 for axis in range(values.ndim)]) for axis_at in (source, target)]
    chosen = jax.random.permutation(key, blocks)[partner]
    strong = (owner == chosen) | (owner == (partner + blocks // 2) % blocks)
    return jnp.where(strong, factor * values, values)


def shard_levels(stream_key, dims, cuts, smallest, top_value):
    factor_of = 1.0
    for position, blocks in cuts:
        steps = jax.random.uniform(jax.random.fold_in(jax.random.fold_in(stream_key, 6), position), (blocks,), jnp.float32, smallest / len(cuts), top_value / len(cuts))
        factor_of = factor_of * jnp.repeat(jnp.exp(steps), dims[position] // blocks).reshape((-1,) + (1,) * (len(dims) - 1 - position))
    return factor_of


def shared_out(rng, own, number, rows, number_of, top, bound, skew):
    order = jax.random.permutation(rng, number_of)
    crowded, usual = portions_of(number_of, rows * top, bound, skew, True), portions_of(number_of, rows * top, bound, skew, False)
    places = jnp.arange(number_of)

    def named(sizes, offset_by):
        used = int((sizes > 0).sum())
        fixed = max(1, used // 4)
        moved = fixed + (places - fixed + offset_by * (used - fixed)) % max(1, number_of - fixed)
        return jnp.zeros((number_of,), jnp.int32).at[order[jnp.where(places < fixed, places, moved)]].set(jnp.asarray(sizes, jnp.int32))

    sizes = jnp.where(number % 4 == 0, named(crowded, number // 4), named(usual, number - number // 4 - 1))
    mixed = jax.random.permutation(jax.random.fold_in(own, 3), number_of)
    donor, receiver = mixed[0:number_of // 2 * 2:2], mixed[1:number_of // 2 * 2:2]
    slack = jnp.minimum(sizes[donor] - 1, bound - sizes[receiver]) // 2
    slack = jnp.where((donor == order[0]) | (receiver == order[0]) | (sizes[receiver] == 0), 0, jnp.maximum(slack, 0))
    moved = jax.random.randint(jax.random.fold_in(own, 4), (number_of // 2,), 0, 1 << 20) % (slack + 1)
    sizes = sizes.at[donor].add(-moved).at[receiver].add(moved)
    items = jnp.searchsorted(jnp.cumsum(sizes), jnp.arange(rows * top), side="right").astype(jnp.int32)
    table = items.reshape(top, rows).T
    table = table[jax.random.permutation(jax.random.fold_in(own, 1), rows)]
    offset_by = jax.random.randint(jax.random.fold_in(own, 2), (rows, 1), 0, top)
    return jnp.take_along_axis(table, (jnp.arange(top)[None, :] + offset_by) % top, axis=1)


def portions_of(amount, total, limit, lean, full):
    loads = [(1 << 20) // math.isqrt(rank ** lean) + 1 for rank in range(1, amount + 1)]
    largest = limit if full else min(limit, max(-(-total // amount), total * loads[0] // sum(loads)))
    least = 1 if total - largest >= amount - 1 else 0
    given, spare = [largest] + [least] * (amount - 1), total - largest - least * (amount - 1)
    while spare > 0:
        movable = [i for i in range(1, amount) if given[i] < largest] or [i for i in range(1, amount) if given[i] < limit]
        whole, left = sum([loads[i] for i in movable]), spare
        for i in movable:
            extra = min(limit - given[i], max(1, left * loads[i] // whole), spare)
            given[i] = given[i] + extra
            spare = spare - extra
    return np.array(given)


def noise(rng, dims, spread, bound, shards=(), held_as=jnp.bfloat16):
    values = spread * jax.random.normal(rng, dims, jnp.float32)
    if shards:
        values = values * shard_levels(rng, dims, shards, -0.22, 0.18)
    return jnp.clip(values, -bound, bound).astype(held_as)


def gaussian_with(key, extent, scale, limit, cuts, heavy, kind=jnp.bfloat16):
    result = scale * jax.random.normal(key, extent, jnp.float32)
    if cuts:
        result = result * shard_levels(key, extent, cuts, -0.22, 0.18)
    return jnp.clip(with_spikes(result, jax.random.fold_in(key, 3), *heavy), -limit, limit).astype(kind)


def setup_inputs(seed: int = 0) -> dict:
    key_list = jax.random.split(jax.random.key(seed), 14)
    embedded = gaussian_with(key_list[0], (TOKENS, MODEL_WIDTH), 0.0833, 1.0, ((0, 32),), (0, 1, 32, 2.75))
    document_numbers = draw_document_numbers(jax.random.fold_in(key_list[13], 71), 0)
    expert_ids_keys = jax.random.split(jax.random.fold_in(key_list[2], 1), TOKENS // TOK_DEV)
    expert_ids_turns = jax.random.permutation(jax.random.fold_in(key_list[2], 3), TOKENS // TOK_DEV)
    expert_ids = jax.vmap(lambda own, number: shared_out(jax.random.fold_in(key_list[2], 2), own, number, TOK_DEV, EXPERTS, TOPK, CAP, 1))(expert_ids_keys, expert_ids_turns).reshape((TOKENS, TOPK))
    attn_gain = jnp.clip(1.0 + 0.1 * jax.random.normal(key_list[3], (MODEL_WIDTH,), jnp.float32), 0.5, 1.5)
    ffn_gain = jnp.clip(1.0 + 0.1 * jax.random.normal(key_list[4], (MODEL_WIDTH,), jnp.float32), 0.5, 1.5)
    w_query = noise(key_list[5], (MODEL_WIDTH, QUERY_HEADS * HEAD_SIZE), (MODEL_WIDTH // 16) ** -0.5, 0.75, ((0, 32),), jnp.float32)
    key_projection = noise(key_list[6], (MODEL_WIDTH, KEY_VALUE_HEADS * HEAD_SIZE), (MODEL_WIDTH // 16) ** -0.5, 0.75, ((0, 32),), jnp.float32)
    value_projection = noise(key_list[7], (MODEL_WIDTH, KEY_VALUE_HEADS * HEAD_SIZE), MODEL_WIDTH ** -0.5, 0.1875, ((0, 32),), jnp.float32)
    w_out = noise(key_list[8], (QUERY_HEADS * HEAD_SIZE, MODEL_WIDTH), 4 ** -0.5, 3.0, ((0, 32),), jnp.float32)
    w_router = noise(key_list[9], (MODEL_WIDTH, EXPERTS), (4 * MODEL_WIDTH) ** -0.5, 0.09375, ((0, 32),), jnp.float32)
    expert_in = noise(key_list[10], (EXPERTS, MODEL_WIDTH, 2 * FF), MODEL_WIDTH ** -0.5, 0.1875, ((0, 8), (1, 4)))
    expert_out = noise(key_list[11], (EXPERTS, FF, MODEL_WIDTH), 2 ** -0.5, 4.0, ((0, 8), (1, 4)))
    cotangent = noise(key_list[12], (TOKENS, MODEL_WIDTH), 1.0, 6.0, ((0, 32),))
    return dict(embedded=embedded, document_numbers=document_numbers, expert_ids=expert_ids, attn_gain=attn_gain, ffn_gain=ffn_gain, w_query=w_query, key_projection=key_projection, value_projection=value_projection, w_out=w_out, w_router=w_router, expert_in=expert_in, expert_out=expert_out, cotangent=cotangent)


@jax.custom_vjp
def lower_precision(v):
    return lax.optimization_barrier(v.astype(jnp.bfloat16)).astype(jnp.float32)

@jax.custom_vjp
def lower_precision_backward(v):
    return v

def low_keep(v):
    return (lower_precision(v), None)

def low_pass(kept, grad):
    return (grad,)

def back_keep(v):
    return (v, None)

def back_low(kept, grad):
    return (lower_precision(grad),)
lower_precision.defvjp(low_keep, low_pass)
lower_precision_backward.defvjp(back_keep, back_low)
embed_scale = 12.0
attn_scale = 0.015625
resid_scale = 0.22
norm_eps = 1e-06
rope_base = 10000.0
highest = lax.Precision.HIGHEST

def matmul(left, right):
    return jnp.dot(left, right, precision=highest)

def rms_norm(value_heads, gain):
    return value_heads * lax.rsqrt(lax.optimization_barrier(jnp.mean(value_heads * value_heads, axis=-1, keepdims=True)) + norm_eps) * gain

def rope_tables(segments):
    sequence_length = segments.shape[0]
    key_index = jnp.arange(sequence_length, dtype=jnp.int32)
    change = jnp.concatenate([jnp.ones((1,), jnp.bool_), segments[1:] != segments[:-1]])
    begins = lax.cummax(jnp.where(change, key_index, 0), axis=0)
    places = (key_index - begins).astype(jnp.float32)
    freqs = rope_base ** (-2.0 * jnp.arange(HEAD_SIZE // 2, dtype=jnp.float32) / HEAD_SIZE)
    angles = places[:, None] * freqs[None, :]
    return (jnp.cos(angles), jnp.sin(angles))

def apply_rotation(value_heads, cosine_table, sine_table):
    halfway = value_heads.shape[-1] // 2
    first_half = value_heads[..., :halfway]
    second_half = value_heads[..., halfway:]
    cos_part = cosine_table[:, None, :]
    sin_part = sine_table[:, None, :]
    return jnp.concatenate([first_half * cos_part - second_half * sin_part, second_half * cos_part + first_half * sin_part], axis=-1)

def sequence_attention(unrotated_query, unrotated_key, projected_value, segments):
    sequence_length = segments.shape[0]
    cosine_table, sine_table = rope_tables(segments)
    query_heads = lower_precision(apply_rotation(lower_precision_backward(unrotated_query).reshape(sequence_length, QUERY_HEADS, HEAD_SIZE), cosine_table, sine_table))
    key_heads = lower_precision(apply_rotation(lower_precision_backward(unrotated_key).reshape(sequence_length, KEY_VALUE_HEADS, HEAD_SIZE), cosine_table, sine_table))
    value_heads = lower_precision(lower_precision_backward(projected_value)).reshape(sequence_length, KEY_VALUE_HEADS, HEAD_SIZE)
    query_heads = query_heads.reshape(sequence_length, KEY_VALUE_HEADS, QUERY_HEADS // KEY_VALUE_HEADS, HEAD_SIZE)
    scores = lower_precision_backward(jnp.einsum('qhgd,khd->hgqk', query_heads, key_heads, precision=highest) * attn_scale)
    key_index = jnp.arange(sequence_length, dtype=jnp.int32)
    allowed = (key_index[None, :] <= key_index[:, None]) & (segments[None, :] == segments[:, None])
    scores = jnp.where(allowed, scores, -1e+30)
    shifted = scores - lax.optimization_barrier(jnp.max(scores, axis=-1, keepdims=True))
    exps = jnp.exp(shifted)
    probs = exps / lax.optimization_barrier(jnp.sum(exps, axis=-1, keepdims=True))
    mixed_heads_output = jnp.einsum('hgqk,khd->qhgd', lower_precision(probs), value_heads, precision=highest)
    return lower_precision(lower_precision_backward(mixed_heads_output.reshape(sequence_length, QUERY_HEADS * HEAD_SIZE)))

def attend_single_sequence(packed):
    return sequence_attention(packed[0], packed[1], packed[2], packed[3])

def slot_tables(expert_ids):
    flat_ids = expert_ids.reshape(-1)
    count_all = flat_ids.shape[0]
    matches = (flat_ids[:, None] == jnp.arange(EXPERTS, dtype=jnp.int32)[None, :]).astype(jnp.int32)
    before = jnp.cumsum(matches, axis=0).astype(jnp.int32) - 1
    ranking = lax.optimization_barrier(jnp.sum(before * matches, axis=1)).astype(jnp.int32)
    target = flat_ids * CAP + ranking
    source = jnp.zeros((EXPERTS * CAP,), jnp.int32).at[target].set(jnp.arange(count_all, dtype=jnp.int32))
    filled = jnp.zeros((EXPERTS * CAP,), jnp.int32).at[target].set(jnp.ones((count_all,), jnp.int32))
    return (target, source, filled)

def layer(document_numbers, expert_ids, embedded, attn_gain, ffn_gain, w_query, key_projection, value_projection, w_out, w_router, expert_in, expert_out):
    resid = embed_scale * embedded
    normed = lower_precision(rms_norm(resid, lower_precision(attn_gain)))
    unrotated_query = matmul(normed, lower_precision(w_query))
    unrotated_key = matmul(normed, lower_precision(key_projection))
    projected_value = matmul(normed, lower_precision(value_projection))
    sequence_count = document_numbers.shape[0]
    packed_length = document_numbers.shape[1]
    mixed_heads_output = lax.map(jax.checkpoint(attend_single_sequence), (unrotated_query.reshape(sequence_count, packed_length, QUERY_HEADS * HEAD_SIZE), unrotated_key.reshape(sequence_count, packed_length, KEY_VALUE_HEADS * HEAD_SIZE), projected_value.reshape(sequence_count, packed_length, KEY_VALUE_HEADS * HEAD_SIZE), document_numbers))
    mixed_heads_output = mixed_heads_output.reshape(sequence_count * packed_length, QUERY_HEADS * HEAD_SIZE)
    middle = resid + resid_scale * lower_precision_backward(matmul(mixed_heads_output, lower_precision(w_out)))
    normed2 = lower_precision(rms_norm(middle, lower_precision(ffn_gain)))
    logits = lower_precision_backward(matmul(normed2, lower_precision(w_router)))
    chosen = jnp.take_along_axis(logits, expert_ids, axis=1)
    exps = jnp.exp(chosen - lax.optimization_barrier(jnp.max(chosen, axis=1, keepdims=True)))
    gates = exps / lax.optimization_barrier(jnp.sum(exps, axis=1, keepdims=True))
    gates_flat = gates.reshape(-1)
    blocks = expert_ids.shape[0] // TOK_DEV
    targets, sources, filled = jax.vmap(slot_tables)(expert_ids.reshape(blocks, TOK_DEV, TOPK))
    offsets = (jnp.arange(blocks, dtype=jnp.int32) * (TOK_DEV * TOPK))[:, None]
    global_src = (sources + offsets).astype(jnp.int32).reshape(blocks, EXPERTS, CAP).transpose(1, 0, 2).reshape(EXPERTS, blocks * CAP)
    alive_all = filled.reshape(blocks, EXPERTS, CAP).transpose(1, 0, 2).reshape(EXPERTS, blocks * CAP).astype(jnp.float32)

    def expert_step(total_sum, packed):
        weight_in, weight_out, slot_src, alive = packed
        tokens_of = slot_src // TOPK
        rows_in = lower_precision_backward(normed2[tokens_of])
        gate_up = lower_precision_backward(matmul(rows_in, weight_in))
        hidden = lower_precision(jax.nn.silu(gate_up[:, :FF]) * gate_up[:, FF:])
        produced = lower_precision(lower_precision_backward(matmul(hidden, weight_out)))
        weights = gates_flat[slot_src] * alive
        return (total_sum.at[tokens_of].add(weights[:, None] * produced), None)
    moe, unused = lax.scan(jax.checkpoint(expert_step), jnp.zeros_like(resid), (expert_in, expert_out, global_src, alive_all))
    return middle + resid_scale * moe

def reference(embedded, document_numbers, expert_ids, attn_gain, ffn_gain, w_query, key_projection, value_projection, w_out, w_router, expert_in, expert_out, cotangent):
    forward = partial(layer, document_numbers, expert_ids)
    output, pullback = jax.vjp(forward, embedded.astype(jnp.float32), attn_gain, ffn_gain, w_query, key_projection, value_projection, w_out, w_router, expert_in.astype(jnp.float32), expert_out.astype(jnp.float32))
    grads = pullback(cotangent.astype(jnp.float32))
    return (output.astype(jnp.bfloat16), grads[0].astype(jnp.bfloat16), grads[1], grads[2], grads[3], grads[4], grads[5], grads[6], grads[7], grads[8], grads[9])
```

```python
import jax
import jax.numpy as jnp
from jax import lax
from jax.sharding import PartitionSpec as P

MODEL_WIDTH = 1024
QUERY_HEADS = 16
KEY_VALUE_HEADS = 8
HEAD_SIZE = 64
FF = 512
EXPERTS = 32
TOPK = 8
CAP = 128


embed_scale = 12.0
attn_scale = 0.015625
resid_scale = 0.22
norm_eps = 1e-06
rope_base = 10000.0


def rope_tables(segments):
    sequence_length = segments.shape[0]
    key_index = jnp.arange(sequence_length, dtype=jnp.int32)
    change = jnp.concatenate([jnp.ones((1,), jnp.bool_), segments[1:] != segments[:-1]])
    begins = lax.cummax(jnp.where(change, key_index, 0), axis=0)
    places = (key_index - begins).astype(jnp.float32)
    freqs = rope_base ** (-2.0 * jnp.arange(HEAD_SIZE // 2, dtype=jnp.float32) / HEAD_SIZE)
    angles = places[:, None] * freqs[None, :]
    return (jnp.cos(angles), jnp.sin(angles))


def apply_rotation(value_heads, cosine_table, sine_table):
    halfway = value_heads.shape[-1] // 2
    first_half = value_heads[..., :halfway]
    second_half = value_heads[..., halfway:]
    cos_part = cosine_table[:, None, :]
    sin_part = sine_table[:, None, :]
    return jnp.concatenate(
        [
            first_half * cos_part - second_half * sin_part,
            second_half * cos_part + first_half * sin_part,
        ],
        axis=-1,
    )


def reverse_rotation(grads, cosine_table, sine_table):
    halfway = grads.shape[-1] // 2
    first_half = grads[..., :halfway]
    second_half = grads[..., halfway:]
    cos_part = cosine_table[:, None, :]
    sin_part = sine_table[:, None, :]
    return jnp.concatenate(
        [
            first_half * cos_part + second_half * sin_part,
            second_half * cos_part - first_half * sin_part,
        ],
        axis=-1,
    )


def norm_forward(value_heads):
    inverse = lax.rsqrt(jnp.mean(value_heads * value_heads, axis=1, keepdims=True) + norm_eps)
    return (value_heads * inverse, inverse)


def norm_backward(upstream, unit_values, inverse, gain):
    scaled = upstream * gain
    grad_values = inverse * (
        scaled - unit_values * jnp.mean(scaled * unit_values, axis=1, keepdims=True)
    )
    return (grad_values, jnp.sum(upstream * unit_values, axis=0))


def slot_tables(expert_ids):
    flat_ids = expert_ids.reshape(-1)
    count_all = flat_ids.shape[0]
    matches = (flat_ids[:, None] == jnp.arange(EXPERTS, dtype=jnp.int32)[None, :]).astype(jnp.int32)
    before = jnp.cumsum(matches, axis=0) - 1
    ranking = jnp.sum(before * matches, axis=1)
    target = flat_ids * CAP + ranking
    source = (
        jnp.zeros((EXPERTS * CAP,), jnp.int32)
        .at[target]
        .set(jnp.arange(count_all, dtype=jnp.int32))
    )
    filled = (
        jnp.zeros((EXPERTS * CAP,), jnp.int32).at[target].set(jnp.ones((count_all,), jnp.int32))
    )
    return (target, source, filled)


def silu_parts(gate_up):
    gate_part = gate_up[..., :FF]
    up_part = gate_up[..., FF:]
    sigmoid_gate = jax.nn.sigmoid(gate_part)
    hidden = (gate_part * sigmoid_gate * up_part).astype(jnp.bfloat16)
    return (gate_part, up_part, sigmoid_gate, hidden)


def per_device_general(
    embedded,
    document_numbers,
    expert_ids,
    attn_gain,
    ffn_gain,
    w_query,
    key_projection,
    value_projection,
    w_out,
    w_router,
    expert_in,
    expert_out,
    cotangent,
):
    mixer = (
        lax.all_gather(attn_gain.astype(jnp.bfloat16), ("expert", "shard"), axis=0, tiled=True),
        lax.all_gather(ffn_gain.astype(jnp.bfloat16), ("expert", "shard"), axis=0, tiled=True),
        lax.all_gather(w_query.astype(jnp.bfloat16), ("expert", "shard"), axis=0, tiled=True),
        lax.all_gather(
            key_projection.astype(jnp.bfloat16), ("expert", "shard"), axis=0, tiled=True
        ),
        lax.all_gather(
            value_projection.astype(jnp.bfloat16), ("expert", "shard"), axis=0, tiled=True
        ),
        lax.all_gather(w_out.astype(jnp.bfloat16), ("expert", "shard"), axis=0, tiled=True),
        lax.all_gather(w_router.astype(jnp.bfloat16), ("expert", "shard"), axis=0, tiled=True),
    )
    gain_attn, gain_ffn, query_w, key_w, value_w, out_w, router_w = mixer
    full_in, full_out = (
        lax.all_gather(expert_in, "shard", axis=1, tiled=True),
        lax.all_gather(expert_out, "shard", axis=1, tiled=True),
    )
    sequence_length = embedded.shape[0]
    query_groups = QUERY_HEADS // KEY_VALUE_HEADS
    owners = lax.axis_size("expert")
    local_count = EXPERTS // owners
    received = owners * CAP
    resid = embed_scale * embedded.astype(jnp.float32)
    unit_attn, inverse_attn = norm_forward(resid)
    normed = (unit_attn * gain_attn.astype(jnp.float32)).astype(jnp.bfloat16)
    unrotated_query = jnp.dot(normed, query_w, preferred_element_type=jnp.float32)
    unrotated_key = jnp.dot(normed, key_w, preferred_element_type=jnp.float32)
    projected_value = jnp.dot(normed, value_w, preferred_element_type=jnp.float32)
    segments = document_numbers[0]
    cosine_table, sine_table = rope_tables(segments)
    query_heads = (
        apply_rotation(
            unrotated_query.reshape(sequence_length, QUERY_HEADS, HEAD_SIZE),
            cosine_table,
            sine_table,
        )
        .astype(jnp.bfloat16)
        .reshape(sequence_length, KEY_VALUE_HEADS, query_groups, HEAD_SIZE)
    )
    key_heads = apply_rotation(
        unrotated_key.reshape(sequence_length, KEY_VALUE_HEADS, HEAD_SIZE), cosine_table, sine_table
    ).astype(jnp.bfloat16)
    value_heads = projected_value.astype(jnp.bfloat16).reshape(
        sequence_length, KEY_VALUE_HEADS, HEAD_SIZE
    )
    block_rows = min(512, sequence_length)
    starts = jnp.arange(sequence_length // block_rows, dtype=jnp.int32) * block_rows
    key_index = jnp.arange(sequence_length, dtype=jnp.int32)

    def block_scores(first_row):
        row_index = first_row + jnp.arange(block_rows, dtype=jnp.int32)
        raw_scores = (
            jnp.einsum("qhgd,khd->hgqk", query_heads, key_heads, preferred_element_type=jnp.float32)
            * attn_scale
        )
        allowed = (key_index[None, :] <= row_index[:, None]) & (
            segments[None, :] == segments[:, None]
        )
        return (jnp.where(allowed, raw_scores, -1e30), query_heads)

    def attend_block(first_row):
        scores, query_rows = block_scores(first_row)
        row_max = jnp.max(scores, axis=-1, keepdims=True)
        exps = jnp.exp(scores - row_max)
        totals = jnp.sum(exps, axis=-1, keepdims=True)
        weights = (exps / totals).astype(jnp.bfloat16)
        mixed_rows = jnp.einsum(
            "hgqk,khd->qhgd", weights, value_heads, preferred_element_type=jnp.float32
        )
        return (mixed_rows.astype(jnp.bfloat16), (row_max + jnp.log(totals))[..., 0])

    mixed_blocks, log_totals = lax.map(attend_block, starts)
    mixed_heads_output = mixed_blocks.reshape(sequence_length, QUERY_HEADS * HEAD_SIZE)
    middle = resid + resid_scale * jnp.dot(
        mixed_heads_output, out_w, preferred_element_type=jnp.float32
    )
    unit_ffn, inverse_ffn = norm_forward(middle)
    normed2 = (unit_ffn * gain_ffn.astype(jnp.float32)).astype(jnp.bfloat16)
    logits = jnp.dot(normed2, router_w, preferred_element_type=jnp.float32)
    pick_table = expert_ids[:, :, None] == jnp.arange(EXPERTS, dtype=jnp.int32)[None, None, :]
    chosen = jnp.sum(jnp.where(pick_table, logits[:, None, :], 0.0), axis=2)
    exps_chosen = jnp.exp(chosen - jnp.max(chosen, axis=1, keepdims=True))
    gates = exps_chosen / jnp.sum(exps_chosen, axis=1, keepdims=True)
    target, source, filled = slot_tables(expert_ids)
    live_slots = filled[:, None] == 1
    zero_bf = jnp.zeros((), jnp.bfloat16)
    send_rows = jnp.where(live_slots, normed2[source // TOPK], zero_bf).reshape(
        owners, local_count, CAP, MODEL_WIDTH
    )
    arrived = lax.all_to_all(send_rows, "expert", split_axis=0, concat_axis=2, tiled=True).reshape(
        local_count, received, MODEL_WIDTH
    )
    gate_up = jnp.einsum("erd,edf->erf", arrived, full_in, preferred_element_type=jnp.float32)
    gate_part, up_part, sigmoid_gate, hidden = silu_parts(gate_up)
    produced = jnp.einsum(
        "erf,efd->erd", hidden, full_out, preferred_element_type=jnp.float32
    ).astype(jnp.bfloat16)
    returned = lax.all_to_all(
        produced.reshape(1, local_count, received, MODEL_WIDTH),
        "expert",
        split_axis=2,
        concat_axis=0,
        tiled=True,
    ).reshape(EXPERTS * CAP, MODEL_WIDTH)
    slot_values = returned[target].reshape(sequence_length, TOPK, MODEL_WIDTH)
    moe = jnp.einsum("tk,tkd->td", gates, slot_values.astype(jnp.float32))
    output = (middle + resid_scale * moe).astype(jnp.bfloat16)
    grad_output = cotangent.astype(jnp.float32)
    grad_mix = resid_scale * grad_output
    gate_grads = jnp.einsum("tkd,td->tk", slot_values.astype(jnp.float32), grad_mix)
    slot_grads = (
        (gates[:, :, None] * grad_mix[:, None, :])
        .astype(jnp.bfloat16)
        .reshape(sequence_length * TOPK, MODEL_WIDTH)
    )
    grad_send = jnp.where(live_slots, slot_grads[source], zero_bf).reshape(
        owners, local_count, CAP, MODEL_WIDTH
    )
    grad_arrived = lax.all_to_all(
        grad_send, "expert", split_axis=0, concat_axis=2, tiled=True
    ).reshape(local_count, received, MODEL_WIDTH)
    owner_rows = lax.all_to_all(
        send_rows, "expert", split_axis=0, concat_axis=2, tiled=True
    ).reshape(local_count, received, MODEL_WIDTH)
    owner_gate_up = jnp.einsum(
        "erd,edf->erf", owner_rows, full_in, preferred_element_type=jnp.float32
    )
    owner_gate, owner_up, owner_sigmoid, owner_hidden = silu_parts(owner_gate_up)
    hidden_grad = jnp.einsum(
        "erd,efd->erf", grad_arrived, full_out, preferred_element_type=jnp.float32
    )
    gate_grad_part = (
        hidden_grad * owner_up * owner_sigmoid * (1.0 + owner_gate * (1.0 - owner_sigmoid))
    )
    up_grad_part = hidden_grad * owner_gate * owner_sigmoid
    gate_up_grad = jnp.concatenate([gate_grad_part, up_grad_part], axis=-1).astype(jnp.bfloat16)
    grad_full_out = jnp.einsum(
        "erf,erd->efd", owner_hidden, grad_arrived, preferred_element_type=jnp.float32
    )
    grad_full_in = jnp.einsum(
        "erd,erf->edf", owner_rows, gate_up_grad, preferred_element_type=jnp.float32
    )
    row_grads = jnp.einsum(
        "erf,edf->erd", gate_up_grad, full_in, preferred_element_type=jnp.float32
    ).astype(jnp.bfloat16)
    grad_returned = lax.all_to_all(
        row_grads.reshape(1, local_count, received, MODEL_WIDTH),
        "expert",
        split_axis=2,
        concat_axis=0,
        tiled=True,
    ).reshape(EXPERTS * CAP, MODEL_WIDTH)
    grad_expert_in, grad_expert_out = (
        lax.psum_scatter(
            grad_full_in.astype(jnp.bfloat16), "shard", scatter_dimension=1, tiled=True
        ).astype(jnp.float32),
        lax.psum_scatter(
            grad_full_out.astype(jnp.bfloat16), "shard", scatter_dimension=1, tiled=True
        ).astype(jnp.float32),
    )
    mixer_back = (
        lax.all_gather(attn_gain.astype(jnp.bfloat16), ("expert", "shard"), axis=0, tiled=True),
        lax.all_gather(ffn_gain.astype(jnp.bfloat16), ("expert", "shard"), axis=0, tiled=True),
        lax.all_gather(w_query.astype(jnp.bfloat16), ("expert", "shard"), axis=0, tiled=True),
        lax.all_gather(
            key_projection.astype(jnp.bfloat16), ("expert", "shard"), axis=0, tiled=True
        ),
        lax.all_gather(
            value_projection.astype(jnp.bfloat16), ("expert", "shard"), axis=0, tiled=True
        ),
        lax.all_gather(w_out.astype(jnp.bfloat16), ("expert", "shard"), axis=0, tiled=True),
        lax.all_gather(w_router.astype(jnp.bfloat16), ("expert", "shard"), axis=0, tiled=True),
    )
    back_gain_attn, back_gain_ffn, back_query, back_key, back_value, back_out, back_router = (
        mixer_back
    )
    chosen_grad = gates * (gate_grads - jnp.sum(gates * gate_grads, axis=1, keepdims=True))
    logit_grads = jnp.sum(jnp.where(pick_table, chosen_grad[:, :, None], 0.0), axis=1).astype(
        jnp.bfloat16
    )
    grad_router_full = jnp.einsum(
        "td,te->de", normed2, logit_grads, preferred_element_type=jnp.float32
    )
    normed2_grad = jnp.sum(
        grad_returned[target].reshape(sequence_length, TOPK, MODEL_WIDTH), axis=1, dtype=jnp.float32
    )
    normed2_grad = normed2_grad + jnp.einsum(
        "te,de->td", logit_grads, back_router, preferred_element_type=jnp.float32
    )
    middle_norm_grad, grad_gain_ffn = norm_backward(
        normed2_grad, unit_ffn, inverse_ffn, back_gain_ffn.astype(jnp.float32)
    )
    middle_grad = grad_output + middle_norm_grad
    attn_grad = (resid_scale * middle_grad).astype(jnp.bfloat16)
    grad_out_full = jnp.einsum(
        "tf,td->fd", mixed_heads_output, attn_grad, preferred_element_type=jnp.float32
    )
    mixed_output_gradient = jnp.einsum(
        "td,fd->tf", attn_grad, back_out, preferred_element_type=jnp.float32
    ).astype(jnp.bfloat16)
    mixed_gradient_by_head = mixed_output_gradient.reshape(
        sequence_length, KEY_VALUE_HEADS, query_groups, HEAD_SIZE
    )

    def attend_back(carries, packed):
        key_acc, value_acc = carries
        first_row, log_rows = packed
        scores, query_rows = block_scores(first_row)
        probs = jnp.exp(scores - log_rows[..., None])
        prob_grads = jnp.einsum(
            "qhgd,khd->hgqk",
            mixed_gradient_by_head,
            value_heads,
            preferred_element_type=jnp.float32,
        )
        score_grads = (
            probs * (prob_grads - jnp.sum(probs * prob_grads, axis=-1, keepdims=True))
        ).astype(jnp.bfloat16)
        query_grads = (
            jnp.einsum("hgqk,khd->qhgd", score_grads, key_heads, preferred_element_type=jnp.float32)
            * attn_scale
        )
        key_acc = (
            key_acc
            + jnp.einsum(
                "hgqk,qhgd->khd", score_grads, query_rows, preferred_element_type=jnp.float32
            )
            * attn_scale
        )
        value_acc = value_acc + jnp.einsum(
            "hgqk,qhgd->khd",
            probs.astype(jnp.bfloat16),
            mixed_gradient_by_head,
            preferred_element_type=jnp.float32,
        )
        return ((key_acc, value_acc), query_grads)

    empty_head_rows = jnp.zeros((sequence_length, KEY_VALUE_HEADS, HEAD_SIZE), jnp.float32)
    (summed_key_gradient, summed_value_gradient), query_grad_blocks = lax.scan(
        attend_back, (empty_head_rows, empty_head_rows), (starts, log_totals)
    )
    query_raw_grad = (
        reverse_rotation(
            query_grad_blocks.reshape(sequence_length, QUERY_HEADS, HEAD_SIZE),
            cosine_table,
            sine_table,
        )
        .astype(jnp.bfloat16)
        .reshape(sequence_length, QUERY_HEADS * HEAD_SIZE)
    )
    key_raw_grad = (
        reverse_rotation(summed_key_gradient, cosine_table, sine_table)
        .astype(jnp.bfloat16)
        .reshape(sequence_length, KEY_VALUE_HEADS * HEAD_SIZE)
    )
    projected_value_gradient = summed_value_gradient.astype(jnp.bfloat16).reshape(
        sequence_length, KEY_VALUE_HEADS * HEAD_SIZE
    )
    grad_query_full = jnp.einsum(
        "td,tf->df", normed, query_raw_grad, preferred_element_type=jnp.float32
    )
    grad_key_full = jnp.einsum(
        "td,tf->df", normed, key_raw_grad, preferred_element_type=jnp.float32
    )
    grad_value_full = jnp.einsum(
        "td,tf->df", normed, projected_value_gradient, preferred_element_type=jnp.float32
    )
    normed_grad = jnp.einsum(
        "tf,df->td", query_raw_grad, back_query, preferred_element_type=jnp.float32
    )
    normed_grad = normed_grad + jnp.einsum(
        "tf,df->td", key_raw_grad, back_key, preferred_element_type=jnp.float32
    )
    normed_grad = normed_grad + jnp.einsum(
        "tf,df->td", projected_value_gradient, back_value, preferred_element_type=jnp.float32
    )
    resid_norm_grad, grad_gain_attn = norm_backward(
        normed_grad, unit_attn, inverse_attn, back_gain_attn.astype(jnp.float32)
    )
    resid_grad = middle_grad + resid_norm_grad
    grad_embedded = (embed_scale * resid_grad).astype(jnp.bfloat16)
    summed = (
        lax.psum_scatter(grad_gain_attn, ("expert", "shard"), scatter_dimension=0, tiled=True),
        lax.psum_scatter(grad_gain_ffn, ("expert", "shard"), scatter_dimension=0, tiled=True),
        lax.psum_scatter(grad_query_full, ("expert", "shard"), scatter_dimension=0, tiled=True),
        lax.psum_scatter(grad_key_full, ("expert", "shard"), scatter_dimension=0, tiled=True),
        lax.psum_scatter(grad_value_full, ("expert", "shard"), scatter_dimension=0, tiled=True),
        lax.psum_scatter(grad_out_full, ("expert", "shard"), scatter_dimension=0, tiled=True),
        lax.psum_scatter(grad_router_full, ("expert", "shard"), scatter_dimension=0, tiled=True),
    )
    return (
        output,
        grad_embedded,
        summed[0],
        summed[1],
        summed[2],
        summed[3],
        summed[4],
        summed[5],
        summed[6],
        grad_expert_in,
        grad_expert_out,
    )


BF16 = jnp.bfloat16
F32 = jnp.float32
PAIR = 2
OWN = 2
BLOCKS = 16


def over_expert(value, bits):
    return lax.ppermute(value, "expert", [(i, i ^ bits) for i in range(8)])


def over_shard(value, bits):
    return lax.ppermute(value, "shard", [(i, i ^ bits) for i in range(4)])


def dot_f32(left, right, dims):
    return lax.dot_general(left, right, dims, preferred_element_type=F32)


def gather_blocks(block):
    pair = jnp.stack([block, over_shard(block, 1)])
    quarter = [pair] + [over_expert(pair, bits) for bits in (2, 4, 6)]
    half = jnp.concatenate(quarter)
    return jnp.concatenate([half, over_expert(half, 1)])


def scatter_blocks(blocks):
    half = (blocks[:8].astype(F32) + over_expert(blocks[8:], 1).astype(F32)).astype(BF16)
    pair = half[0:2].astype(F32)
    for number, bits in ((1, 2), (2, 4), (3, 6)):
        pair = pair + over_expert(half[2 * number : 2 * number + 2], bits).astype(F32)
    pair = pair.astype(BF16)
    return pair[0].astype(F32) + over_shard(pair[1], 1).astype(F32)


def reduce_rows(partial, e, z):
    columns = partial.shape[1]
    parts = partial.astype(BF16).reshape(4, 2, 4, 32, columns)
    core = e % 2
    quad = e // 2
    mine = lax.dynamic_index_in_dim(parts, core, 1, keepdims=False)
    other = lax.dynamic_index_in_dim(parts, 1 - core, 1, keepdims=False)
    total = (mine.astype(F32) + over_expert(other, 1).astype(F32)).astype(BF16)
    plane = lax.dynamic_index_in_dim(total, quad, 0, keepdims=False).astype(F32)
    for step in (1, 2, 3):
        sent = lax.dynamic_index_in_dim(total, quad ^ step, 0, keepdims=False)
        plane = plane + over_expert(sent, 2 * step).astype(F32)
    plane = plane.astype(BF16)
    result = lax.dynamic_index_in_dim(plane, z, 0, keepdims=False).astype(F32)
    for step in (1, 2, 3):
        sent = lax.dynamic_index_in_dim(plane, z ^ step, 0, keepdims=False)
        result = result + over_shard(sent, step).astype(F32)
    return result


def exchange_weights(weights, z):
    h = z % 2
    same = lax.dynamic_slice_in_dim(weights, 2 * h, 2, 0)
    other = lax.dynamic_slice_in_dim(weights, 2 * (1 - h), 2, 0)
    pieces = [same, over_shard(other, 1), over_shard(same, 2), over_shard(other, 3)]
    stacked = jnp.stack(pieces)
    return jnp.concatenate(
        [lax.dynamic_index_in_dim(stacked, z ^ i, 0, keepdims=False) for i in range(4)], axis=1
    )


def exchange_grads(full, z):
    h = z % 2
    rows = full.shape[1] // 4
    pick = lambda k: lax.dynamic_slice_in_dim(full, (z ^ k) * rows, rows, 1)
    sent = [over_shard(pick(k).astype(BF16), k) for k in (1, 2, 3)]
    same = pick(0).astype(F32) + sent[1].astype(F32)
    other = sent[0].astype(F32) + sent[2].astype(F32)
    return jnp.where(
        h == 0, jnp.concatenate([same, other]), jnp.concatenate([other, same])
    )


def split_parts(value):
    high = value.astype(BF16)
    rest = value - high.astype(F32)
    middle = rest.astype(BF16)
    low = (rest - middle.astype(F32)).astype(BF16)
    return high, middle, low


def rows_of(table):
    quarter = table.shape[0] // 4
    return jnp.concatenate([table[i * quarter : (i + 1) * quarter] for i in range(4)], axis=1)


def table_of(rows):
    return jnp.concatenate([rows[..., 256 * i : 256 * i + 256] for i in range(4)], axis=-2)


def per_device_fast(
    embedded,
    document_numbers,
    expert_ids,
    attn_gain,
    ffn_gain,
    w_query,
    key_projection,
    value_projection,
    w_out,
    w_router,
    expert_in,
    expert_out,
    cotangent,
):
    e = lax.axis_index("expert")
    z = lax.axis_index("shard")
    h = z % 2
    length = embedded.shape[0]
    groups = QUERY_HEADS // KEY_VALUE_HEADS
    small = jnp.concatenate(
        [attn_gain[:, None], ffn_gain[:, None], jnp.zeros((32, 30), F32), w_router,
         jnp.zeros((32, 64), F32)], axis=1)
    packed = jnp.concatenate(
        [w_query, key_projection, value_projection, w_out, small], axis=1
    ).astype(BF16)
    mixer = lax.all_gather(packed, ("expert", "shard"), axis=0, tiled=True)
    query_w, key_w, value_w = mixer[:, :1024], mixer[:, 1024:1536], mixer[:, 1536:2048]
    out_w = mixer[:, 2048:3072]
    gain_attn, gain_ffn = mixer[:, 3072].astype(F32), mixer[:, 3073].astype(F32)
    router_w = mixer[:, 3104:3136]
    full_in = exchange_weights(expert_in, z)
    full_out = exchange_weights(expert_out, z)
    all_grads = gather_blocks(cotangent)

    resid = embed_scale * embedded.astype(F32)
    unit_attn, inverse_attn = norm_forward(resid)
    normed = (unit_attn * gain_attn).astype(BF16)
    unrotated_query = jnp.dot(normed, query_w, preferred_element_type=F32)
    unrotated_key = jnp.dot(normed, key_w, preferred_element_type=F32)
    projected_value = jnp.dot(normed, value_w, preferred_element_type=F32)
    segments = document_numbers[0]
    cosine_table, sine_table = rope_tables(segments)
    query_heads = (
        apply_rotation(unrotated_query.reshape(length, QUERY_HEADS, HEAD_SIZE), cosine_table, sine_table)
        .astype(BF16)
        .reshape(length, KEY_VALUE_HEADS, groups, HEAD_SIZE)
    )
    key_heads = apply_rotation(
        unrotated_key.reshape(length, KEY_VALUE_HEADS, HEAD_SIZE), cosine_table, sine_table
    ).astype(BF16)
    value_heads = projected_value.astype(BF16).reshape(length, KEY_VALUE_HEADS, HEAD_SIZE)
    key_index = jnp.arange(length, dtype=jnp.int32)
    allowed = (key_index[None, :] <= key_index[:, None]) & (segments[None, :] == segments[:, None])
    scores = jnp.einsum("qhgd,khd->hgqk", query_heads, key_heads, preferred_element_type=F32) * attn_scale
    scores = jnp.where(allowed, scores, -1e30)
    exps = jnp.exp(scores - jnp.max(scores, axis=-1, keepdims=True))
    probs = exps / jnp.sum(exps, axis=-1, keepdims=True)
    probs_low = probs.astype(BF16)
    mixed = (
        jnp.einsum("hgqk,khd->qhgd", probs_low, value_heads, preferred_element_type=F32)
        .astype(BF16)
        .reshape(length, QUERY_HEADS * HEAD_SIZE)
    )
    middle = resid + resid_scale * jnp.dot(mixed, out_w, preferred_element_type=F32)
    unit_ffn, inverse_ffn = norm_forward(middle)
    normed2 = (unit_ffn * gain_ffn).astype(BF16)
    logits = jnp.dot(normed2, router_w, preferred_element_type=F32)

    expert_range = jnp.arange(EXPERTS, dtype=jnp.int32)
    member = jnp.any(expert_ids[:, :, None] == expert_range, axis=1)
    below = (key_index[None, :] < key_index[:, None]).astype(BF16)
    rank = jnp.dot(below, member.astype(BF16), preferred_element_type=F32)
    code = jnp.where(member, rank, -1.0)
    masked = jnp.where(member, logits, -1e30)
    raised = jnp.where(member, jnp.exp(masked - jnp.max(masked, axis=1, keepdims=True)), 0.0)
    gates = raised / jnp.sum(raised, axis=1, keepdims=True)
    parts = [part.T for part in split_parts(gates)]
    aux = rows_of(jnp.concatenate([code.T.astype(BF16)] + parts))
    tokens = gather_blocks(jnp.concatenate([normed2, aux]))
    all_rows, tables = tokens[:, :256], table_of(tokens[:, 256:])

    first = e * 4 + h * OWN
    table = tables.reshape(BLOCKS, 4, EXPERTS, 256).astype(F32)
    table = lax.dynamic_slice_in_dim(table, first, OWN, 2)
    slot_index = jnp.arange(CAP, dtype=jnp.int32).astype(F32)
    select32 = (table[:, 0][:, :, None, :] == slot_index[None, None, :, None]).transpose(1, 0, 2, 3)
    select = select32.astype(BF16)
    gate_table = (table[:, 1] + table[:, 2] + table[:, 3]).transpose(1, 0, 2)
    slot_gates = jnp.sum(jnp.where(select32, gate_table[:, :, None, :], 0.0), axis=-1)
    pick = lambda rows: jnp.einsum("jbst,btd->jbsd", select, rows, preferred_element_type=F32)
    arrived = pick(all_rows).astype(BF16).reshape(OWN, BLOCKS * CAP, MODEL_WIDTH)
    slot_out = pick(all_grads).reshape(OWN, BLOCKS * CAP, MODEL_WIDTH)
    slot_gates = slot_gates.reshape(OWN, BLOCKS * CAP, 1)
    gate_up = jnp.einsum("erd,edf->erf", arrived, full_in, preferred_element_type=F32)
    gate_part, up_part, sigmoid_gate, hidden = silu_parts(gate_up)
    produced = jnp.einsum("erf,efd->erd", hidden, full_out, preferred_element_type=F32).astype(BF16)
    scaled_out = resid_scale * slot_out
    slot_grads = (slot_gates * scaled_out).astype(BF16)
    gate_dots = jnp.sum(produced.astype(F32) * scaled_out, axis=-1)
    weighted = (slot_gates * produced.astype(F32)).astype(BF16)
    back = lambda rows: jnp.einsum(
        "jbst,jbsd->btd", select, rows.reshape(OWN, BLOCKS, CAP, MODEL_WIDTH), preferred_element_type=F32
    )
    moe_blocks = back(weighted).astype(BF16)
    hidden_grad = jnp.einsum("erd,efd->erf", slot_grads, full_out, preferred_element_type=F32)
    gate_grad_part = hidden_grad * up_part * sigmoid_gate * (1.0 + gate_part * (1.0 - sigmoid_gate))
    up_grad_part = hidden_grad * gate_part * sigmoid_gate
    gate_up_grad = jnp.concatenate([gate_grad_part, up_grad_part], axis=-1).astype(BF16)
    row_grads = jnp.einsum("erf,edf->erd", gate_up_grad, full_in, preferred_element_type=F32).astype(BF16)
    row_blocks = back(row_grads).astype(BF16)
    dots = jnp.sum(
        jnp.where(select32, gate_dots.reshape(OWN, BLOCKS, CAP, 1), 0.0), axis=2
    )
    high, low, _ = split_parts(dots.transpose(1, 0, 2))
    place = jnp.zeros((BLOCKS, 2, EXPERTS, 256), BF16)
    place = lax.dynamic_update_slice(place, jnp.stack([high, low], axis=1), (0, 0, first, 0))
    flat = place.reshape(BLOCKS, 64, 256)
    flat = jnp.concatenate([flat[:, 16 * i : 16 * i + 16] for i in range(4)], axis=2)
    returned = scatter_blocks(jnp.concatenate([row_blocks, flat], axis=1))
    normed2_grad, dot_rows = returned[:256], table_of(returned[256:])
    gate_grads = (dot_rows[:EXPERTS] + dot_rows[EXPERTS:]).T

    grad_full_out = jnp.einsum("erf,erd->efd", hidden, slot_grads, preferred_element_type=F32)
    grad_full_in = jnp.einsum("erd,erf->edf", arrived, gate_up_grad, preferred_element_type=F32)
    grad_expert_in = exchange_grads(grad_full_in, z)
    grad_expert_out = exchange_grads(grad_full_out, z)
    moe = scatter_blocks(moe_blocks)
    output = (middle + resid_scale * moe).astype(BF16)

    grad_output = cotangent.astype(F32)
    chosen_grad = gates * (gate_grads - jnp.sum(gates * gate_grads, axis=1, keepdims=True))
    logit_grads = chosen_grad.astype(BF16)
    grad_router_full = jnp.einsum("td,te->de", normed2, logit_grads, preferred_element_type=F32)
    normed2_grad = normed2_grad + jnp.einsum("te,de->td", logit_grads, router_w, preferred_element_type=F32)
    middle_norm_grad, grad_gain_ffn = norm_backward(normed2_grad, unit_ffn, inverse_ffn, gain_ffn)
    middle_grad = grad_output + middle_norm_grad
    attn_grad = (resid_scale * middle_grad).astype(BF16)
    grad_out_full = jnp.einsum("tf,td->fd", mixed, attn_grad, preferred_element_type=F32)
    mixed_grad = (
        jnp.einsum("td,fd->tf", attn_grad, out_w, preferred_element_type=F32)
        .astype(BF16)
        .reshape(length, KEY_VALUE_HEADS, groups, HEAD_SIZE)
    )
    prob_grads = jnp.einsum("qhgd,khd->hgqk", mixed_grad, value_heads, preferred_element_type=F32)
    score_grads = (probs * (prob_grads - jnp.sum(probs * prob_grads, axis=-1, keepdims=True))).astype(BF16)
    query_grads = jnp.einsum("hgqk,khd->qhgd", score_grads, key_heads, preferred_element_type=F32) * attn_scale
    key_grads = jnp.einsum("hgqk,qhgd->khd", score_grads, query_heads, preferred_element_type=F32) * attn_scale
    value_grads = jnp.einsum("hgqk,qhgd->khd", probs_low, mixed_grad, preferred_element_type=F32)
    query_raw = reverse_rotation(
        query_grads.reshape(length, QUERY_HEADS, HEAD_SIZE), cosine_table, sine_table
    ).astype(BF16).reshape(length, QUERY_HEADS * HEAD_SIZE)
    key_raw = reverse_rotation(key_grads, cosine_table, sine_table).astype(BF16).reshape(length, 512)
    value_raw = value_grads.astype(BF16).reshape(length, 512)
    raw = jnp.concatenate([query_raw, key_raw, value_raw], axis=1)
    grad_qkv_full = jnp.einsum("td,tf->df", normed, raw, preferred_element_type=F32)
    normed_grad = jnp.einsum("tf,df->td", raw, mixer[:, :2048], preferred_element_type=F32)
    resid_norm_grad, grad_gain_attn = norm_backward(normed_grad, unit_attn, inverse_attn, gain_attn)
    grad_embedded = (embed_scale * (middle_grad + resid_norm_grad)).astype(BF16)

    gains = jnp.concatenate(
        [part[:, None] for gain in (grad_gain_attn, grad_gain_ffn) for part in split_parts(gain)[:2]]
        + [jnp.zeros((1024, 28), BF16)], axis=1).astype(F32)
    side = jnp.concatenate([gains, grad_router_full, jnp.zeros((1024, 64), F32)], axis=1)
    late = reduce_rows(jnp.concatenate([grad_qkv_full, side], axis=1), e, z)
    early = reduce_rows(grad_out_full, e, z)
    return (
        output,
        grad_embedded,
        late[:, 2048] + late[:, 2049],
        late[:, 2050] + late[:, 2051],
        late[:, :1024],
        late[:, 1024:1536],
        late[:, 1536:2048],
        early,
        late[:, 2080:2112],
        grad_expert_in,
        grad_expert_out,
    )


def solution(mesh):
    owners, shards = mesh.shape["expert"], mesh.shape["shard"]
    fast = owners == 8 and shards == 4
    both = ("expert", "shard")
    rows = P(both, None)
    weights = P("expert", "shard", None)
    return jax.shard_map(
        per_device_fast if fast else per_device_general,
        mesh=mesh,
        in_specs=(rows,) * 3 + (P(both),) * 2 + (rows,) * 5 + (weights,) * 2 + (rows,),
        out_specs=(rows,) * 2 + (P(both),) * 2 + (rows,) * 5 + (weights,) * 2,
        check_vma=False,
    )
```

```python
import functools

import jax
import jax.numpy as jnp
from jax import lax
from jax.experimental import pallas as pl
from jax.experimental.pallas import tpu as pltpu
from jax.sharding import PartitionSpec as P

MODEL_WIDTH = 1024
QUERY_HEADS = 16
KEY_VALUE_HEADS = 8
HEAD_SIZE = 64
FF = 512
EXPERTS = 32
TOPK = 8
CAP = 128


embed_scale = 12.0
attn_scale = 0.015625
resid_scale = 0.22
norm_eps = 1e-06
rope_base = 10000.0


def rope_tables(segments):
    sequence_length = segments.shape[0]
    key_index = jnp.arange(sequence_length, dtype=jnp.int32)
    change = jnp.concatenate([jnp.ones((1,), jnp.bool_), segments[1:] != segments[:-1]])
    begins = lax.cummax(jnp.where(change, key_index, 0), axis=0)
    places = (key_index - begins).astype(jnp.float32)
    freqs = rope_base ** (-2.0 * jnp.arange(HEAD_SIZE // 2, dtype=jnp.float32) / HEAD_SIZE)
    angles = places[:, None] * freqs[None, :]
    return (jnp.cos(angles), jnp.sin(angles))


def apply_rotation(value_heads, cosine_table, sine_table):
    halfway = value_heads.shape[-1] // 2
    first_half = value_heads[..., :halfway]
    second_half = value_heads[..., halfway:]
    cos_part = cosine_table[:, None, :]
    sin_part = sine_table[:, None, :]
    return jnp.concatenate(
        [
            first_half * cos_part - second_half * sin_part,
            second_half * cos_part + first_half * sin_part,
        ],
        axis=-1,
    )


def reverse_rotation(grads, cosine_table, sine_table):
    halfway = grads.shape[-1] // 2
    first_half = grads[..., :halfway]
    second_half = grads[..., halfway:]
    cos_part = cosine_table[:, None, :]
    sin_part = sine_table[:, None, :]
    return jnp.concatenate(
        [
            first_half * cos_part + second_half * sin_part,
            second_half * cos_part - first_half * sin_part,
        ],
        axis=-1,
    )


def norm_forward(value_heads):
    inverse = lax.rsqrt(jnp.mean(value_heads * value_heads, axis=1, keepdims=True) + norm_eps)
    return (value_heads * inverse, inverse)


def norm_backward(upstream, unit_values, inverse, gain):
    scaled = upstream * gain
    grad_values = inverse * (
        scaled - unit_values * jnp.mean(scaled * unit_values, axis=1, keepdims=True)
    )
    return (grad_values, jnp.sum(upstream * unit_values, axis=0))


def slot_tables(expert_ids):
    flat_ids = expert_ids.reshape(-1)
    count_all = flat_ids.shape[0]
    matches = (flat_ids[:, None] == jnp.arange(EXPERTS, dtype=jnp.int32)[None, :]).astype(jnp.int32)
    before = jnp.cumsum(matches, axis=0) - 1
    ranking = jnp.sum(before * matches, axis=1)
    target = flat_ids * CAP + ranking
    source = (
        jnp.zeros((EXPERTS * CAP,), jnp.int32)
        .at[target]
        .set(jnp.arange(count_all, dtype=jnp.int32))
    )
    filled = (
        jnp.zeros((EXPERTS * CAP,), jnp.int32).at[target].set(jnp.ones((count_all,), jnp.int32))
    )
    return (target, source, filled)


def silu_parts(gate_up):
    gate_part = gate_up[..., :FF]
    up_part = gate_up[..., FF:]
    sigmoid_gate = jax.nn.sigmoid(gate_part)
    hidden = (gate_part * sigmoid_gate * up_part).astype(jnp.bfloat16)
    return (gate_part, up_part, sigmoid_gate, hidden)


def per_device_general(
    embedded,
    document_numbers,
    expert_ids,
    attn_gain,
    ffn_gain,
    w_query,
    key_projection,
    value_projection,
    w_out,
    w_router,
    expert_in,
    expert_out,
    cotangent,
):
    mixer = (
        lax.all_gather(attn_gain.astype(jnp.bfloat16), ("expert", "shard"), axis=0, tiled=True),
        lax.all_gather(ffn_gain.astype(jnp.bfloat16), ("expert", "shard"), axis=0, tiled=True),
        lax.all_gather(w_query.astype(jnp.bfloat16), ("expert", "shard"), axis=0, tiled=True),
        lax.all_gather(
            key_projection.astype(jnp.bfloat16), ("expert", "shard"), axis=0, tiled=True
        ),
        lax.all_gather(
            value_projection.astype(jnp.bfloat16), ("expert", "shard"), axis=0, tiled=True
        ),
        lax.all_gather(w_out.astype(jnp.bfloat16), ("expert", "shard"), axis=0, tiled=True),
        lax.all_gather(w_router.astype(jnp.bfloat16), ("expert", "shard"), axis=0, tiled=True),
    )
    gain_attn, gain_ffn, query_w, key_w, value_w, out_w, router_w = mixer
    full_in, full_out = (
        lax.all_gather(expert_in, "shard", axis=1, tiled=True),
        lax.all_gather(expert_out, "shard", axis=1, tiled=True),
    )
    sequence_length = embedded.shape[0]
    query_groups = QUERY_HEADS // KEY_VALUE_HEADS
    owners = lax.axis_size("expert")
    local_count = EXPERTS // owners
    received = owners * CAP
    resid = embed_scale * embedded.astype(jnp.float32)
    unit_attn, inverse_attn = norm_forward(resid)
    normed = (unit_attn * gain_attn.astype(jnp.float32)).astype(jnp.bfloat16)
    unrotated_query = jnp.dot(normed, query_w, preferred_element_type=jnp.float32)
    unrotated_key = jnp.dot(normed, key_w, preferred_element_type=jnp.float32)
    projected_value = jnp.dot(normed, value_w, preferred_element_type=jnp.float32)
    segments = document_numbers[0]
    cosine_table, sine_table = rope_tables(segments)
    query_heads = (
        apply_rotation(
            unrotated_query.reshape(sequence_length, QUERY_HEADS, HEAD_SIZE),
            cosine_table,
            sine_table,
        )
        .astype(jnp.bfloat16)
        .reshape(sequence_length, KEY_VALUE_HEADS, query_groups, HEAD_SIZE)
    )
    key_heads = apply_rotation(
        unrotated_key.reshape(sequence_length, KEY_VALUE_HEADS, HEAD_SIZE), cosine_table, sine_table
    ).astype(jnp.bfloat16)
    value_heads = projected_value.astype(jnp.bfloat16).reshape(
        sequence_length, KEY_VALUE_HEADS, HEAD_SIZE
    )
    block_rows = min(512, sequence_length)
    starts = jnp.arange(sequence_length // block_rows, dtype=jnp.int32) * block_rows
    key_index = jnp.arange(sequence_length, dtype=jnp.int32)

    def block_scores(first_row):
        row_index = first_row + jnp.arange(block_rows, dtype=jnp.int32)
        raw_scores = (
            jnp.einsum("qhgd,khd->hgqk", query_heads, key_heads, preferred_element_type=jnp.float32)
            * attn_scale
        )
        allowed = (key_index[None, :] <= row_index[:, None]) & (
            segments[None, :] == segments[:, None]
        )
        return (jnp.where(allowed, raw_scores, -1e30), query_heads)

    def attend_block(first_row):
        scores, query_rows = block_scores(first_row)
        row_max = jnp.max(scores, axis=-1, keepdims=True)
        exps = jnp.exp(scores - row_max)
        totals = jnp.sum(exps, axis=-1, keepdims=True)
        weights = (exps / totals).astype(jnp.bfloat16)
        mixed_rows = jnp.einsum(
            "hgqk,khd->qhgd", weights, value_heads, preferred_element_type=jnp.float32
        )
        return (mixed_rows.astype(jnp.bfloat16), (row_max + jnp.log(totals))[..., 0])

    mixed_blocks, log_totals = lax.map(attend_block, starts)
    mixed_heads_output = mixed_blocks.reshape(sequence_length, QUERY_HEADS * HEAD_SIZE)
    middle = resid + resid_scale * jnp.dot(
        mixed_heads_output, out_w, preferred_element_type=jnp.float32
    )
    unit_ffn, inverse_ffn = norm_forward(middle)
    normed2 = (unit_ffn * gain_ffn.astype(jnp.float32)).astype(jnp.bfloat16)
    logits = jnp.dot(normed2, router_w, preferred_element_type=jnp.float32)
    pick_table = expert_ids[:, :, None] == jnp.arange(EXPERTS, dtype=jnp.int32)[None, None, :]
    chosen = jnp.sum(jnp.where(pick_table, logits[:, None, :], 0.0), axis=2)
    exps_chosen = jnp.exp(chosen - jnp.max(chosen, axis=1, keepdims=True))
    gates = exps_chosen / jnp.sum(exps_chosen, axis=1, keepdims=True)
    target, source, filled = slot_tables(expert_ids)
    live_slots = filled[:, None] == 1
    zero_bf = jnp.zeros((), jnp.bfloat16)
    send_rows = jnp.where(live_slots, normed2[source // TOPK], zero_bf).reshape(
        owners, local_count, CAP, MODEL_WIDTH
    )
    arrived = lax.all_to_all(send_rows, "expert", split_axis=0, concat_axis=2, tiled=True).reshape(
        local_count, received, MODEL_WIDTH
    )
    gate_up = jnp.einsum("erd,edf->erf", arrived, full_in, preferred_element_type=jnp.float32)
    gate_part, up_part, sigmoid_gate, hidden = silu_parts(gate_up)
    produced = jnp.einsum(
        "erf,efd->erd", hidden, full_out, preferred_element_type=jnp.float32
    ).astype(jnp.bfloat16)
    returned = lax.all_to_all(
        produced.reshape(1, local_count, received, MODEL_WIDTH),
        "expert",
        split_axis=2,
        concat_axis=0,
        tiled=True,
    ).reshape(EXPERTS * CAP, MODEL_WIDTH)
    slot_values = returned[target].reshape(sequence_length, TOPK, MODEL_WIDTH)
    moe = jnp.einsum("tk,tkd->td", gates, slot_values.astype(jnp.float32))
    output = (middle + resid_scale * moe).astype(jnp.bfloat16)
    grad_output = cotangent.astype(jnp.float32)
    grad_mix = resid_scale * grad_output
    gate_grads = jnp.einsum("tkd,td->tk", slot_values.astype(jnp.float32), grad_mix)
    slot_grads = (
        (gates[:, :, None] * grad_mix[:, None, :])
        .astype(jnp.bfloat16)
        .reshape(sequence_length * TOPK, MODEL_WIDTH)
    )
    grad_send = jnp.where(live_slots, slot_grads[source], zero_bf).reshape(
        owners, local_count, CAP, MODEL_WIDTH
    )
    grad_arrived = lax.all_to_all(
        grad_send, "expert", split_axis=0, concat_axis=2, tiled=True
    ).reshape(local_count, received, MODEL_WIDTH)
    owner_rows = lax.all_to_all(
        send_rows, "expert", split_axis=0, concat_axis=2, tiled=True
    ).reshape(local_count, received, MODEL_WIDTH)
    owner_gate_up = jnp.einsum(
        "erd,edf->erf", owner_rows, full_in, preferred_element_type=jnp.float32
    )
    owner_gate, owner_up, owner_sigmoid, owner_hidden = silu_parts(owner_gate_up)
    hidden_grad = jnp.einsum(
        "erd,efd->erf", grad_arrived, full_out, preferred_element_type=jnp.float32
    )
    gate_grad_part = (
        hidden_grad * owner_up * owner_sigmoid * (1.0 + owner_gate * (1.0 - owner_sigmoid))
    )
    up_grad_part = hidden_grad * owner_gate * owner_sigmoid
    gate_up_grad = jnp.concatenate([gate_grad_part, up_grad_part], axis=-1).astype(jnp.bfloat16)
    grad_full_out = jnp.einsum(
        "erf,erd->efd", owner_hidden, grad_arrived, preferred_element_type=jnp.float32
    )
    grad_full_in = jnp.einsum(
        "erd,erf->edf", owner_rows, gate_up_grad, preferred_element_type=jnp.float32
    )
    row_grads = jnp.einsum(
        "erf,edf->erd", gate_up_grad, full_in, preferred_element_type=jnp.float32
    ).astype(jnp.bfloat16)
    grad_returned = lax.all_to_all(
        row_grads.reshape(1, local_count, received, MODEL_WIDTH),
        "expert",
        split_axis=2,
        concat_axis=0,
        tiled=True,
    ).reshape(EXPERTS * CAP, MODEL_WIDTH)
    grad_expert_in, grad_expert_out = (
        lax.psum_scatter(
            grad_full_in.astype(jnp.bfloat16), "shard", scatter_dimension=1, tiled=True
        ).astype(jnp.float32),
        lax.psum_scatter(
            grad_full_out.astype(jnp.bfloat16), "shard", scatter_dimension=1, tiled=True
        ).astype(jnp.float32),
    )
    mixer_back = (
        lax.all_gather(attn_gain.astype(jnp.bfloat16), ("expert", "shard"), axis=0, tiled=True),
        lax.all_gather(ffn_gain.astype(jnp.bfloat16), ("expert", "shard"), axis=0, tiled=True),
        lax.all_gather(w_query.astype(jnp.bfloat16), ("expert", "shard"), axis=0, tiled=True),
        lax.all_gather(
            key_projection.astype(jnp.bfloat16), ("expert", "shard"), axis=0, tiled=True
        ),
        lax.all_gather(
            value_projection.astype(jnp.bfloat16), ("expert", "shard"), axis=0, tiled=True
        ),
        lax.all_gather(w_out.astype(jnp.bfloat16), ("expert", "shard"), axis=0, tiled=True),
        lax.all_gather(w_router.astype(jnp.bfloat16), ("expert", "shard"), axis=0, tiled=True),
    )
    back_gain_attn, back_gain_ffn, back_query, back_key, back_value, back_out, back_router = (
        mixer_back
    )
    chosen_grad = gates * (gate_grads - jnp.sum(gates * gate_grads, axis=1, keepdims=True))
    logit_grads = jnp.sum(jnp.where(pick_table, chosen_grad[:, :, None], 0.0), axis=1).astype(
        jnp.bfloat16
    )
    grad_router_full = jnp.einsum(
        "td,te->de", normed2, logit_grads, preferred_element_type=jnp.float32
    )
    normed2_grad = jnp.sum(
        grad_returned[target].reshape(sequence_length, TOPK, MODEL_WIDTH), axis=1, dtype=jnp.float32
    )
    normed2_grad = normed2_grad + jnp.einsum(
        "te,de->td", logit_grads, back_router, preferred_element_type=jnp.float32
    )
    middle_norm_grad, grad_gain_ffn = norm_backward(
        normed2_grad, unit_ffn, inverse_ffn, back_gain_ffn.astype(jnp.float32)
    )
    middle_grad = grad_output + middle_norm_grad
    attn_grad = (resid_scale * middle_grad).astype(jnp.bfloat16)
    grad_out_full = jnp.einsum(
        "tf,td->fd", mixed_heads_output, attn_grad, preferred_element_type=jnp.float32
    )
    mixed_output_gradient = jnp.einsum(
        "td,fd->tf", attn_grad, back_out, preferred_element_type=jnp.float32
    ).astype(jnp.bfloat16)
    mixed_gradient_by_head = mixed_output_gradient.reshape(
        sequence_length, KEY_VALUE_HEADS, query_groups, HEAD_SIZE
    )

    def attend_back(carries, packed):
        key_acc, value_acc = carries
        first_row, log_rows = packed
        scores, query_rows = block_scores(first_row)
        probs = jnp.exp(scores - log_rows[..., None])
        prob_grads = jnp.einsum(
            "qhgd,khd->hgqk",
            mixed_gradient_by_head,
            value_heads,
            preferred_element_type=jnp.float32,
        )
        score_grads = (
            probs * (prob_grads - jnp.sum(probs * prob_grads, axis=-1, keepdims=True))
        ).astype(jnp.bfloat16)
        query_grads = (
            jnp.einsum("hgqk,khd->qhgd", score_grads, key_heads, preferred_element_type=jnp.float32)
            * attn_scale
        )
        key_acc = (
            key_acc
            + jnp.einsum(
                "hgqk,qhgd->khd", score_grads, query_rows, preferred_element_type=jnp.float32
            )
            * attn_scale
        )
        value_acc = value_acc + jnp.einsum(
            "hgqk,qhgd->khd",
            probs.astype(jnp.bfloat16),
            mixed_gradient_by_head,
            preferred_element_type=jnp.float32,
        )
        return ((key_acc, value_acc), query_grads)

    empty_head_rows = jnp.zeros((sequence_length, KEY_VALUE_HEADS, HEAD_SIZE), jnp.float32)
    (summed_key_gradient, summed_value_gradient), query_grad_blocks = lax.scan(
        attend_back, (empty_head_rows, empty_head_rows), (starts, log_totals)
    )
    query_raw_grad = (
        reverse_rotation(
            query_grad_blocks.reshape(sequence_length, QUERY_HEADS, HEAD_SIZE),
            cosine_table,
            sine_table,
        )
        .astype(jnp.bfloat16)
        .reshape(sequence_length, QUERY_HEADS * HEAD_SIZE)
    )
    key_raw_grad = (
        reverse_rotation(summed_key_gradient, cosine_table, sine_table)
        .astype(jnp.bfloat16)
        .reshape(sequence_length, KEY_VALUE_HEADS * HEAD_SIZE)
    )
    projected_value_gradient = summed_value_gradient.astype(jnp.bfloat16).reshape(
        sequence_length, KEY_VALUE_HEADS * HEAD_SIZE
    )
    grad_query_full = jnp.einsum(
        "td,tf->df", normed, query_raw_grad, preferred_element_type=jnp.float32
    )
    grad_key_full = jnp.einsum(
        "td,tf->df", normed, key_raw_grad, preferred_element_type=jnp.float32
    )
    grad_value_full = jnp.einsum(
        "td,tf->df", normed, projected_value_gradient, preferred_element_type=jnp.float32
    )
    normed_grad = jnp.einsum(
        "tf,df->td", query_raw_grad, back_query, preferred_element_type=jnp.float32
    )
    normed_grad = normed_grad + jnp.einsum(
        "tf,df->td", key_raw_grad, back_key, preferred_element_type=jnp.float32
    )
    normed_grad = normed_grad + jnp.einsum(
        "tf,df->td", projected_value_gradient, back_value, preferred_element_type=jnp.float32
    )
    resid_norm_grad, grad_gain_attn = norm_backward(
        normed_grad, unit_attn, inverse_attn, back_gain_attn.astype(jnp.float32)
    )
    resid_grad = middle_grad + resid_norm_grad
    grad_embedded = (embed_scale * resid_grad).astype(jnp.bfloat16)
    summed = (
        lax.psum_scatter(grad_gain_attn, ("expert", "shard"), scatter_dimension=0, tiled=True),
        lax.psum_scatter(grad_gain_ffn, ("expert", "shard"), scatter_dimension=0, tiled=True),
        lax.psum_scatter(grad_query_full, ("expert", "shard"), scatter_dimension=0, tiled=True),
        lax.psum_scatter(grad_key_full, ("expert", "shard"), scatter_dimension=0, tiled=True),
        lax.psum_scatter(grad_value_full, ("expert", "shard"), scatter_dimension=0, tiled=True),
        lax.psum_scatter(grad_out_full, ("expert", "shard"), scatter_dimension=0, tiled=True),
        lax.psum_scatter(grad_router_full, ("expert", "shard"), scatter_dimension=0, tiled=True),
    )
    return (
        output,
        grad_embedded,
        summed[0],
        summed[1],
        summed[2],
        summed[3],
        summed[4],
        summed[5],
        summed[6],
        grad_expert_in,
        grad_expert_out,
    )


BF16 = jnp.bfloat16
F32 = jnp.float32
PAIR = 2
OWN = 2
BLOCKS = 16


def over_expert(value, bits):
    return lax.ppermute(value, "expert", [(i, i ^ bits) for i in range(8)])


def over_shard(value, bits):
    return lax.ppermute(value, "shard", [(i, i ^ bits) for i in range(4)])


def dot_f32(left, right, dims):
    return lax.dot_general(left, right, dims, preferred_element_type=F32)


CONTRACT_LAST = (((1,), (1,)), ((), ()))
CONTRACT_FIRST = (((0,), (0,)), ((), ()))
CONTRACT_PLAIN = (((1,), (0,)), ((), ()))
STEP_BLOCKS = 2
STEPS = BLOCKS // STEP_BLOCKS
STEP_ROWS = STEP_BLOCKS * CAP


def expert_body(first_part, number_ref, *refs):
    if first_part:
        tok_own, tok_far, out_own, out_far, w_ref = refs[:5]
        refs = refs[5:]
        befores = None
    else:
        tok_own, tok_far, out_own, out_far, w_ref = refs[:5]
        befores = refs[5:9]
        refs = refs[9:]
    row_own, row_far, moe_own, moe_far, grad_ref, x_s, g_s, gate_s, table_s, back_s, mix_s, dot_s, in_acc, out_acc = refs
    step = pl.program_id(0)
    number = number_ref[0]
    own = step < STEPS // 2

    def mask_of(i):
        slot = lax.broadcasted_iota(jnp.int32, (CAP, 256), 0).astype(F32)
        return slot == table_s[i, 0:1, :]

    def load(tok_ref, g_ref):
        for i in range(STEP_BLOCKS):
            aux = tok_ref[i, 256:288, :].astype(F32)
            line = lax.broadcasted_iota(jnp.int32, (EXPERTS, 1024), 0)
            line = jnp.sum(jnp.where(line == number, aux, 0.0), axis=0, keepdims=True)
            table_s[i, 0:1, :] = line[:, :256]
            gate = line[:, 256:512] + line[:, 512:768] + line[:, 768:]
            mask = mask_of(i)
            pick = jnp.where(mask, 1.0, 0.0).astype(BF16)
            at = slice(i * CAP, (i + 1) * CAP)
            x_s[at, :] = dot_f32(pick, tok_ref[i, 0:256, :], CONTRACT_PLAIN).astype(BF16)
            g_s[at, :] = resid_scale * dot_f32(pick, g_ref[i], CONTRACT_PLAIN)
            gate_s[at, :] = jnp.sum(jnp.where(mask, gate, 0.0), axis=1, keepdims=True)

    @pl.when(own)
    def _():
        load(tok_own, out_own)

    @pl.when(jnp.logical_not(own))
    def _():
        load(tok_far, out_far)

    w_in = w_ref[:, 0:256, :].reshape(1024, 1024)
    w_out = w_ref[:, 256:384, :].reshape(512, 1024)
    x = x_s[...]
    gate_up = dot_f32(x, w_in, CONTRACT_PLAIN)
    gate_part, up_part = gate_up[:, :FF], gate_up[:, FF:]
    sigmoid = jax.nn.sigmoid(gate_part)
    hidden = (gate_part * sigmoid * up_part).astype(BF16)
    produced = dot_f32(hidden, w_out, CONTRACT_PLAIN).astype(BF16).astype(F32)
    slot_gate = gate_s[...]
    scaled = g_s[...]
    slot_grad = (slot_gate * scaled).astype(BF16)
    dot_s[...] = jnp.sum(produced * scaled, axis=1, keepdims=True)
    mix_s[...] = (slot_gate * produced).astype(BF16)
    hidden_grad = dot_f32(slot_grad, w_out, CONTRACT_LAST)
    gate_grad = hidden_grad * up_part * sigmoid * (1.0 + gate_part * (1.0 - sigmoid))
    up_grad = hidden_grad * gate_part * sigmoid
    gate_up_grad = jnp.concatenate([gate_grad.astype(BF16), up_grad.astype(BF16)], axis=1)
    back_s[...] = dot_f32(gate_up_grad, w_in, CONTRACT_LAST).astype(BF16)
    in_part = dot_f32(x, gate_up_grad, CONTRACT_FIRST)
    out_part = dot_f32(hidden, slot_grad, CONTRACT_FIRST)

    @pl.when(step == 0)
    def _():
        in_acc[...] = in_part
        out_acc[...] = out_part

    @pl.when(step > 0)
    def _():
        in_acc[...] += in_part
        out_acc[...] += out_part

    def store(row_ref, moe_ref, row_before, moe_before):
        for i in range(STEP_BLOCKS):
            at = slice(i * CAP, (i + 1) * CAP)
            mask = mask_of(i)
            pick = jnp.where(mask, 1.0, 0.0).astype(BF16)
            rows = dot_f32(pick, back_s[at, :], CONTRACT_FIRST)
            mixed = dot_f32(pick, mix_s[at, :], CONTRACT_FIRST)
            dots = jnp.sum(jnp.where(mask, dot_s[at, :], 0.0), axis=0, keepdims=True)
            high = dots.astype(BF16).astype(F32)
            low = dots - high
            wide = jnp.concatenate([high, high, low, low], axis=1)
            line = lax.broadcasted_iota(jnp.int32, (16, 1024), 0)
            lane = lax.broadcasted_iota(jnp.int32, (16, 1024), 1) // 256
            here = (line == number % 16) & (lane % 2 == number // 16)
            side = jnp.where(here, jnp.broadcast_to(wide, (16, 1024)), 0.0)
            if row_before is not None:
                rows = rows + row_before[i, 0:256, :].astype(F32)
                mixed = mixed + moe_before[i].astype(F32)
                side = side + row_before[i, 256:272, :].astype(F32)
            row_ref[i, 0:256, :] = rows.astype(BF16)
            row_ref[i, 256:272, :] = side.astype(BF16)
            moe_ref[i] = mixed.astype(BF16)

    own_before, far_before, own_moe_before, far_moe_before = befores or (None,) * 4

    @pl.when(own)
    def _():
        store(row_own, moe_own, own_before, own_moe_before)

    @pl.when(jnp.logical_not(own))
    def _():
        store(row_far, moe_far, far_before, far_moe_before)

    @pl.when(step == STEPS - 1)
    def _():
        for d in range(4):
            grad_ref[d, 0:256, :] = in_acc[d * 256 : (d + 1) * 256, :].astype(BF16)
            grad_ref[d, 256:384, :] = out_acc[d * 128 : (d + 1) * 128, :].astype(BF16)


def expert_call(number, tok_own, tok_far, out_own, out_far, weights, before=None):
    half = STEPS // 2
    own_at = lambda s, n: (jnp.minimum(s, half - 1), 0, 0)
    far_at = lambda s, n: (jnp.maximum(s - half, 0), 0, 0)
    whole = lambda s, n: (0, 0, 0)
    spec = lambda rows, at: pl.BlockSpec((STEP_BLOCKS, rows, 1024), at)
    w_spec = pl.BlockSpec((4, 384, 1024), whole, pipeline_mode=pl.Buffered(1))
    outs = [spec(272, own_at), spec(272, far_at), spec(256, own_at), spec(256, far_at)]
    ins = [spec(288, own_at), spec(288, far_at), spec(256, own_at), spec(256, far_at), w_spec]
    operands = [tok_own, tok_far, out_own, out_far, weights]
    aliases = {}
    if before is not None:
        ins = ins + outs
        operands = operands + list(before)
        aliases = {6 + i: i for i in range(4)}
    shapes = [jax.ShapeDtypeStruct((8, rows, 1024), BF16) for rows in (272, 272, 256, 256)]
    rows_f32 = pltpu.VMEM((STEP_ROWS, 1), F32)
    wide = pltpu.VMEM((STEP_ROWS, 1024), BF16)
    return pl.pallas_call(
        functools.partial(expert_body, before is None),
        out_shape=shapes + [jax.ShapeDtypeStruct((4, 384, 1024), BF16)],
        grid_spec=pltpu.PrefetchScalarGridSpec(
            num_scalar_prefetch=1,
            grid=(STEPS,),
            in_specs=ins,
            out_specs=outs + [w_spec],
            scratch_shapes=[
                wide, pltpu.VMEM((STEP_ROWS, 1024), F32), rows_f32, pltpu.VMEM((STEP_BLOCKS, 8, 256), F32),
                wide, wide, rows_f32, pltpu.VMEM((1024, 1024), F32), pltpu.VMEM((512, 1024), F32),
            ],
        ),
        input_output_aliases=aliases,
        compiler_params=pltpu.CompilerParams(
            dimension_semantics=("arbitrary",), vmem_limit_bytes=60 * 1024 * 1024
        ),
        cost_estimate=pl.CostEstimate(
            flops=24_000_000_000, bytes_accessed=45_000_000, transcendentals=1_000_000
        ),
        name="expert",
    )(number, *operands)


LANES = 128
GAIN_ATTN = 32
GAIN_FFN = 33
SEQUENCE = 256


def group_of(e, r):
    return pl.ds(pl.multiple_of((e ^ r) * LANES, LANES), LANES)


def turn_halves(value):
    lane = lax.broadcasted_iota(jnp.int32, value.shape, 1) % HEAD_SIZE
    width = value.shape[1]
    return jnp.where(
        lane < HEAD_SIZE // 2,
        -pltpu.roll(value, width - HEAD_SIZE // 2, 1),
        pltpu.roll(value, HEAD_SIZE // 2, 1),
    )


def wide_table(table, width):
    return jnp.concatenate([table] * (width // LANES), axis=1)


def inverse_rms(value):
    return lax.rsqrt(jnp.mean(value * value, axis=1, keepdims=True) + norm_eps)


def attention_probs(queries, keys, allowed):
    scores = jnp.where(allowed, dot_f32(queries, keys, CONTRACT_LAST) * attn_scale, -1e30)
    exps = jnp.exp(scores - jnp.max(scores, axis=1, keepdims=True))
    return exps / jnp.sum(exps, axis=1, keepdims=True)


def allowed_of(column_ref, row_ref):
    shape = (2 * SEQUENCE, SEQUENCE)
    query = lax.broadcasted_iota(jnp.int32, shape, 0) % SEQUENCE
    key = lax.broadcasted_iota(jnp.int32, shape, 1)
    column = column_ref[...]
    same = jnp.concatenate([column, column], axis=0) == row_ref[...]
    return (key <= query) & same


def heads_of(block, first, count):
    return jnp.concatenate(
        [block[:, HEAD_SIZE * (first + i) : HEAD_SIZE * (first + i + 1)] for i in range(count)], axis=0
    )


def attend_body(e_ref, x_ref, column_ref, row_ref, cos_ref, sin_ref, own_ref, far_ref,
                normed_ref, q_ref, k_ref, v_ref, mixed_ref):
    e = e_ref[0]
    resid = embed_scale * x_ref[...].astype(F32)
    inverse = inverse_rms(resid)
    for part, w_ref in ((0, own_ref), (1, far_ref)):
        gain = w_ref[:, 2048:].astype(F32).T[GAIN_ATTN : GAIN_ATTN + 1, :]
        for q in range(4):
            block = embed_scale * x_ref[:, group_of(e, 2 * q + part)].astype(F32)
            scaled = block * inverse * gain[:, LANES * q : LANES * (q + 1)]
            at = 512 * part + LANES * q
            normed_ref[:, at : at + LANES] = scaled.astype(BF16)
    own = normed_ref[:, :512]
    far = normed_ref[:, 512:]
    project = lambda a, b: dot_f32(own, own_ref[:, a:b], CONTRACT_PLAIN) + dot_f32(
        far, far_ref[:, a:b], CONTRACT_PLAIN
    )
    rotate = lambda u: u * wide_table(cos_ref[...], u.shape[1]) + turn_halves(u) * wide_table(
        sin_ref[...], u.shape[1]
    )
    q_ref[...] = rotate(project(0, 1024)).astype(BF16)
    k_ref[...] = rotate(project(1024, 1536)).astype(BF16)
    v_ref[...] = project(1536, 2048).astype(BF16)
    allowed = allowed_of(column_ref, row_ref)

    def pair(step, _):
        wide = pl.ds(pl.multiple_of(step * 256, 256), 256)
        narrow = pl.ds(pl.multiple_of(step * LANES, LANES), LANES)
        q_block, k_block, v_block = q_ref[:, wide], k_ref[:, narrow], v_ref[:, narrow]
        outs = []
        for i in range(2):
            probs = attention_probs(heads_of(q_block, 2 * i, 2), heads_of(k_block, i, 1), allowed)
            rows = dot_f32(probs.astype(BF16), heads_of(v_block, i, 1), CONTRACT_PLAIN)
            outs += [rows[:SEQUENCE], rows[SEQUENCE:]]
        mixed_ref[:, wide] = jnp.concatenate(outs, axis=1).astype(BF16)
        return 0

    lax.fori_loop(0, 4, pair, 0)


def route_body(e_ref, x_ref, mixed_ref, w_own_ref, w_far_ref, small_own_ref, small_far_ref, code_ref,
               pay_ref, gates_ref, middle_ref, small_ref):
    e = e_ref[0]
    total = jnp.zeros((SEQUENCE, 1024), F32)
    for part, w_ref, s_ref in ((0, w_own_ref, small_own_ref), (1, w_far_ref, small_far_ref)):
        features = jnp.concatenate([mixed_ref[:, group_of(e, 2 * q + part)] for q in range(4)], axis=1)
        total = total + dot_f32(features, w_ref[...], CONTRACT_PLAIN)
        for q in range(4):
            small_ref[group_of(e, 2 * q + part), :] = s_ref[LANES * q : LANES * (q + 1), :]
    middle = embed_scale * x_ref[...].astype(F32) + resid_scale * total
    middle_ref[...] = middle
    gain = small_ref[...].astype(F32).T[GAIN_FFN : GAIN_FFN + 1, :]
    normed2 = (middle * inverse_rms(middle) * gain).astype(BF16)
    pay_ref[0:256, :] = normed2
    logits = dot_f32(normed2, small_ref[...], CONTRACT_PLAIN)
    code = code_ref[...]
    member = code >= 0.0
    masked = jnp.where(member, logits, -1e30)
    raised = jnp.where(member, jnp.exp(masked - jnp.max(masked, axis=1, keepdims=True)), 0.0)
    gates = raised / jnp.sum(raised, axis=1, keepdims=True)
    gates_ref[...] = gates
    rows = lambda value: value.T[:EXPERTS, :]
    turned = rows(gates)
    high = turned.astype(BF16).astype(F32)
    middle_part = (turned - high).astype(BF16).astype(F32)
    low = turned - high - middle_part
    pay_ref[256:288, :] = jnp.concatenate([rows(code), high, middle_part, low], axis=1).astype(BF16)


def turn_body(e_ref, sum_ref, add_ref, grad_ref, middle_ref, gates_ref, small_ref, normed2_ref, mixed_ref,
              w_own_ref, w_far_ref, own_ref, far_ref, mixed_grad_ref, middle_grad_ref, side_ref):
    e = e_ref[0]
    upstream = sum_ref[0:256, :].astype(F32) + add_ref[0:256, :].astype(F32)
    table = sum_ref[256:272, :].astype(F32) + add_ref[256:272, :].astype(F32)
    dots = jnp.concatenate([table[:, :256], table[:, 256:512]], axis=0) + jnp.concatenate(
        [table[:, 512:768], table[:, 768:]], axis=0
    )
    dots = jnp.concatenate([dots, jnp.zeros((LANES - EXPERTS, SEQUENCE), F32)], axis=0).T
    gates = gates_ref[...]
    logit_grads = (gates * (dots - jnp.sum(gates * dots, axis=1, keepdims=True))).astype(BF16)
    small = small_ref[...]
    upstream = upstream + dot_f32(logit_grads, small, CONTRACT_LAST)
    middle = middle_ref[...]
    inverse = inverse_rms(middle)
    unit = middle * inverse
    gain = small.astype(F32).T[GAIN_FFN : GAIN_FFN + 1, :]
    gain_grad = jnp.sum(upstream * unit, axis=0, keepdims=True)
    scaled = upstream * gain
    middle_grad = grad_ref[...].astype(F32) + inverse * (
        scaled - unit * jnp.mean(scaled * unit, axis=1, keepdims=True)
    )
    middle_grad_ref[...] = middle_grad
    attn_grad = (resid_scale * middle_grad).astype(BF16)
    line = lax.broadcasted_iota(jnp.int32, (LANES, 1024), 0)
    side_ref[...] = dot_f32(normed2_ref[0:256, :], logit_grads, CONTRACT_FIRST) + jnp.where(
        line == GAIN_FFN, gain_grad, 0.0
    ).T
    for part, w_ref, out_ref in ((0, w_own_ref, own_ref), (1, w_far_ref, far_ref)):
        features = jnp.concatenate([mixed_ref[:, group_of(e, 2 * q + part)] for q in range(4)], axis=1)
        out_ref[:, :1024] = dot_f32(features, attn_grad, CONTRACT_FIRST).astype(BF16)
        back = dot_f32(attn_grad, w_ref[...], CONTRACT_LAST).astype(BF16)
        for q in range(4):
            mixed_grad_ref[:, group_of(e, 2 * q + part)] = back[:, LANES * q : LANES * (q + 1)]
            at = slice(LANES * q, LANES * (q + 1))
            out_ref[at, 1024:] = side_ref[group_of(e, 2 * q + part), :].astype(BF16)


def attend_back_body(e_ref, x_ref, column_ref, row_ref, cos_ref, sin_ref, q_ref, k_ref, v_ref, grad_ref,
                     normed_ref, w_own_ref, w_far_ref, middle_grad_ref,
                     own_ref, far_ref, embed_ref, raw_ref, scaled_ref):
    e = e_ref[0]
    allowed = allowed_of(column_ref, row_ref)
    unrotate = lambda u: (
        u * wide_table(cos_ref[...], u.shape[1]) - turn_halves(u) * wide_table(sin_ref[...], u.shape[1])
    ).astype(BF16)

    def pair(step, _):
        wide = pl.ds(pl.multiple_of(step * 256, 256), 256)
        narrow = lambda base: pl.ds(pl.multiple_of(base + step * LANES, LANES), LANES)
        q_block, d_block = q_ref[:, wide], grad_ref[:, wide]
        k_block, v_block = k_ref[:, narrow(0)], v_ref[:, narrow(0)]
        q_outs, k_outs, v_outs = [], [], []
        for i in range(2):
            queries, keys = heads_of(q_block, 2 * i, 2), heads_of(k_block, i, 1)
            upstream = heads_of(d_block, 2 * i, 2)
            probs = attention_probs(queries, keys, allowed)
            prob_grads = dot_f32(upstream, heads_of(v_block, i, 1), CONTRACT_LAST)
            centre = jnp.sum(probs * prob_grads, axis=1, keepdims=True)
            score_grads = (probs * (prob_grads - centre)).astype(BF16)
            rows = dot_f32(score_grads, keys, CONTRACT_PLAIN) * attn_scale
            q_outs += [rows[:SEQUENCE], rows[SEQUENCE:]]
            k_outs.append(dot_f32(score_grads, queries, CONTRACT_FIRST) * attn_scale)
            v_outs.append(dot_f32(probs.astype(BF16), upstream, CONTRACT_FIRST))
        raw_ref[:, wide] = unrotate(jnp.concatenate(q_outs, axis=1))
        raw_ref[:, narrow(1024)] = unrotate(jnp.concatenate(k_outs, axis=1))
        raw_ref[:, narrow(1536)] = jnp.concatenate(v_outs, axis=1).astype(BF16)
        return 0

    lax.fori_loop(0, 4, pair, 0)
    resid = embed_scale * x_ref[...].astype(F32)
    inverse = inverse_rms(resid)
    for part, w_ref, out_ref in ((0, w_own_ref, own_ref), (1, w_far_ref, far_ref)):
        for c in range(4):
            at = slice(512 * c, 512 * c + 512)
            out_ref[:, at] = dot_f32(
                normed_ref[:, 512 * part : 512 * part + 512], raw_ref[:, at], CONTRACT_FIRST
            ).astype(BF16)
        back = dot_f32(raw_ref[...], w_ref[:, :2048], CONTRACT_LAST)
        gain = w_ref[:, 2048:].astype(F32).T[GAIN_ATTN : GAIN_ATTN + 1, :]
        gain_grads = []
        for q in range(4):
            at = slice(LANES * q, LANES * (q + 1))
            group = group_of(e, 2 * q + part)
            unit = embed_scale * x_ref[:, group].astype(F32) * inverse
            gain_grads.append(jnp.sum(back[:, at] * unit, axis=0, keepdims=True))
            scaled_ref[:, group] = back[:, at] * gain[:, at]
        line = lax.broadcasted_iota(jnp.int32, (LANES, 512), 0)
        side = jnp.where(line == GAIN_ATTN, jnp.concatenate(gain_grads, axis=1), 0.0).T
        out_ref[:, 2048:] = side.astype(BF16)
    unit = resid * inverse
    scaled = scaled_ref[...]
    resid_grad = middle_grad_ref[...] + inverse * (
        scaled - unit * jnp.mean(scaled * unit, axis=1, keepdims=True)
    )
    embed_ref[...] = (embed_scale * resid_grad).astype(BF16)


def local_kernel(body, name, outs, scratch, flops, number, *operands):
    bytes_moved = sum(a.size * a.dtype.itemsize for a in operands)
    vmem = pl.BlockSpec(memory_space=pltpu.VMEM)
    return pl.pallas_call(
        body,
        out_shape=[jax.ShapeDtypeStruct(shape, dtype) for shape, dtype in outs],
        in_specs=[pl.BlockSpec(memory_space=pltpu.SMEM)] + [vmem] * len(operands),
        out_specs=[vmem] * len(outs),
        scratch_shapes=[pltpu.VMEM(shape, dtype) for shape, dtype in scratch],
        compiler_params=pltpu.CompilerParams(vmem_limit_bytes=56 * 1024 * 1024),
        cost_estimate=pl.CostEstimate(flops=flops, bytes_accessed=bytes_moved, transcendentals=0),
        name=name,
    )(number, *operands)


def together(*values):
    return lax.optimization_barrier(values)


def plane_gather(value):
    return jnp.concatenate([value] + [over_expert(value, bits) for bits in (2, 4, 6)])


def plane_sum(total):
    rows = total.shape[0] // 4
    part = total[:rows].astype(F32)
    for q in (1, 2, 3):
        part = part + over_expert(total[rows * q : rows * q + rows], 2 * q).astype(F32)
    return part.astype(BF16)


def core_sum(own, far):
    return (own.astype(F32) + over_expert(far, 1).astype(F32)).astype(BF16)


def xor_order(pieces, at):
    stacked = jnp.stack(pieces)
    return jnp.concatenate(
        [lax.dynamic_index_in_dim(stacked, at ^ i, 0, keepdims=False) for i in range(len(pieces))]
    )


def shard_sum(plane, z):
    rows = lambda k: lax.dynamic_slice_in_dim(plane, (z ^ k) * 32, 32, 0)
    result = rows(0).astype(F32)
    for k in (1, 2, 3):
        result = result + over_shard(rows(k), k).astype(F32)
    return result


def exchange(slices):
    return lax.all_to_all(slices, "shard", split_axis=0, concat_axis=0, tiled=True)


def expert_slices(expert_in, expert_out, part):
    chosen = [OWN * (d % PAIR) + part for d in range(4)]
    return jnp.stack([jnp.concatenate([expert_in[c], expert_out[c]]) for c in chosen])


def per_device_fast(
    embedded,
    document_numbers,
    expert_ids,
    attn_gain,
    ffn_gain,
    w_query,
    key_projection,
    value_projection,
    w_out,
    w_router,
    expert_in,
    expert_out,
    cotangent,
):
    e = lax.axis_index("expert")
    z = lax.axis_index("shard")
    place = e.reshape(1)
    zeros = jnp.zeros((32, LANES - EXPERTS - 2), F32)
    small = [w_router, attn_gain[:, None], ffn_gain[:, None], zeros]
    pack = jnp.concatenate([w_query, key_projection, value_projection] + small + [w_out], axis=1)
    pack = pack.astype(BF16)
    plane = xor_order([pack] + [over_shard(pack, k) for k in (1, 2, 3)], z)
    slices = [expert_slices(expert_in, expert_out, part) for part in range(OWN)]
    plane, out_grad, slices[0] = together(plane, cotangent, slices[0])
    weights0 = exchange(slices[0])
    out_pair = jnp.stack([out_grad, over_shard(out_grad, 1)])
    in_own = plane_gather(plane[:, :2176])
    in_own, plane = together(in_own, plane)
    in_far = over_expert(in_own, 1)
    in_far, weights0 = together(in_far, weights0)
    out_w_own = plane_gather(plane[:, 2176:])
    out_w_own, out_pair = together(out_w_own, out_pair)
    out_w_far = over_expert(out_w_own, 1)
    out_own = plane_gather(out_pair)

    segments = document_numbers[0]
    column, row = segments[:, None], segments[None, :]
    cosine, sine = (jnp.concatenate([table] * 4, axis=1) for table in rope_tables(segments))
    lanes = jnp.arange(LANES, dtype=jnp.int32)
    member = jnp.any(expert_ids[:, :, None] == lanes, axis=1)
    index = jnp.arange(SEQUENCE, dtype=jnp.int32)
    below = (index[None, :] < index[:, None]).astype(BF16)
    rank = jnp.dot(below, member.astype(BF16), preferred_element_type=F32)
    code = jnp.where(member, rank, -1.0)

    wide, half = (SEQUENCE, 1024), (SEQUENCE, 512)
    normed, queries, keys, values, mixed = local_kernel(
        attend_body, "attend", [(wide, BF16), (wide, BF16), (half, BF16), (half, BF16), (wide, BF16)], [],
        4_000_000_000, place, embedded, column, row, cosine, sine, in_own, in_far,
    )
    payload, gates, middle, small_all = local_kernel(
        route_body, "route",
        [((288, 1024), BF16), ((SEQUENCE, LANES), F32), (wide, F32), ((1024, LANES), BF16)], [],
        2_000_000_000, place, embedded, mixed, out_w_own, out_w_far, in_own[:, 2048:], in_far[:, 2048:], code,
    )
    pay_pair = jnp.stack([payload, over_shard(payload, 1)])
    pay_pair, slices[1] = together(pay_pair, slices[1])
    weights1 = exchange(slices[1])
    tok_own = plane_gather(pay_pair)
    tok_own, out_own = together(tok_own, out_own)
    tok_far, out_far = over_expert(tok_own, 1), over_expert(out_own, 1)
    tok_far, weights1 = together(tok_far, weights1)
    first = (e * 4 + z % PAIR * OWN).reshape(1)
    operands = (tok_own, tok_far, out_own, out_far)
    *sums, expert_grad0 = expert_call(first, *operands, weights0)
    row_own, row_far, moe_own, moe_far, expert_grad1 = expert_call(first + 1, *operands, weights1, sums)
    slices0 = exchange(expert_grad0)
    slices0, row_far, expert_grad1 = together(slices0, row_far, expert_grad1)
    slices1 = exchange(expert_grad1)
    row_half = core_sum(row_own, row_far)
    row_half, moe_own, moe_far = together(row_half, moe_own, moe_far)
    moe_half = core_sum(moe_own, moe_far)
    row_pair = plane_sum(row_half)
    row_pair, moe_half, slices1 = together(row_pair, moe_half, slices1)
    returned = over_shard(row_pair[1], 1)
    moe_pair = plane_sum(moe_half)
    moe_other = over_shard(moe_pair[1], 1)
    early_own, early_far, mixed_grad, middle_grad = local_kernel(
        turn_body, "turn", [((512, 1152), BF16), ((512, 1152), BF16), (wide, BF16), (wide, F32)],
        [((1024, LANES), F32)], 4_000_000_000, place, row_pair[0], returned, cotangent, middle, gates,
        small_all, payload, mixed, out_w_own, out_w_far,
    )
    late_own, late_far, grad_embedded = local_kernel(
        attend_back_body, "attend_back", [((512, 2176), BF16), ((512, 2176), BF16), (wide, BF16)],
        [((SEQUENCE, 2048), BF16), (wide, F32)], 8_000_000_000, place, embedded, column, row, cosine, sine,
        queries, keys, values, mixed_grad, normed, in_own, in_far, middle_grad,
    )
    early_plane = plane_sum(core_sum(early_own, early_far))
    late_plane = plane_sum(core_sum(late_own, late_far))
    early = shard_sum(early_plane, z)
    late = shard_sum(late_plane, z)
    slices0, slices1 = slices0.astype(F32), slices1.astype(F32)
    expert_grads = jnp.stack(
        [slices0[0] + slices0[2], slices1[0] + slices1[2], slices0[1] + slices0[3], slices1[1] + slices1[3]]
    )
    grad_expert_in, grad_expert_out = expert_grads[:, :256], expert_grads[:, 256:]
    moe = moe_pair[0].astype(F32) + moe_other.astype(F32)
    output = (middle + resid_scale * moe).astype(BF16)
    return (
        output,
        grad_embedded,
        late[:, 2048 + GAIN_ATTN],
        early[:, 1024 + GAIN_FFN],
        late[:, :1024],
        late[:, 1024:1536],
        late[:, 1536:2048],
        early[:, :1024],
        early[:, 1024 : 1024 + EXPERTS],
        grad_expert_in,
        grad_expert_out,
    )


def solution(mesh):
    owners, shards = mesh.shape["expert"], mesh.shape["shard"]
    fast = owners == 8 and shards == 4
    both = ("expert", "shard")
    rows = P(both, None)
    weights = P("expert", "shard", None)
    return jax.shard_map(
        per_device_fast if fast else per_device_general,
        mesh=mesh,
        in_specs=(rows,) * 3 + (P(both),) * 2 + (rows,) * 5 + (weights,) * 2 + (rows,),
        out_specs=(rows,) * 2 + (P(both),) * 2 + (rows,) * 5 + (weights,) * 2,
        check_vma=False,
    )
```

```python
import functools

import jax
import jax.numpy as jnp
from jax import lax
from jax.experimental import pallas as pl
from jax.experimental.pallas import tpu as pltpu
from jax.sharding import PartitionSpec as P

MODEL_WIDTH = 1024
QUERY_HEADS = 16
KEY_VALUE_HEADS = 8
HEAD_SIZE = 64
FF = 512
EXPERTS = 32
TOPK = 8
CAP = 128


embed_scale = 12.0
attn_scale = 0.015625
resid_scale = 0.22
norm_eps = 1e-06
rope_base = 10000.0


def rope_tables(segments):
    sequence_length = segments.shape[0]
    key_index = jnp.arange(sequence_length, dtype=jnp.int32)
    change = jnp.concatenate([jnp.ones((1,), jnp.bool_), segments[1:] != segments[:-1]])
    begins = lax.cummax(jnp.where(change, key_index, 0), axis=0)
    places = (key_index - begins).astype(jnp.float32)
    freqs = rope_base ** (-2.0 * jnp.arange(HEAD_SIZE // 2, dtype=jnp.float32) / HEAD_SIZE)
    angles = places[:, None] * freqs[None, :]
    return (jnp.cos(angles), jnp.sin(angles))


def apply_rotation(value_heads, cosine_table, sine_table):
    halfway = value_heads.shape[-1] // 2
    first_half = value_heads[..., :halfway]
    second_half = value_heads[..., halfway:]
    cos_part = cosine_table[:, None, :]
    sin_part = sine_table[:, None, :]
    return jnp.concatenate(
        [
            first_half * cos_part - second_half * sin_part,
            second_half * cos_part + first_half * sin_part,
        ],
        axis=-1,
    )


def reverse_rotation(grads, cosine_table, sine_table):
    halfway = grads.shape[-1] // 2
    first_half = grads[..., :halfway]
    second_half = grads[..., halfway:]
    cos_part = cosine_table[:, None, :]
    sin_part = sine_table[:, None, :]
    return jnp.concatenate(
        [
            first_half * cos_part + second_half * sin_part,
            second_half * cos_part - first_half * sin_part,
        ],
        axis=-1,
    )


def norm_forward(value_heads):
    inverse = lax.rsqrt(jnp.mean(value_heads * value_heads, axis=1, keepdims=True) + norm_eps)
    return (value_heads * inverse, inverse)


def norm_backward(upstream, unit_values, inverse, gain):
    scaled = upstream * gain
    grad_values = inverse * (
        scaled - unit_values * jnp.mean(scaled * unit_values, axis=1, keepdims=True)
    )
    return (grad_values, jnp.sum(upstream * unit_values, axis=0))


def slot_tables(expert_ids):
    flat_ids = expert_ids.reshape(-1)
    count_all = flat_ids.shape[0]
    matches = (flat_ids[:, None] == jnp.arange(EXPERTS, dtype=jnp.int32)[None, :]).astype(jnp.int32)
    before = jnp.cumsum(matches, axis=0) - 1
    ranking = jnp.sum(before * matches, axis=1)
    target = flat_ids * CAP + ranking
    source = (
        jnp.zeros((EXPERTS * CAP,), jnp.int32)
        .at[target]
        .set(jnp.arange(count_all, dtype=jnp.int32))
    )
    filled = (
        jnp.zeros((EXPERTS * CAP,), jnp.int32).at[target].set(jnp.ones((count_all,), jnp.int32))
    )
    return (target, source, filled)


def silu_parts(gate_up):
    gate_part = gate_up[..., :FF]
    up_part = gate_up[..., FF:]
    sigmoid_gate = jax.nn.sigmoid(gate_part)
    hidden = (gate_part * sigmoid_gate * up_part).astype(jnp.bfloat16)
    return (gate_part, up_part, sigmoid_gate, hidden)


def per_device_general(
    embedded,
    document_numbers,
    expert_ids,
    attn_gain,
    ffn_gain,
    w_query,
    key_projection,
    value_projection,
    w_out,
    w_router,
    expert_in,
    expert_out,
    cotangent,
):
    mixer = (
        lax.all_gather(attn_gain.astype(jnp.bfloat16), ("expert", "shard"), axis=0, tiled=True),
        lax.all_gather(ffn_gain.astype(jnp.bfloat16), ("expert", "shard"), axis=0, tiled=True),
        lax.all_gather(w_query.astype(jnp.bfloat16), ("expert", "shard"), axis=0, tiled=True),
        lax.all_gather(
            key_projection.astype(jnp.bfloat16), ("expert", "shard"), axis=0, tiled=True
        ),
        lax.all_gather(
            value_projection.astype(jnp.bfloat16), ("expert", "shard"), axis=0, tiled=True
        ),
        lax.all_gather(w_out.astype(jnp.bfloat16), ("expert", "shard"), axis=0, tiled=True),
        lax.all_gather(w_router.astype(jnp.bfloat16), ("expert", "shard"), axis=0, tiled=True),
    )
    gain_attn, gain_ffn, query_w, key_w, value_w, out_w, router_w = mixer
    full_in, full_out = (
        lax.all_gather(expert_in, "shard", axis=1, tiled=True),
        lax.all_gather(expert_out, "shard", axis=1, tiled=True),
    )
    sequence_length = embedded.shape[0]
    query_groups = QUERY_HEADS // KEY_VALUE_HEADS
    owners = lax.axis_size("expert")
    local_count = EXPERTS // owners
    received = owners * CAP
    resid = embed_scale * embedded.astype(jnp.float32)
    unit_attn, inverse_attn = norm_forward(resid)
    normed = (unit_attn * gain_attn.astype(jnp.float32)).astype(jnp.bfloat16)
    unrotated_query = jnp.dot(normed, query_w, preferred_element_type=jnp.float32)
    unrotated_key = jnp.dot(normed, key_w, preferred_element_type=jnp.float32)
    projected_value = jnp.dot(normed, value_w, preferred_element_type=jnp.float32)
    segments = document_numbers[0]
    cosine_table, sine_table = rope_tables(segments)
    query_heads = (
        apply_rotation(
            unrotated_query.reshape(sequence_length, QUERY_HEADS, HEAD_SIZE),
            cosine_table,
            sine_table,
        )
        .astype(jnp.bfloat16)
        .reshape(sequence_length, KEY_VALUE_HEADS, query_groups, HEAD_SIZE)
    )
    key_heads = apply_rotation(
        unrotated_key.reshape(sequence_length, KEY_VALUE_HEADS, HEAD_SIZE), cosine_table, sine_table
    ).astype(jnp.bfloat16)
    value_heads = projected_value.astype(jnp.bfloat16).reshape(
        sequence_length, KEY_VALUE_HEADS, HEAD_SIZE
    )
    block_rows = min(512, sequence_length)
    starts = jnp.arange(sequence_length // block_rows, dtype=jnp.int32) * block_rows
    key_index = jnp.arange(sequence_length, dtype=jnp.int32)

    def block_scores(first_row):
        row_index = first_row + jnp.arange(block_rows, dtype=jnp.int32)
        raw_scores = (
            jnp.einsum("qhgd,khd->hgqk", query_heads, key_heads, preferred_element_type=jnp.float32)
            * attn_scale
        )
        allowed = (key_index[None, :] <= row_index[:, None]) & (
            segments[None, :] == segments[:, None]
        )
        return (jnp.where(allowed, raw_scores, -1e30), query_heads)

    def attend_block(first_row):
        scores, query_rows = block_scores(first_row)
        row_max = jnp.max(scores, axis=-1, keepdims=True)
        exps = jnp.exp(scores - row_max)
        totals = jnp.sum(exps, axis=-1, keepdims=True)
        weights = (exps / totals).astype(jnp.bfloat16)
        mixed_rows = jnp.einsum(
            "hgqk,khd->qhgd", weights, value_heads, preferred_element_type=jnp.float32
        )
        return (mixed_rows.astype(jnp.bfloat16), (row_max + jnp.log(totals))[..., 0])

    mixed_blocks, log_totals = lax.map(attend_block, starts)
    mixed_heads_output = mixed_blocks.reshape(sequence_length, QUERY_HEADS * HEAD_SIZE)
    middle = resid + resid_scale * jnp.dot(
        mixed_heads_output, out_w, preferred_element_type=jnp.float32
    )
    unit_ffn, inverse_ffn = norm_forward(middle)
    normed2 = (unit_ffn * gain_ffn.astype(jnp.float32)).astype(jnp.bfloat16)
    logits = jnp.dot(normed2, router_w, preferred_element_type=jnp.float32)
    pick_table = expert_ids[:, :, None] == jnp.arange(EXPERTS, dtype=jnp.int32)[None, None, :]
    chosen = jnp.sum(jnp.where(pick_table, logits[:, None, :], 0.0), axis=2)
    exps_chosen = jnp.exp(chosen - jnp.max(chosen, axis=1, keepdims=True))
    gates = exps_chosen / jnp.sum(exps_chosen, axis=1, keepdims=True)
    target, source, filled = slot_tables(expert_ids)
    live_slots = filled[:, None] == 1
    zero_bf = jnp.zeros((), jnp.bfloat16)
    send_rows = jnp.where(live_slots, normed2[source // TOPK], zero_bf).reshape(
        owners, local_count, CAP, MODEL_WIDTH
    )
    arrived = lax.all_to_all(send_rows, "expert", split_axis=0, concat_axis=2, tiled=True).reshape(
        local_count, received, MODEL_WIDTH
    )
    gate_up = jnp.einsum("erd,edf->erf", arrived, full_in, preferred_element_type=jnp.float32)
    gate_part, up_part, sigmoid_gate, hidden = silu_parts(gate_up)
    produced = jnp.einsum(
        "erf,efd->erd", hidden, full_out, preferred_element_type=jnp.float32
    ).astype(jnp.bfloat16)
    returned = lax.all_to_all(
        produced.reshape(1, local_count, received, MODEL_WIDTH),
        "expert",
        split_axis=2,
        concat_axis=0,
        tiled=True,
    ).reshape(EXPERTS * CAP, MODEL_WIDTH)
    slot_values = returned[target].reshape(sequence_length, TOPK, MODEL_WIDTH)
    moe = jnp.einsum("tk,tkd->td", gates, slot_values.astype(jnp.float32))
    output = (middle + resid_scale * moe).astype(jnp.bfloat16)
    grad_output = cotangent.astype(jnp.float32)
    grad_mix = resid_scale * grad_output
    gate_grads = jnp.einsum("tkd,td->tk", slot_values.astype(jnp.float32), grad_mix)
    slot_grads = (
        (gates[:, :, None] * grad_mix[:, None, :])
        .astype(jnp.bfloat16)
        .reshape(sequence_length * TOPK, MODEL_WIDTH)
    )
    grad_send = jnp.where(live_slots, slot_grads[source], zero_bf).reshape(
        owners, local_count, CAP, MODEL_WIDTH
    )
    grad_arrived = lax.all_to_all(
        grad_send, "expert", split_axis=0, concat_axis=2, tiled=True
    ).reshape(local_count, received, MODEL_WIDTH)
    owner_rows = lax.all_to_all(
        send_rows, "expert", split_axis=0, concat_axis=2, tiled=True
    ).reshape(local_count, received, MODEL_WIDTH)
    owner_gate_up = jnp.einsum(
        "erd,edf->erf", owner_rows, full_in, preferred_element_type=jnp.float32
    )
    owner_gate, owner_up, owner_sigmoid, owner_hidden = silu_parts(owner_gate_up)
    hidden_grad = jnp.einsum(
        "erd,efd->erf", grad_arrived, full_out, preferred_element_type=jnp.float32
    )
    gate_grad_part = (
        hidden_grad * owner_up * owner_sigmoid * (1.0 + owner_gate * (1.0 - owner_sigmoid))
    )
    up_grad_part = hidden_grad * owner_gate * owner_sigmoid
    gate_up_grad = jnp.concatenate([gate_grad_part, up_grad_part], axis=-1).astype(jnp.bfloat16)
    grad_full_out = jnp.einsum(
        "erf,erd->efd", owner_hidden, grad_arrived, preferred_element_type=jnp.float32
    )
    grad_full_in = jnp.einsum(
        "erd,erf->edf", owner_rows, gate_up_grad, preferred_element_type=jnp.float32
    )
    row_grads = jnp.einsum(
        "erf,edf->erd", gate_up_grad, full_in, preferred_element_type=jnp.float32
    ).astype(jnp.bfloat16)
    grad_returned = lax.all_to_all(
        row_grads.reshape(1, local_count, received, MODEL_WIDTH),
        "expert",
        split_axis=2,
        concat_axis=0,
        tiled=True,
    ).reshape(EXPERTS * CAP, MODEL_WIDTH)
    grad_expert_in, grad_expert_out = (
        lax.psum_scatter(
            grad_full_in.astype(jnp.bfloat16), "shard", scatter_dimension=1, tiled=True
        ).astype(jnp.float32),
        lax.psum_scatter(
            grad_full_out.astype(jnp.bfloat16), "shard", scatter_dimension=1, tiled=True
        ).astype(jnp.float32),
    )
    mixer_back = (
        lax.all_gather(attn_gain.astype(jnp.bfloat16), ("expert", "shard"), axis=0, tiled=True),
        lax.all_gather(ffn_gain.astype(jnp.bfloat16), ("expert", "shard"), axis=0, tiled=True),
        lax.all_gather(w_query.astype(jnp.bfloat16), ("expert", "shard"), axis=0, tiled=True),
        lax.all_gather(
            key_projection.astype(jnp.bfloat16), ("expert", "shard"), axis=0, tiled=True
        ),
        lax.all_gather(
            value_projection.astype(jnp.bfloat16), ("expert", "shard"), axis=0, tiled=True
        ),
        lax.all_gather(w_out.astype(jnp.bfloat16), ("expert", "shard"), axis=0, tiled=True),
        lax.all_gather(w_router.astype(jnp.bfloat16), ("expert", "shard"), axis=0, tiled=True),
    )
    back_gain_attn, back_gain_ffn, back_query, back_key, back_value, back_out, back_router = (
        mixer_back
    )
    chosen_grad = gates * (gate_grads - jnp.sum(gates * gate_grads, axis=1, keepdims=True))
    logit_grads = jnp.sum(jnp.where(pick_table, chosen_grad[:, :, None], 0.0), axis=1).astype(
        jnp.bfloat16
    )
    grad_router_full = jnp.einsum(
        "td,te->de", normed2, logit_grads, preferred_element_type=jnp.float32
    )
    normed2_grad = jnp.sum(
        grad_returned[target].reshape(sequence_length, TOPK, MODEL_WIDTH), axis=1, dtype=jnp.float32
    )
    normed2_grad = normed2_grad + jnp.einsum(
        "te,de->td", logit_grads, back_router, preferred_element_type=jnp.float32
    )
    middle_norm_grad, grad_gain_ffn = norm_backward(
        normed2_grad, unit_ffn, inverse_ffn, back_gain_ffn.astype(jnp.float32)
    )
    middle_grad = grad_output + middle_norm_grad
    attn_grad = (resid_scale * middle_grad).astype(jnp.bfloat16)
    grad_out_full = jnp.einsum(
        "tf,td->fd", mixed_heads_output, attn_grad, preferred_element_type=jnp.float32
    )
    mixed_output_gradient = jnp.einsum(
        "td,fd->tf", attn_grad, back_out, preferred_element_type=jnp.float32
    ).astype(jnp.bfloat16)
    mixed_gradient_by_head = mixed_output_gradient.reshape(
        sequence_length, KEY_VALUE_HEADS, query_groups, HEAD_SIZE
    )

    def attend_back(carries, packed):
        key_acc, value_acc = carries
        first_row, log_rows = packed
        scores, query_rows = block_scores(first_row)
        probs = jnp.exp(scores - log_rows[..., None])
        prob_grads = jnp.einsum(
            "qhgd,khd->hgqk",
            mixed_gradient_by_head,
            value_heads,
            preferred_element_type=jnp.float32,
        )
        score_grads = (
            probs * (prob_grads - jnp.sum(probs * prob_grads, axis=-1, keepdims=True))
        ).astype(jnp.bfloat16)
        query_grads = (
            jnp.einsum("hgqk,khd->qhgd", score_grads, key_heads, preferred_element_type=jnp.float32)
            * attn_scale
        )
        key_acc = (
            key_acc
            + jnp.einsum(
                "hgqk,qhgd->khd", score_grads, query_rows, preferred_element_type=jnp.float32
            )
            * attn_scale
        )
        value_acc = value_acc + jnp.einsum(
            "hgqk,qhgd->khd",
            probs.astype(jnp.bfloat16),
            mixed_gradient_by_head,
            preferred_element_type=jnp.float32,
        )
        return ((key_acc, value_acc), query_grads)

    empty_head_rows = jnp.zeros((sequence_length, KEY_VALUE_HEADS, HEAD_SIZE), jnp.float32)
    (summed_key_gradient, summed_value_gradient), query_grad_blocks = lax.scan(
        attend_back, (empty_head_rows, empty_head_rows), (starts, log_totals)
    )
    query_raw_grad = (
        reverse_rotation(
            query_grad_blocks.reshape(sequence_length, QUERY_HEADS, HEAD_SIZE),
            cosine_table,
            sine_table,
        )
        .astype(jnp.bfloat16)
        .reshape(sequence_length, QUERY_HEADS * HEAD_SIZE)
    )
    key_raw_grad = (
        reverse_rotation(summed_key_gradient, cosine_table, sine_table)
        .astype(jnp.bfloat16)
        .reshape(sequence_length, KEY_VALUE_HEADS * HEAD_SIZE)
    )
    projected_value_gradient = summed_value_gradient.astype(jnp.bfloat16).reshape(
        sequence_length, KEY_VALUE_HEADS * HEAD_SIZE
    )
    grad_query_full = jnp.einsum(
        "td,tf->df", normed, query_raw_grad, preferred_element_type=jnp.float32
    )
    grad_key_full = jnp.einsum(
        "td,tf->df", normed, key_raw_grad, preferred_element_type=jnp.float32
    )
    grad_value_full = jnp.einsum(
        "td,tf->df", normed, projected_value_gradient, preferred_element_type=jnp.float32
    )
    normed_grad = jnp.einsum(
        "tf,df->td", query_raw_grad, back_query, preferred_element_type=jnp.float32
    )
    normed_grad = normed_grad + jnp.einsum(
        "tf,df->td", key_raw_grad, back_key, preferred_element_type=jnp.float32
    )
    normed_grad = normed_grad + jnp.einsum(
        "tf,df->td", projected_value_gradient, back_value, preferred_element_type=jnp.float32
    )
    resid_norm_grad, grad_gain_attn = norm_backward(
        normed_grad, unit_attn, inverse_attn, back_gain_attn.astype(jnp.float32)
    )
    resid_grad = middle_grad + resid_norm_grad
    grad_embedded = (embed_scale * resid_grad).astype(jnp.bfloat16)
    summed = (
        lax.psum_scatter(grad_gain_attn, ("expert", "shard"), scatter_dimension=0, tiled=True),
        lax.psum_scatter(grad_gain_ffn, ("expert", "shard"), scatter_dimension=0, tiled=True),
        lax.psum_scatter(grad_query_full, ("expert", "shard"), scatter_dimension=0, tiled=True),
        lax.psum_scatter(grad_key_full, ("expert", "shard"), scatter_dimension=0, tiled=True),
        lax.psum_scatter(grad_value_full, ("expert", "shard"), scatter_dimension=0, tiled=True),
        lax.psum_scatter(grad_out_full, ("expert", "shard"), scatter_dimension=0, tiled=True),
        lax.psum_scatter(grad_router_full, ("expert", "shard"), scatter_dimension=0, tiled=True),
    )
    return (
        output,
        grad_embedded,
        summed[0],
        summed[1],
        summed[2],
        summed[3],
        summed[4],
        summed[5],
        summed[6],
        grad_expert_in,
        grad_expert_out,
    )


BF16 = jnp.bfloat16
F32 = jnp.float32
PAIR = 2
OWN = 2


def over_expert(value, bits):
    return lax.ppermute(value, "expert", [(i, i ^ bits) for i in range(8)])


def over_shard(value, bits):
    return lax.ppermute(value, "shard", [(i, i ^ bits) for i in range(4)])


def dot_f32(left, right, dims):
    return lax.dot_general(left, right, dims, preferred_element_type=F32)


CONTRACT_LAST = (((1,), (1,)), ((), ()))
CONTRACT_FIRST = (((0,), (0,)), ((), ()))
CONTRACT_PLAIN = (((1,), (0,)), ((), ()))
BLOCKS = 8
HALF = 4
ROWS = HALF * CAP
PAY_ROWS = 288
SUM_ROWS = 272


def expert_body(first_part, number_ref, *refs):
    refs = list(refs)
    take = lambda count: [refs.pop(0) for _ in range(count)]
    tok_refs, out_refs = take(BLOCKS), take(BLOCKS)
    (w_ref,) = take(1)
    row_before, moe_before = ([], []) if first_part else (take(BLOCKS), take(BLOCKS))
    row_outs, moe_outs = take(BLOCKS), take(BLOCKS)
    (grad_ref,) = take(1)
    (tok_s, out_s, w_s, row_s, moe_s, grad_s, x_s, g_s, gate_s, table_s, back_s, mix_s, dot_s,
     in_acc, out_acc, tok_sem, out_sem, w_sem, row_sem, moe_sem, row_out_sem, moe_out_sem, grad_sem) = refs
    number = number_ref[0]
    copy = pltpu.make_async_copy
    for j in range(BLOCKS):
        copy(tok_refs[j], tok_s.at[j], tok_sem.at[j]).start()
        copy(out_refs[j], out_s.at[j], out_sem.at[j]).start()
        if j == HALF - 1:
            copy(w_ref, w_s, w_sem.at[0]).start()
    if not first_part:
        for j in range(BLOCKS):
            copy(row_before[j], row_s.at[j], row_sem.at[j]).start()
            copy(moe_before[j], moe_s.at[j], moe_sem.at[j]).start()

    def mask_of(i):
        slot = lax.broadcasted_iota(jnp.int32, (CAP, 256), 0).astype(F32)
        return slot == table_s[i, 0:1, :]

    def half_step(half, _):
        for i in range(HALF):
            j = half * HALF + i
            copy(tok_s.at[j], tok_s.at[j], tok_sem.at[j]).wait()
            copy(out_s.at[j], out_s.at[j], out_sem.at[j]).wait()
            aux = tok_s[j, 256:PAY_ROWS, :].astype(F32)
            line = lax.broadcasted_iota(jnp.int32, (EXPERTS, 1024), 0)
            line = jnp.sum(jnp.where(line == number, aux, 0.0), axis=0, keepdims=True)
            table_s[i, 0:1, :] = line[:, :256]
            gate = line[:, 256:512] + line[:, 512:768] + line[:, 768:]
            mask = mask_of(i)
            pick = jnp.where(mask, 1.0, 0.0).astype(BF16)
            at = slice(i * CAP, (i + 1) * CAP)
            x_s[at, :] = dot_f32(pick, tok_s[j, 0:256, :], CONTRACT_PLAIN).astype(BF16)
            g_s[at, :] = resid_scale * dot_f32(pick, out_s[j], CONTRACT_PLAIN)
            gate_s[at, :] = jnp.sum(jnp.where(mask, gate, 0.0), axis=1, keepdims=True)

        @pl.when(half == 0)
        def _():
            copy(w_ref, w_s, w_sem.at[0]).wait()

        w_in = w_s[:, 0:256, :].reshape(1024, 1024)
        w_out = w_s[:, 256:384, :].reshape(512, 1024)
        x = x_s[...]
        gate_up = dot_f32(x, w_in, CONTRACT_PLAIN)
        gate_part, up_part = gate_up[:, :FF], gate_up[:, FF:]
        sigmoid = jax.nn.sigmoid(gate_part)
        hidden = (gate_part * sigmoid * up_part).astype(BF16)
        produced = dot_f32(hidden, w_out, CONTRACT_PLAIN).astype(BF16).astype(F32)
        slot_gate = gate_s[...]
        scaled = g_s[...]
        slot_grad = (slot_gate * scaled).astype(BF16)
        dot_s[...] = jnp.sum(produced * scaled, axis=1, keepdims=True)
        mix_s[...] = (slot_gate * produced).astype(BF16)
        hidden_grad = dot_f32(slot_grad, w_out, CONTRACT_LAST)
        gate_grad = hidden_grad * up_part * sigmoid * (1.0 + gate_part * (1.0 - sigmoid))
        up_grad = hidden_grad * gate_part * sigmoid
        gate_up_grad = jnp.concatenate([gate_grad.astype(BF16), up_grad.astype(BF16)], axis=1)
        back_s[...] = dot_f32(gate_up_grad, w_in, CONTRACT_LAST).astype(BF16)
        in_part = dot_f32(x, gate_up_grad, CONTRACT_FIRST)
        out_part = dot_f32(hidden, slot_grad, CONTRACT_FIRST)

        @pl.when(half == 0)
        def _():
            in_acc[...] = in_part
            out_acc[...] = out_part

        @pl.when(half == 1)
        def _():
            for d in range(4):
                wide, narrow = slice(d * 256, (d + 1) * 256), slice(d * 128, (d + 1) * 128)
                grad_s[d, 0:256, :] = (in_acc[wide, :] + in_part[wide, :]).astype(BF16)
                grad_s[d, 256:384, :] = (out_acc[narrow, :] + out_part[narrow, :]).astype(BF16)
            copy(grad_s, grad_ref, grad_sem.at[0]).start()

        for i in range(HALF):
            j = half * HALF + i
            at = slice(i * CAP, (i + 1) * CAP)
            mask = mask_of(i)
            pick = jnp.where(mask, 1.0, 0.0).astype(BF16)
            rows = dot_f32(pick, back_s[at, :], CONTRACT_FIRST)
            mixed = dot_f32(pick, mix_s[at, :], CONTRACT_FIRST)
            dots = jnp.sum(jnp.where(mask, dot_s[at, :], 0.0), axis=0, keepdims=True)
            high = dots.astype(BF16).astype(F32)
            low = dots - high
            wide = jnp.concatenate([high, high, low, low], axis=1)
            line = lax.broadcasted_iota(jnp.int32, (16, 1024), 0)
            lane = lax.broadcasted_iota(jnp.int32, (16, 1024), 1) // 256
            here = (line == number % 16) & (lane % 2 == number // 16)
            side = jnp.where(here, jnp.broadcast_to(wide, (16, 1024)), 0.0)
            if not first_part:
                copy(row_s.at[j], row_s.at[j], row_sem.at[j]).wait()
                copy(moe_s.at[j], moe_s.at[j], moe_sem.at[j]).wait()
                rows = rows + row_s[j, 0:256, :].astype(F32)
                mixed = mixed + moe_s[j].astype(F32)
                side = side + row_s[j, 256:SUM_ROWS, :].astype(F32)
            row_s[j, 0:256, :] = rows.astype(BF16)
            row_s[j, 256:SUM_ROWS, :] = side.astype(BF16)
            moe_s[j] = mixed.astype(BF16)
            for part in range(2):

                @pl.when(half == part)
                def _():
                    k = part * HALF + i
                    copy(row_s.at[k], row_outs[k], row_out_sem.at[k]).start()
                    copy(moe_s.at[k], moe_outs[k], moe_out_sem.at[k]).start()

        return 0

    lax.fori_loop(0, 2, half_step, 0)
    copy(grad_s, grad_ref, grad_sem.at[0]).wait()
    for j in range(BLOCKS):
        copy(row_s.at[j], row_outs[j], row_out_sem.at[j]).wait()
        copy(moe_s.at[j], moe_outs[j], moe_out_sem.at[j]).wait()


def expert_call(number, tokens, grads, weights, before=None):
    operands = list(tokens) + list(grads) + [weights] + ([] if before is None else list(before))
    block = lambda rows: jax.ShapeDtypeStruct((rows, 1024), BF16)
    outs = [block(SUM_ROWS)] * BLOCKS + [block(256)] * BLOCKS + [jax.ShapeDtypeStruct((4, 384, 1024), BF16)]
    anywhere = pl.BlockSpec(memory_space=pl.ANY)
    blocks = lambda rows: pltpu.VMEM((BLOCKS, rows, 1024), BF16)
    column, wide = pltpu.VMEM((ROWS, 1), F32), pltpu.VMEM((ROWS, 1024), BF16)
    sems = [pltpu.SemaphoreType.DMA((count,)) for count in (8, 8, 1, 8, 8, 8, 8, 1)]
    results = pl.pallas_call(
        functools.partial(expert_body, before is None),
        out_shape=outs,
        in_specs=[pl.BlockSpec(memory_space=pltpu.SMEM)] + [anywhere] * len(operands),
        out_specs=[anywhere] * len(outs),
        scratch_shapes=[
            blocks(PAY_ROWS), blocks(256), pltpu.VMEM((4, 384, 1024), BF16), blocks(SUM_ROWS), blocks(256),
            pltpu.VMEM((4, 384, 1024), BF16), wide, pltpu.VMEM((ROWS, 1024), F32), column,
            pltpu.VMEM((HALF, 8, 256), F32), wide, wide, column,
            pltpu.VMEM((1024, 1024), F32), pltpu.VMEM((512, 1024), F32),
        ] + sems,
        compiler_params=pltpu.CompilerParams(vmem_limit_bytes=60 * 1024 * 1024),
        cost_estimate=pl.CostEstimate(
            flops=12_000_000_000, bytes_accessed=30_000_000, transcendentals=1_000_000
        ),
        name="expert",
    )(number, *operands)
    return results[: 2 * BLOCKS], results[2 * BLOCKS]


LANES = 128
GAIN_ATTN = 32
GAIN_FFN = 33
SEQUENCE = 256


def group_of(e, r):
    return pl.ds(pl.multiple_of((e ^ r) * LANES, LANES), LANES)


def turn_halves(value):
    lane = lax.broadcasted_iota(jnp.int32, value.shape, 1) % HEAD_SIZE
    width = value.shape[1]
    return jnp.where(
        lane < HEAD_SIZE // 2,
        -pltpu.roll(value, width - HEAD_SIZE // 2, 1),
        pltpu.roll(value, HEAD_SIZE // 2, 1),
    )


def wide_table(table, width):
    return jnp.concatenate([table] * (width // LANES), axis=1)


def inverse_rms(value):
    return lax.rsqrt(jnp.mean(value * value, axis=1, keepdims=True) + norm_eps)


def attention_probs(queries, keys, allowed):
    scores = jnp.where(allowed, dot_f32(queries, keys, CONTRACT_LAST) * attn_scale, -1e30)
    exps = jnp.exp(scores - jnp.max(scores, axis=1, keepdims=True))
    return exps / jnp.sum(exps, axis=1, keepdims=True)


def allowed_of(column_ref, row_ref):
    shape = (2 * SEQUENCE, SEQUENCE)
    query = lax.broadcasted_iota(jnp.int32, shape, 0) % SEQUENCE
    key = lax.broadcasted_iota(jnp.int32, shape, 1)
    column = column_ref[...]
    same = jnp.concatenate([column, column], axis=0) == row_ref[...]
    return (key <= query) & same


def heads_of(block, first, count):
    return jnp.concatenate(
        [block[:, HEAD_SIZE * (first + i) : HEAD_SIZE * (first + i + 1)] for i in range(count)], axis=0
    )


def attend_body(e_ref, x_ref, column_ref, row_ref, cos_ref, sin_ref, own_ref, far_ref,
                normed_ref, q_ref, k_ref, v_ref, mixed_ref):
    e = e_ref[0]
    resid = embed_scale * x_ref[...].astype(F32)
    inverse = inverse_rms(resid)
    for part, w_ref in ((0, own_ref), (1, far_ref)):
        gain = w_ref[:, 2048:].astype(F32).T[GAIN_ATTN : GAIN_ATTN + 1, :]
        for q in range(4):
            block = embed_scale * x_ref[:, group_of(e, 2 * q + part)].astype(F32)
            scaled = block * inverse * gain[:, LANES * q : LANES * (q + 1)]
            at = 512 * part + LANES * q
            normed_ref[:, at : at + LANES] = scaled.astype(BF16)
    own = normed_ref[:, :512]
    far = normed_ref[:, 512:]
    project = lambda a, b: dot_f32(own, own_ref[:, a:b], CONTRACT_PLAIN) + dot_f32(
        far, far_ref[:, a:b], CONTRACT_PLAIN
    )
    rotate = lambda u: u * wide_table(cos_ref[...], u.shape[1]) + turn_halves(u) * wide_table(
        sin_ref[...], u.shape[1]
    )
    q_ref[...] = rotate(project(0, 1024)).astype(BF16)
    k_ref[...] = rotate(project(1024, 1536)).astype(BF16)
    v_ref[...] = project(1536, 2048).astype(BF16)
    allowed = allowed_of(column_ref, row_ref)

    def pair(step, _):
        wide = pl.ds(pl.multiple_of(step * 256, 256), 256)
        narrow = pl.ds(pl.multiple_of(step * LANES, LANES), LANES)
        q_block, k_block, v_block = q_ref[:, wide], k_ref[:, narrow], v_ref[:, narrow]
        outs = []
        for i in range(2):
            probs = attention_probs(heads_of(q_block, 2 * i, 2), heads_of(k_block, i, 1), allowed)
            rows = dot_f32(probs.astype(BF16), heads_of(v_block, i, 1), CONTRACT_PLAIN)
            outs += [rows[:SEQUENCE], rows[SEQUENCE:]]
        mixed_ref[:, wide] = jnp.concatenate(outs, axis=1).astype(BF16)
        return 0

    lax.fori_loop(0, 4, pair, 0)


def route_body(e_ref, x_ref, mixed_ref, w_own_ref, w_far_ref, small_own_ref, small_far_ref, code_ref,
               pay_ref, gates_ref, middle_ref, small_ref):
    e = e_ref[0]
    total = jnp.zeros((SEQUENCE, 1024), F32)
    for part, w_ref, s_ref in ((0, w_own_ref, small_own_ref), (1, w_far_ref, small_far_ref)):
        features = jnp.concatenate([mixed_ref[:, group_of(e, 2 * q + part)] for q in range(4)], axis=1)
        total = total + dot_f32(features, w_ref[...], CONTRACT_PLAIN)
        for q in range(4):
            small_ref[group_of(e, 2 * q + part), :] = s_ref[LANES * q : LANES * (q + 1), :]
    middle = embed_scale * x_ref[...].astype(F32) + resid_scale * total
    middle_ref[...] = middle
    gain = small_ref[...].astype(F32).T[GAIN_FFN : GAIN_FFN + 1, :]
    normed2 = (middle * inverse_rms(middle) * gain).astype(BF16)
    pay_ref[0:256, :] = normed2
    logits = dot_f32(normed2, small_ref[...], CONTRACT_PLAIN)
    code = code_ref[...]
    member = code >= 0.0
    masked = jnp.where(member, logits, -1e30)
    raised = jnp.where(member, jnp.exp(masked - jnp.max(masked, axis=1, keepdims=True)), 0.0)
    gates = raised / jnp.sum(raised, axis=1, keepdims=True)
    gates_ref[...] = gates
    rows = lambda value: value.T[:EXPERTS, :]
    turned = rows(gates)
    high = turned.astype(BF16).astype(F32)
    middle_part = (turned - high).astype(BF16).astype(F32)
    low = turned - high - middle_part
    pay_ref[256:288, :] = jnp.concatenate([rows(code), high, middle_part, low], axis=1).astype(BF16)


def turn_body(e_ref, sum_ref, add_ref, grad_ref, middle_ref, gates_ref, small_ref, normed2_ref, mixed_ref,
              w_own_ref, w_far_ref, own_ref, far_ref, mixed_grad_ref, middle_grad_ref, side_ref):
    e = e_ref[0]
    upstream = sum_ref[0:256, :].astype(F32) + add_ref[0:256, :].astype(F32)
    table = sum_ref[256:272, :].astype(F32) + add_ref[256:272, :].astype(F32)
    dots = jnp.concatenate([table[:, :256], table[:, 256:512]], axis=0) + jnp.concatenate(
        [table[:, 512:768], table[:, 768:]], axis=0
    )
    dots = jnp.concatenate([dots, jnp.zeros((LANES - EXPERTS, SEQUENCE), F32)], axis=0).T
    gates = gates_ref[...]
    logit_grads = (gates * (dots - jnp.sum(gates * dots, axis=1, keepdims=True))).astype(BF16)
    small = small_ref[...]
    upstream = upstream + dot_f32(logit_grads, small, CONTRACT_LAST)
    middle = middle_ref[...]
    inverse = inverse_rms(middle)
    unit = middle * inverse
    gain = small.astype(F32).T[GAIN_FFN : GAIN_FFN + 1, :]
    gain_grad = jnp.sum(upstream * unit, axis=0, keepdims=True)
    scaled = upstream * gain
    middle_grad = grad_ref[...].astype(F32) + inverse * (
        scaled - unit * jnp.mean(scaled * unit, axis=1, keepdims=True)
    )
    middle_grad_ref[...] = middle_grad
    attn_grad = (resid_scale * middle_grad).astype(BF16)
    line = lax.broadcasted_iota(jnp.int32, (LANES, 1024), 0)
    side_ref[...] = dot_f32(normed2_ref[0:256, :], logit_grads, CONTRACT_FIRST) + jnp.where(
        line == GAIN_FFN, gain_grad, 0.0
    ).T
    for part, w_ref, out_ref in ((0, w_own_ref, own_ref), (1, w_far_ref, far_ref)):
        features = jnp.concatenate([mixed_ref[:, group_of(e, 2 * q + part)] for q in range(4)], axis=1)
        out_ref[:, :1024] = dot_f32(features, attn_grad, CONTRACT_FIRST).astype(BF16)
        back = dot_f32(attn_grad, w_ref[...], CONTRACT_LAST).astype(BF16)
        for q in range(4):
            mixed_grad_ref[:, group_of(e, 2 * q + part)] = back[:, LANES * q : LANES * (q + 1)]
            at = slice(LANES * q, LANES * (q + 1))
            out_ref[at, 1024:] = side_ref[group_of(e, 2 * q + part), :].astype(BF16)


def attend_back_body(e_ref, x_ref, column_ref, row_ref, cos_ref, sin_ref, q_ref, k_ref, v_ref, grad_ref,
                     normed_ref, w_own_ref, w_far_ref, middle_grad_ref,
                     own_ref, far_ref, embed_ref, raw_ref, scaled_ref):
    e = e_ref[0]
    allowed = allowed_of(column_ref, row_ref)
    unrotate = lambda u: (
        u * wide_table(cos_ref[...], u.shape[1]) - turn_halves(u) * wide_table(sin_ref[...], u.shape[1])
    ).astype(BF16)

    def pair(step, _):
        wide = pl.ds(pl.multiple_of(step * 256, 256), 256)
        narrow = lambda base: pl.ds(pl.multiple_of(base + step * LANES, LANES), LANES)
        q_block, d_block = q_ref[:, wide], grad_ref[:, wide]
        k_block, v_block = k_ref[:, narrow(0)], v_ref[:, narrow(0)]
        q_outs, k_outs, v_outs = [], [], []
        for i in range(2):
            queries, keys = heads_of(q_block, 2 * i, 2), heads_of(k_block, i, 1)
            upstream = heads_of(d_block, 2 * i, 2)
            probs = attention_probs(queries, keys, allowed)
            prob_grads = dot_f32(upstream, heads_of(v_block, i, 1), CONTRACT_LAST)
            centre = jnp.sum(probs * prob_grads, axis=1, keepdims=True)
            score_grads = (probs * (prob_grads - centre)).astype(BF16)
            rows = dot_f32(score_grads, keys, CONTRACT_PLAIN) * attn_scale
            q_outs += [rows[:SEQUENCE], rows[SEQUENCE:]]
            k_outs.append(dot_f32(score_grads, queries, CONTRACT_FIRST) * attn_scale)
            v_outs.append(dot_f32(probs.astype(BF16), upstream, CONTRACT_FIRST))
        raw_ref[:, wide] = unrotate(jnp.concatenate(q_outs, axis=1))
        raw_ref[:, narrow(1024)] = unrotate(jnp.concatenate(k_outs, axis=1))
        raw_ref[:, narrow(1536)] = jnp.concatenate(v_outs, axis=1).astype(BF16)
        return 0

    lax.fori_loop(0, 4, pair, 0)
    resid = embed_scale * x_ref[...].astype(F32)
    inverse = inverse_rms(resid)
    for part, w_ref, out_ref in ((0, w_own_ref, own_ref), (1, w_far_ref, far_ref)):
        for c in range(4):
            at = slice(512 * c, 512 * c + 512)
            out_ref[:, at] = dot_f32(
                normed_ref[:, 512 * part : 512 * part + 512], raw_ref[:, at], CONTRACT_FIRST
            ).astype(BF16)
        back = dot_f32(raw_ref[...], w_ref[:, :2048], CONTRACT_LAST)
        gain = w_ref[:, 2048:].astype(F32).T[GAIN_ATTN : GAIN_ATTN + 1, :]
        gain_grads = []
        for q in range(4):
            at = slice(LANES * q, LANES * (q + 1))
            group = group_of(e, 2 * q + part)
            unit = embed_scale * x_ref[:, group].astype(F32) * inverse
            gain_grads.append(jnp.sum(back[:, at] * unit, axis=0, keepdims=True))
            scaled_ref[:, group] = back[:, at] * gain[:, at]
        line = lax.broadcasted_iota(jnp.int32, (LANES, 512), 0)
        side = jnp.where(line == GAIN_ATTN, jnp.concatenate(gain_grads, axis=1), 0.0).T
        out_ref[:, 2048:] = side.astype(BF16)
    unit = resid * inverse
    scaled = scaled_ref[...]
    resid_grad = middle_grad_ref[...] + inverse * (
        scaled - unit * jnp.mean(scaled * unit, axis=1, keepdims=True)
    )
    embed_ref[...] = (embed_scale * resid_grad).astype(BF16)


def local_kernel(body, name, outs, scratch, flops, number, *operands):
    bytes_moved = sum(a.size * a.dtype.itemsize for a in operands)
    vmem = pl.BlockSpec(memory_space=pltpu.VMEM)
    return pl.pallas_call(
        body,
        out_shape=[jax.ShapeDtypeStruct(shape, dtype) for shape, dtype in outs],
        in_specs=[pl.BlockSpec(memory_space=pltpu.SMEM)] + [vmem] * len(operands),
        out_specs=[vmem] * len(outs),
        scratch_shapes=[pltpu.VMEM(shape, dtype) for shape, dtype in scratch],
        compiler_params=pltpu.CompilerParams(vmem_limit_bytes=56 * 1024 * 1024),
        cost_estimate=pl.CostEstimate(flops=flops, bytes_accessed=bytes_moved, transcendentals=0),
        name=name,
    )(number, *operands)


def together(*values):
    return lax.optimization_barrier(values)


def plane_gather(value):
    return jnp.concatenate([value] + [over_expert(value, bits) for bits in (2, 4, 6)])


def plane_sum(total):
    rows = total.shape[0] // 4
    part = total[:rows].astype(F32)
    for q in (1, 2, 3):
        part = part + over_expert(total[rows * q : rows * q + rows], 2 * q).astype(F32)
    return part.astype(BF16)


def core_sum(own, far):
    return (own.astype(F32) + over_expert(far, 1).astype(F32)).astype(BF16)


def xor_order(pieces, at):
    stacked = jnp.stack(pieces)
    return jnp.concatenate(
        [lax.dynamic_index_in_dim(stacked, at ^ i, 0, keepdims=False) for i in range(len(pieces))]
    )


def shard_sum(plane, z):
    rows = lambda k: lax.dynamic_slice_in_dim(plane, (z ^ k) * 32, 32, 0)
    result = rows(0).astype(F32)
    for k in (1, 2, 3):
        result = result + over_shard(rows(k), k).astype(F32)
    return result


def exchange(slices):
    return lax.all_to_all(slices, "shard", split_axis=0, concat_axis=0, tiled=True)


def expert_slices(expert_in, expert_out, part):
    chosen = [OWN * (d % PAIR) + part for d in range(4)]
    return jnp.stack([jnp.concatenate([expert_in[c], expert_out[c]]) for c in chosen])


def over_x(value):
    return over_expert(value, 2)


def over_y(value):
    return over_expert(value, 4)


def spread(value, first, second):
    near = {first: first(value), second: second(value)}
    return [value, near[over_x], near[over_y], second(near[first])]


def fold(parts, first, second):
    one, two = (1, 2) if first is over_x else (2, 1)
    passing, mine = first(parts[3]), first(parts[one])
    other = (parts[two].astype(F32) + passing.astype(F32)).astype(BF16)
    return parts[0].astype(F32) + mine.astype(F32) + second(other).astype(F32)


def fold_both(parts):
    own, pair = parts[:4], parts[4:]
    pair_pass, own_pass = over_x(pair[3]), over_y(own[3])
    pair_mine = over_x(pair[1])
    pair_other = over_y(bf_sum(pair[2], pair_pass))
    mine, pair_pass = together(own[2], pair_pass)
    own_mine = over_y(mine)
    own_other = over_x(bf_sum(own[1], own_pass))
    pair_sum = bf_sum(pair[0], pair_mine, pair_other)
    return bf_sum(own[0], own_mine, own_other), pair_sum


def bf_sum(*values):
    return sum(value.astype(F32) for value in values).astype(BF16)


def pack_body(query_ref, key_ref, value_ref, router_ref, attn_ref, ffn_ref, out_ref, pack_ref):
    pack_ref[:, 0:1024] = query_ref[...].astype(BF16)
    pack_ref[:, 1024:1536] = key_ref[...].astype(BF16)
    pack_ref[:, 1536:2048] = value_ref[...].astype(BF16)
    zeros = jnp.zeros((32, LANES - EXPERTS - 2), F32)
    small = jnp.concatenate([router_ref[...], attn_ref[...], ffn_ref[...], zeros], axis=1)
    pack_ref[:, 2048:2176] = small.astype(BF16)
    pack_ref[:, 2176:] = out_ref[...].astype(BF16)


def pack_call(*operands):
    return pl.pallas_call(
        pack_body,
        out_shape=jax.ShapeDtypeStruct((32, 3200), BF16),
        in_specs=[pl.BlockSpec(memory_space=pltpu.VMEM)] * len(operands),
        out_specs=pl.BlockSpec(memory_space=pltpu.VMEM),
        name="pack",
    )(*operands)


def per_device_fast(
    embedded,
    document_numbers,
    expert_ids,
    attn_gain,
    ffn_gain,
    w_query,
    key_projection,
    value_projection,
    w_out,
    w_router,
    expert_in,
    expert_out,
    cotangent,
):
    e = lax.axis_index("expert")
    z = lax.axis_index("shard")
    place = e.reshape(1)
    pack = pack_call(
        w_query, key_projection, value_projection, w_router, attn_gain[:, None], ffn_gain[:, None], w_out
    )
    pack, grad_early = together(pack, cotangent)
    plane = xor_order([pack] + [over_shard(pack, k) for k in (1, 2, 3)], z)
    out_pair = over_shard(grad_early, 1)
    out_x, out_y = over_x(grad_early), over_y(grad_early)
    slices = [expert_slices(expert_in, expert_out, part) for part in range(OWN)]
    plane, out_x, out_y, out_pair, slices[0] = together(plane, out_x, out_y, out_pair, slices[0])
    weights0 = exchange(slices[0])
    left = spread(plane[:, :1152], over_x, over_y)
    right = spread(plane[:, 1152:2176], over_y, over_x)
    in_own = jnp.concatenate([jnp.concatenate(left), jnp.concatenate(right)], axis=1)
    in_own, plane, out_x, out_pair = together(in_own, plane, out_x, out_pair)
    in_far = over_expert(in_own, 1)
    out_w_own = plane_gather(plane[:, 2176:])

    segments = document_numbers[0]
    column, row = segments[:, None], segments[None, :]
    cosine, sine = (jnp.concatenate([table] * 4, axis=1) for table in rope_tables(segments))
    lanes = jnp.arange(LANES, dtype=jnp.int32)
    member = jnp.any(expert_ids[:, :, None] == lanes, axis=1)
    index = jnp.arange(SEQUENCE, dtype=jnp.int32)
    below = (index[None, :] < index[:, None]).astype(BF16)
    rank = jnp.dot(below, member.astype(BF16), preferred_element_type=F32)
    code = jnp.where(member, rank, -1.0)

    wide, half = (SEQUENCE, 1024), (SEQUENCE, 512)
    normed, queries, keys, values, mixed = local_kernel(
        attend_body, "attend", [(wide, BF16), (wide, BF16), (half, BF16), (half, BF16), (wide, BF16)], [],
        4_000_000_000, place, embedded, column, row, cosine, sine, in_own, in_far,
    )
    out_w_own, out_pair, out_x, mixed = together(out_w_own, out_pair, out_x, mixed)
    out_w_far = over_expert(out_w_own, 1)
    out_blocks = [cotangent, out_x, out_y, over_y(out_x)] + spread(out_pair, over_y, over_x)
    payload, gates, middle, small_all = local_kernel(
        route_body, "route",
        [((288, 1024), BF16), ((SEQUENCE, LANES), F32), (wide, F32), ((1024, LANES), BF16)], [],
        2_000_000_000, place, embedded, mixed, out_w_own, out_w_far, in_own[:, 2048:], in_far[:, 2048:], code,
    )
    pay_pair = over_shard(payload, 1)
    pay_x, pay_y = over_x(payload), over_y(payload)
    pay_x, pay_y, pay_pair, *out_blocks = together(pay_x, pay_y, pay_pair, *out_blocks)
    tok_pair = [pay_pair, over_x(pay_pair), over_y(pay_pair)]
    tok_own = [payload, pay_x, pay_y, over_y(pay_x)]
    *tok_pair, weights0, slices[1] = together(*tok_pair, weights0, slices[1])
    tok_pair.append(over_x(tok_pair[2]))
    weights1 = exchange(slices[1])
    weights0_far = over_expert(weights0, 1)
    tokens = tok_own + tok_pair
    first = (e * 4 + z % PAIR * OWN).reshape(1)
    first_far = ((e ^ 1) * 4 + z % PAIR * OWN).reshape(1)
    sums, grad_a = expert_call(first, tokens, out_blocks, weights0)
    sums, grad_b = expert_call(first_far, tokens, out_blocks, weights0_far, sums)
    expert_grad0 = core_sum(grad_a, grad_b)
    expert_grad0, weights1 = together(expert_grad0, weights1)
    slices0 = exchange(expert_grad0)
    weights1_far = over_expert(weights1, 1)
    sums, grad_c = expert_call(first + 1, tokens, out_blocks, weights1, sums)
    sums, grad_d = expert_call(first_far + 1, tokens, out_blocks, weights1_far, sums)
    rows, moes = sums[:BLOCKS], sums[BLOCKS:]
    row_own, row_pair = fold_both(rows)
    returned = over_shard(row_pair, 1)
    expert_grad1 = core_sum(grad_c, grad_d)
    row_own, returned, expert_grad1, slices0, *moes = together(row_own, returned, expert_grad1, slices0, *moes)
    slices1 = exchange(expert_grad1)
    moe_pair = fold(moes[4:], over_x, over_y).astype(BF16)
    moe_own = fold(moes[:4], over_y, over_x)
    moe_other = over_shard(moe_pair, 1)
    early_own, early_far, mixed_grad, middle_grad = local_kernel(
        turn_body, "turn", [((512, 1152), BF16), ((512, 1152), BF16), (wide, BF16), (wide, F32)],
        [((1024, LANES), F32)], 4_000_000_000, place, row_own, returned, cotangent, middle, gates,
        small_all, payload, mixed, out_w_own, out_w_far,
    )
    late_own, late_far, grad_embedded = local_kernel(
        attend_back_body, "attend_back", [((512, 2176), BF16), ((512, 2176), BF16), (wide, BF16)],
        [((SEQUENCE, 2048), BF16), (wide, F32)], 8_000_000_000, place, embedded, column, row, cosine, sine,
        queries, keys, values, mixed_grad, normed, in_own, in_far, middle_grad,
    )
    early_plane = plane_sum(core_sum(early_own, early_far))
    late_plane = plane_sum(core_sum(late_own, late_far))
    early = shard_sum(early_plane, z)
    late = shard_sum(late_plane, z)
    slices0, slices1 = slices0.astype(F32), slices1.astype(F32)
    expert_grads = jnp.stack(
        [slices0[0] + slices0[2], slices1[0] + slices1[2], slices0[1] + slices0[3], slices1[1] + slices1[3]]
    )
    grad_expert_in, grad_expert_out = expert_grads[:, :256], expert_grads[:, 256:]
    moe = moe_own + moe_other.astype(F32)
    output = (middle + resid_scale * moe).astype(BF16)
    return (
        output,
        grad_embedded,
        late[:, 2048 + GAIN_ATTN],
        early[:, 1024 + GAIN_FFN],
        late[:, :1024],
        late[:, 1024:1536],
        late[:, 1536:2048],
        early[:, :1024],
        early[:, 1024 : 1024 + EXPERTS],
        grad_expert_in,
        grad_expert_out,
    )


def solution(mesh):
    owners, shards = mesh.shape["expert"], mesh.shape["shard"]
    fast = owners == 8 and shards == 4
    both = ("expert", "shard")
    rows = P(both, None)
    weights = P("expert", "shard", None)
    return jax.shard_map(
        per_device_fast if fast else per_device_general,
        mesh=mesh,
        in_specs=(rows,) * 3 + (P(both),) * 2 + (rows,) * 5 + (weights,) * 2 + (rows,),
        out_specs=(rows,) * 2 + (P(both),) * 2 + (rows,) * 5 + (weights,) * 2,
        check_vma=False,
    )
```

```python
import functools

import jax
import jax.numpy as jnp
from jax import lax
from jax.experimental import pallas as pl
from jax.experimental.pallas import tpu as pltpu
from jax.sharding import PartitionSpec as P

MODEL_WIDTH = 1024
QUERY_HEADS = 16
KEY_VALUE_HEADS = 8
HEAD_SIZE = 64
FF = 512
EXPERTS = 32
TOPK = 8
CAP = 128


embed_scale = 12.0
attn_scale = 0.015625
resid_scale = 0.22
norm_eps = 1e-06
rope_base = 10000.0


def rope_tables(segments):
    sequence_length = segments.shape[0]
    key_index = jnp.arange(sequence_length, dtype=jnp.int32)
    change = jnp.concatenate([jnp.ones((1,), jnp.bool_), segments[1:] != segments[:-1]])
    begins = lax.cummax(jnp.where(change, key_index, 0), axis=0)
    places = (key_index - begins).astype(jnp.float32)
    freqs = rope_base ** (-2.0 * jnp.arange(HEAD_SIZE // 2, dtype=jnp.float32) / HEAD_SIZE)
    angles = places[:, None] * freqs[None, :]
    return (jnp.cos(angles), jnp.sin(angles))


def apply_rotation(value_heads, cosine_table, sine_table):
    halfway = value_heads.shape[-1] // 2
    first_half = value_heads[..., :halfway]
    second_half = value_heads[..., halfway:]
    cos_part = cosine_table[:, None, :]
    sin_part = sine_table[:, None, :]
    return jnp.concatenate(
        [
            first_half * cos_part - second_half * sin_part,
            second_half * cos_part + first_half * sin_part,
        ],
        axis=-1,
    )


def reverse_rotation(grads, cosine_table, sine_table):
    halfway = grads.shape[-1] // 2
    first_half = grads[..., :halfway]
    second_half = grads[..., halfway:]
    cos_part = cosine_table[:, None, :]
    sin_part = sine_table[:, None, :]
    return jnp.concatenate(
        [
            first_half * cos_part + second_half * sin_part,
            second_half * cos_part - first_half * sin_part,
        ],
        axis=-1,
    )


def norm_forward(value_heads):
    inverse = lax.rsqrt(jnp.mean(value_heads * value_heads, axis=1, keepdims=True) + norm_eps)
    return (value_heads * inverse, inverse)


def norm_backward(upstream, unit_values, inverse, gain):
    scaled = upstream * gain
    grad_values = inverse * (
        scaled - unit_values * jnp.mean(scaled * unit_values, axis=1, keepdims=True)
    )
    return (grad_values, jnp.sum(upstream * unit_values, axis=0))


def slot_tables(expert_ids):
    flat_ids = expert_ids.reshape(-1)
    count_all = flat_ids.shape[0]
    matches = (flat_ids[:, None] == jnp.arange(EXPERTS, dtype=jnp.int32)[None, :]).astype(jnp.int32)
    before = jnp.cumsum(matches, axis=0) - 1
    ranking = jnp.sum(before * matches, axis=1)
    target = flat_ids * CAP + ranking
    source = (
        jnp.zeros((EXPERTS * CAP,), jnp.int32)
        .at[target]
        .set(jnp.arange(count_all, dtype=jnp.int32))
    )
    filled = (
        jnp.zeros((EXPERTS * CAP,), jnp.int32).at[target].set(jnp.ones((count_all,), jnp.int32))
    )
    return (target, source, filled)


def silu_parts(gate_up):
    gate_part = gate_up[..., :FF]
    up_part = gate_up[..., FF:]
    sigmoid_gate = jax.nn.sigmoid(gate_part)
    hidden = (gate_part * sigmoid_gate * up_part).astype(jnp.bfloat16)
    return (gate_part, up_part, sigmoid_gate, hidden)


def per_device_general(
    embedded,
    document_numbers,
    expert_ids,
    attn_gain,
    ffn_gain,
    w_query,
    key_projection,
    value_projection,
    w_out,
    w_router,
    expert_in,
    expert_out,
    cotangent,
):
    mixer = (
        lax.all_gather(attn_gain.astype(jnp.bfloat16), ("expert", "shard"), axis=0, tiled=True),
        lax.all_gather(ffn_gain.astype(jnp.bfloat16), ("expert", "shard"), axis=0, tiled=True),
        lax.all_gather(w_query.astype(jnp.bfloat16), ("expert", "shard"), axis=0, tiled=True),
        lax.all_gather(
            key_projection.astype(jnp.bfloat16), ("expert", "shard"), axis=0, tiled=True
        ),
        lax.all_gather(
            value_projection.astype(jnp.bfloat16), ("expert", "shard"), axis=0, tiled=True
        ),
        lax.all_gather(w_out.astype(jnp.bfloat16), ("expert", "shard"), axis=0, tiled=True),
        lax.all_gather(w_router.astype(jnp.bfloat16), ("expert", "shard"), axis=0, tiled=True),
    )
    gain_attn, gain_ffn, query_w, key_w, value_w, out_w, router_w = mixer
    full_in, full_out = (
        lax.all_gather(expert_in, "shard", axis=1, tiled=True),
        lax.all_gather(expert_out, "shard", axis=1, tiled=True),
    )
    sequence_length = embedded.shape[0]
    query_groups = QUERY_HEADS // KEY_VALUE_HEADS
    owners = lax.axis_size("expert")
    local_count = EXPERTS // owners
    received = owners * CAP
    resid = embed_scale * embedded.astype(jnp.float32)
    unit_attn, inverse_attn = norm_forward(resid)
    normed = (unit_attn * gain_attn.astype(jnp.float32)).astype(jnp.bfloat16)
    unrotated_query = jnp.dot(normed, query_w, preferred_element_type=jnp.float32)
    unrotated_key = jnp.dot(normed, key_w, preferred_element_type=jnp.float32)
    projected_value = jnp.dot(normed, value_w, preferred_element_type=jnp.float32)
    segments = document_numbers[0]
    cosine_table, sine_table = rope_tables(segments)
    query_heads = (
        apply_rotation(
            unrotated_query.reshape(sequence_length, QUERY_HEADS, HEAD_SIZE),
            cosine_table,
            sine_table,
        )
        .astype(jnp.bfloat16)
        .reshape(sequence_length, KEY_VALUE_HEADS, query_groups, HEAD_SIZE)
    )
    key_heads = apply_rotation(
        unrotated_key.reshape(sequence_length, KEY_VALUE_HEADS, HEAD_SIZE), cosine_table, sine_table
    ).astype(jnp.bfloat16)
    value_heads = projected_value.astype(jnp.bfloat16).reshape(
        sequence_length, KEY_VALUE_HEADS, HEAD_SIZE
    )
    block_rows = min(512, sequence_length)
    starts = jnp.arange(sequence_length // block_rows, dtype=jnp.int32) * block_rows
    key_index = jnp.arange(sequence_length, dtype=jnp.int32)

    def block_scores(first_row):
        row_index = first_row + jnp.arange(block_rows, dtype=jnp.int32)
        raw_scores = (
            jnp.einsum("qhgd,khd->hgqk", query_heads, key_heads, preferred_element_type=jnp.float32)
            * attn_scale
        )
        allowed = (key_index[None, :] <= row_index[:, None]) & (
            segments[None, :] == segments[:, None]
        )
        return (jnp.where(allowed, raw_scores, -1e30), query_heads)

    def attend_block(first_row):
        scores, query_rows = block_scores(first_row)
        row_max = jnp.max(scores, axis=-1, keepdims=True)
        exps = jnp.exp(scores - row_max)
        totals = jnp.sum(exps, axis=-1, keepdims=True)
        weights = (exps / totals).astype(jnp.bfloat16)
        mixed_rows = jnp.einsum(
            "hgqk,khd->qhgd", weights, value_heads, preferred_element_type=jnp.float32
        )
        return (mixed_rows.astype(jnp.bfloat16), (row_max + jnp.log(totals))[..., 0])

    mixed_blocks, log_totals = lax.map(attend_block, starts)
    mixed_heads_output = mixed_blocks.reshape(sequence_length, QUERY_HEADS * HEAD_SIZE)
    middle = resid + resid_scale * jnp.dot(
        mixed_heads_output, out_w, preferred_element_type=jnp.float32
    )
    unit_ffn, inverse_ffn = norm_forward(middle)
    normed2 = (unit_ffn * gain_ffn.astype(jnp.float32)).astype(jnp.bfloat16)
    logits = jnp.dot(normed2, router_w, preferred_element_type=jnp.float32)
    pick_table = expert_ids[:, :, None] == jnp.arange(EXPERTS, dtype=jnp.int32)[None, None, :]
    chosen = jnp.sum(jnp.where(pick_table, logits[:, None, :], 0.0), axis=2)
    exps_chosen = jnp.exp(chosen - jnp.max(chosen, axis=1, keepdims=True))
    gates = exps_chosen / jnp.sum(exps_chosen, axis=1, keepdims=True)
    target, source, filled = slot_tables(expert_ids)
    live_slots = filled[:, None] == 1
    zero_bf = jnp.zeros((), jnp.bfloat16)
    send_rows = jnp.where(live_slots, normed2[source // TOPK], zero_bf).reshape(
        owners, local_count, CAP, MODEL_WIDTH
    )
    arrived = lax.all_to_all(send_rows, "expert", split_axis=0, concat_axis=2, tiled=True).reshape(
        local_count, received, MODEL_WIDTH
    )
    gate_up = jnp.einsum("erd,edf->erf", arrived, full_in, preferred_element_type=jnp.float32)
    gate_part, up_part, sigmoid_gate, hidden = silu_parts(gate_up)
    produced = jnp.einsum(
        "erf,efd->erd", hidden, full_out, preferred_element_type=jnp.float32
    ).astype(jnp.bfloat16)
    returned = lax.all_to_all(
        produced.reshape(1, local_count, received, MODEL_WIDTH),
        "expert",
        split_axis=2,
        concat_axis=0,
        tiled=True,
    ).reshape(EXPERTS * CAP, MODEL_WIDTH)
    slot_values = returned[target].reshape(sequence_length, TOPK, MODEL_WIDTH)
    moe = jnp.einsum("tk,tkd->td", gates, slot_values.astype(jnp.float32))
    output = (middle + resid_scale * moe).astype(jnp.bfloat16)
    grad_output = cotangent.astype(jnp.float32)
    grad_mix = resid_scale * grad_output
    gate_grads = jnp.einsum("tkd,td->tk", slot_values.astype(jnp.float32), grad_mix)
    slot_grads = (
        (gates[:, :, None] * grad_mix[:, None, :])
        .astype(jnp.bfloat16)
        .reshape(sequence_length * TOPK, MODEL_WIDTH)
    )
    grad_send = jnp.where(live_slots, slot_grads[source], zero_bf).reshape(
        owners, local_count, CAP, MODEL_WIDTH
    )
    grad_arrived = lax.all_to_all(
        grad_send, "expert", split_axis=0, concat_axis=2, tiled=True
    ).reshape(local_count, received, MODEL_WIDTH)
    owner_rows = lax.all_to_all(
        send_rows, "expert", split_axis=0, concat_axis=2, tiled=True
    ).reshape(local_count, received, MODEL_WIDTH)
    owner_gate_up = jnp.einsum(
        "erd,edf->erf", owner_rows, full_in, preferred_element_type=jnp.float32
    )
    owner_gate, owner_up, owner_sigmoid, owner_hidden = silu_parts(owner_gate_up)
    hidden_grad = jnp.einsum(
        "erd,efd->erf", grad_arrived, full_out, preferred_element_type=jnp.float32
    )
    gate_grad_part = (
        hidden_grad * owner_up * owner_sigmoid * (1.0 + owner_gate * (1.0 - owner_sigmoid))
    )
    up_grad_part = hidden_grad * owner_gate * owner_sigmoid
    gate_up_grad = jnp.concatenate([gate_grad_part, up_grad_part], axis=-1).astype(jnp.bfloat16)
    grad_full_out = jnp.einsum(
        "erf,erd->efd", owner_hidden, grad_arrived, preferred_element_type=jnp.float32
    )
    grad_full_in = jnp.einsum(
        "erd,erf->edf", owner_rows, gate_up_grad, preferred_element_type=jnp.float32
    )
    row_grads = jnp.einsum(
        "erf,edf->erd", gate_up_grad, full_in, preferred_element_type=jnp.float32
    ).astype(jnp.bfloat16)
    grad_returned = lax.all_to_all(
        row_grads.reshape(1, local_count, received, MODEL_WIDTH),
        "expert",
        split_axis=2,
        concat_axis=0,
        tiled=True,
    ).reshape(EXPERTS * CAP, MODEL_WIDTH)
    grad_expert_in, grad_expert_out = (
        lax.psum_scatter(
            grad_full_in.astype(jnp.bfloat16), "shard", scatter_dimension=1, tiled=True
        ).astype(jnp.float32),
        lax.psum_scatter(
            grad_full_out.astype(jnp.bfloat16), "shard", scatter_dimension=1, tiled=True
        ).astype(jnp.float32),
    )
    mixer_back = (
        lax.all_gather(attn_gain.astype(jnp.bfloat16), ("expert", "shard"), axis=0, tiled=True),
        lax.all_gather(ffn_gain.astype(jnp.bfloat16), ("expert", "shard"), axis=0, tiled=True),
        lax.all_gather(w_query.astype(jnp.bfloat16), ("expert", "shard"), axis=0, tiled=True),
        lax.all_gather(
            key_projection.astype(jnp.bfloat16), ("expert", "shard"), axis=0, tiled=True
        ),
        lax.all_gather(
            value_projection.astype(jnp.bfloat16), ("expert", "shard"), axis=0, tiled=True
        ),
        lax.all_gather(w_out.astype(jnp.bfloat16), ("expert", "shard"), axis=0, tiled=True),
        lax.all_gather(w_router.astype(jnp.bfloat16), ("expert", "shard"), axis=0, tiled=True),
    )
    back_gain_attn, back_gain_ffn, back_query, back_key, back_value, back_out, back_router = (
        mixer_back
    )
    chosen_grad = gates * (gate_grads - jnp.sum(gates * gate_grads, axis=1, keepdims=True))
    logit_grads = jnp.sum(jnp.where(pick_table, chosen_grad[:, :, None], 0.0), axis=1).astype(
        jnp.bfloat16
    )
    grad_router_full = jnp.einsum(
        "td,te->de", normed2, logit_grads, preferred_element_type=jnp.float32
    )
    normed2_grad = jnp.sum(
        grad_returned[target].reshape(sequence_length, TOPK, MODEL_WIDTH), axis=1, dtype=jnp.float32
    )
    normed2_grad = normed2_grad + jnp.einsum(
        "te,de->td", logit_grads, back_router, preferred_element_type=jnp.float32
    )
    middle_norm_grad, grad_gain_ffn = norm_backward(
        normed2_grad, unit_ffn, inverse_ffn, back_gain_ffn.astype(jnp.float32)
    )
    middle_grad = grad_output + middle_norm_grad
    attn_grad = (resid_scale * middle_grad).astype(jnp.bfloat16)
    grad_out_full = jnp.einsum(
        "tf,td->fd", mixed_heads_output, attn_grad, preferred_element_type=jnp.float32
    )
    mixed_output_gradient = jnp.einsum(
        "td,fd->tf", attn_grad, back_out, preferred_element_type=jnp.float32
    ).astype(jnp.bfloat16)
    mixed_gradient_by_head = mixed_output_gradient.reshape(
        sequence_length, KEY_VALUE_HEADS, query_groups, HEAD_SIZE
    )

    def attend_back(carries, packed):
        key_acc, value_acc = carries
        first_row, log_rows = packed
        scores, query_rows = block_scores(first_row)
        probs = jnp.exp(scores - log_rows[..., None])
        prob_grads = jnp.einsum(
            "qhgd,khd->hgqk",
            mixed_gradient_by_head,
            value_heads,
            preferred_element_type=jnp.float32,
        )
        score_grads = (
            probs * (prob_grads - jnp.sum(probs * prob_grads, axis=-1, keepdims=True))
        ).astype(jnp.bfloat16)
        query_grads = (
            jnp.einsum("hgqk,khd->qhgd", score_grads, key_heads, preferred_element_type=jnp.float32)
            * attn_scale
        )
        key_acc = (
            key_acc
            + jnp.einsum(
                "hgqk,qhgd->khd", score_grads, query_rows, preferred_element_type=jnp.float32
            )
            * attn_scale
        )
        value_acc = value_acc + jnp.einsum(
            "hgqk,qhgd->khd",
            probs.astype(jnp.bfloat16),
            mixed_gradient_by_head,
            preferred_element_type=jnp.float32,
        )
        return ((key_acc, value_acc), query_grads)

    empty_head_rows = jnp.zeros((sequence_length, KEY_VALUE_HEADS, HEAD_SIZE), jnp.float32)
    (summed_key_gradient, summed_value_gradient), query_grad_blocks = lax.scan(
        attend_back, (empty_head_rows, empty_head_rows), (starts, log_totals)
    )
    query_raw_grad = (
        reverse_rotation(
            query_grad_blocks.reshape(sequence_length, QUERY_HEADS, HEAD_SIZE),
            cosine_table,
            sine_table,
        )
        .astype(jnp.bfloat16)
        .reshape(sequence_length, QUERY_HEADS * HEAD_SIZE)
    )
    key_raw_grad = (
        reverse_rotation(summed_key_gradient, cosine_table, sine_table)
        .astype(jnp.bfloat16)
        .reshape(sequence_length, KEY_VALUE_HEADS * HEAD_SIZE)
    )
    projected_value_gradient = summed_value_gradient.astype(jnp.bfloat16).reshape(
        sequence_length, KEY_VALUE_HEADS * HEAD_SIZE
    )
    grad_query_full = jnp.einsum(
        "td,tf->df", normed, query_raw_grad, preferred_element_type=jnp.float32
    )
    grad_key_full = jnp.einsum(
        "td,tf->df", normed, key_raw_grad, preferred_element_type=jnp.float32
    )
    grad_value_full = jnp.einsum(
        "td,tf->df", normed, projected_value_gradient, preferred_element_type=jnp.float32
    )
    normed_grad = jnp.einsum(
        "tf,df->td", query_raw_grad, back_query, preferred_element_type=jnp.float32
    )
    normed_grad = normed_grad + jnp.einsum(
        "tf,df->td", key_raw_grad, back_key, preferred_element_type=jnp.float32
    )
    normed_grad = normed_grad + jnp.einsum(
        "tf,df->td", projected_value_gradient, back_value, preferred_element_type=jnp.float32
    )
    resid_norm_grad, grad_gain_attn = norm_backward(
        normed_grad, unit_attn, inverse_attn, back_gain_attn.astype(jnp.float32)
    )
    resid_grad = middle_grad + resid_norm_grad
    grad_embedded = (embed_scale * resid_grad).astype(jnp.bfloat16)
    summed = (
        lax.psum_scatter(grad_gain_attn, ("expert", "shard"), scatter_dimension=0, tiled=True),
        lax.psum_scatter(grad_gain_ffn, ("expert", "shard"), scatter_dimension=0, tiled=True),
        lax.psum_scatter(grad_query_full, ("expert", "shard"), scatter_dimension=0, tiled=True),
        lax.psum_scatter(grad_key_full, ("expert", "shard"), scatter_dimension=0, tiled=True),
        lax.psum_scatter(grad_value_full, ("expert", "shard"), scatter_dimension=0, tiled=True),
        lax.psum_scatter(grad_out_full, ("expert", "shard"), scatter_dimension=0, tiled=True),
        lax.psum_scatter(grad_router_full, ("expert", "shard"), scatter_dimension=0, tiled=True),
    )
    return (
        output,
        grad_embedded,
        summed[0],
        summed[1],
        summed[2],
        summed[3],
        summed[4],
        summed[5],
        summed[6],
        grad_expert_in,
        grad_expert_out,
    )


BF16 = jnp.bfloat16
F32 = jnp.float32
PAIR = 2
OWN = 2


def over_expert(value, bits):
    return lax.ppermute(value, "expert", [(i, i ^ bits) for i in range(8)])


def over_shard(value, bits):
    return lax.ppermute(value, "shard", [(i, i ^ bits) for i in range(4)])


def dot_f32(left, right, dims):
    return lax.dot_general(left, right, dims, preferred_element_type=F32)


CONTRACT_LAST = (((1,), (1,)), ((), ()))
CONTRACT_FIRST = (((0,), (0,)), ((), ()))
CONTRACT_PLAIN = (((1,), (0,)), ((), ()))
BLOCKS = 8
HALF = 4
ROWS = HALF * CAP
PAY_ROWS = 288
SUM_ROWS = 272


def expert_body(first_part, packed, number_ref, *refs):
    refs = list(refs)
    take = lambda count: [refs.pop(0) for _ in range(count)]
    tok_refs, out_refs = take(BLOCKS), take(BLOCKS)
    if packed:
        (w_ref,) = take(1)
        w_in_ref, w_out_ref = w_ref.at[:, 0:256, :], w_ref.at[:, 256:384, :]
    else:
        w_in_ref, w_out_ref = take(2)
    row_before, moe_before = ([], []) if first_part else (take(BLOCKS), take(BLOCKS))
    row_outs, moe_outs = take(BLOCKS), take(BLOCKS)
    (grad_ref,) = take(1)
    (tok_s, out_s, w_in_s, w_out_s, row_s, moe_s, grad_s, x_s, g_s, gate_s, table_s, back_s, mix_s, dot_s,
     in_acc, out_acc, tok_sem, out_sem, w_sem, row_sem, moe_sem, row_out_sem, moe_out_sem, grad_sem) = refs
    number = number_ref[0]
    copy = pltpu.make_async_copy
    for j in range(BLOCKS):
        copy(tok_refs[j], tok_s.at[j], tok_sem.at[j]).start()
        copy(out_refs[j], out_s.at[j], out_sem.at[j]).start()
        if j == HALF - 1:
            copy(w_in_ref, w_in_s, w_sem.at[0]).start()
            copy(w_out_ref, w_out_s, w_sem.at[1]).start()
    if not first_part:
        for j in range(BLOCKS):
            copy(row_before[j], row_s.at[j], row_sem.at[j]).start()
            copy(moe_before[j], moe_s.at[j], moe_sem.at[j]).start()

    def mask_of(i):
        slot = lax.broadcasted_iota(jnp.int32, (CAP, 256), 0).astype(F32)
        return slot == table_s[i, 0:1, :]

    def half_step(half, _):
        for i in range(HALF):
            j = half * HALF + i
            copy(tok_s.at[j], tok_s.at[j], tok_sem.at[j]).wait()
            copy(out_s.at[j], out_s.at[j], out_sem.at[j]).wait()
            aux = tok_s[j, 256:PAY_ROWS, :].astype(F32)
            line = lax.broadcasted_iota(jnp.int32, (EXPERTS, 1024), 0)
            line = jnp.sum(jnp.where(line == number, aux, 0.0), axis=0, keepdims=True)
            table_s[i, 0:1, :] = line[:, :256]
            gate = line[:, 256:512] + line[:, 512:768] + line[:, 768:]
            mask = mask_of(i)
            pick = jnp.where(mask, 1.0, 0.0).astype(BF16)
            at = slice(i * CAP, (i + 1) * CAP)
            x_s[at, :] = dot_f32(pick, tok_s[j, 0:256, :], CONTRACT_PLAIN).astype(BF16)
            g_s[at, :] = resid_scale * dot_f32(pick, out_s[j], CONTRACT_PLAIN)
            gate_s[at, :] = jnp.sum(jnp.where(mask, gate, 0.0), axis=1, keepdims=True)

        @pl.when(half == 0)
        def _():
            copy(w_in_ref, w_in_s, w_sem.at[0]).wait()
            copy(w_out_ref, w_out_s, w_sem.at[1]).wait()

        w_in = w_in_s[...].reshape(1024, 1024)
        w_out = w_out_s[...].reshape(512, 1024)
        x = x_s[...]
        gate_up = dot_f32(x, w_in, CONTRACT_PLAIN)
        gate_part, up_part = gate_up[:, :FF], gate_up[:, FF:]
        sigmoid = jax.nn.sigmoid(gate_part)
        hidden = (gate_part * sigmoid * up_part).astype(BF16)
        produced = dot_f32(hidden, w_out, CONTRACT_PLAIN).astype(BF16).astype(F32)
        slot_gate = gate_s[...]
        scaled = g_s[...]
        slot_grad = (slot_gate * scaled).astype(BF16)
        dot_s[...] = jnp.sum(produced * scaled, axis=1, keepdims=True)
        mix_s[...] = (slot_gate * produced).astype(BF16)
        hidden_grad = dot_f32(slot_grad, w_out, CONTRACT_LAST)
        gate_grad = hidden_grad * up_part * sigmoid * (1.0 + gate_part * (1.0 - sigmoid))
        up_grad = hidden_grad * gate_part * sigmoid
        gate_up_grad = jnp.concatenate([gate_grad.astype(BF16), up_grad.astype(BF16)], axis=1)
        back_s[...] = dot_f32(gate_up_grad, w_in, CONTRACT_LAST).astype(BF16)
        in_part = dot_f32(x, gate_up_grad, CONTRACT_FIRST)
        out_part = dot_f32(hidden, slot_grad, CONTRACT_FIRST)

        @pl.when(half == 0)
        def _():
            in_acc[...] = in_part
            out_acc[...] = out_part

        @pl.when(half == 1)
        def _():
            for d in range(4):
                wide, narrow = slice(d * 256, (d + 1) * 256), slice(d * 128, (d + 1) * 128)
                grad_s[d, 0:256, :] = (in_acc[wide, :] + in_part[wide, :]).astype(BF16)
                grad_s[d, 256:384, :] = (out_acc[narrow, :] + out_part[narrow, :]).astype(BF16)
            copy(grad_s, grad_ref, grad_sem.at[0]).start()

        for i in range(HALF):
            j = half * HALF + i
            at = slice(i * CAP, (i + 1) * CAP)
            mask = mask_of(i)
            pick = jnp.where(mask, 1.0, 0.0).astype(BF16)
            rows = dot_f32(pick, back_s[at, :], CONTRACT_FIRST)
            mixed = dot_f32(pick, mix_s[at, :], CONTRACT_FIRST)
            dots = jnp.sum(jnp.where(mask, dot_s[at, :], 0.0), axis=0, keepdims=True)
            high = dots.astype(BF16).astype(F32)
            low = dots - high
            wide = jnp.concatenate([high, high, low, low], axis=1)
            line = lax.broadcasted_iota(jnp.int32, (16, 1024), 0)
            lane = lax.broadcasted_iota(jnp.int32, (16, 1024), 1) // 256
            here = (line == number % 16) & (lane % 2 == number // 16)
            side = jnp.where(here, jnp.broadcast_to(wide, (16, 1024)), 0.0)
            if not first_part:
                copy(row_s.at[j], row_s.at[j], row_sem.at[j]).wait()
                copy(moe_s.at[j], moe_s.at[j], moe_sem.at[j]).wait()
                rows = rows + row_s[j, 0:256, :].astype(F32)
                mixed = mixed + moe_s[j].astype(F32)
                side = side + row_s[j, 256:SUM_ROWS, :].astype(F32)
            row_s[j, 0:256, :] = rows.astype(BF16)
            row_s[j, 256:SUM_ROWS, :] = side.astype(BF16)
            moe_s[j] = mixed.astype(BF16)
            for part in range(2):

                @pl.when(half == part)
                def _():
                    k = part * HALF + i
                    copy(row_s.at[k], row_outs[k], row_out_sem.at[k]).start()
                    copy(moe_s.at[k], moe_outs[k], moe_out_sem.at[k]).start()

        return 0

    lax.fori_loop(0, 2, half_step, 0)
    copy(grad_s, grad_ref, grad_sem.at[0]).wait()
    for j in range(BLOCKS):
        copy(row_s.at[j], row_outs[j], row_out_sem.at[j]).wait()
        copy(moe_s.at[j], moe_outs[j], moe_out_sem.at[j]).wait()


def expert_call(number, tokens, grads, weights, before=None):
    operands = list(tokens) + list(grads) + list(weights) + ([] if before is None else list(before))
    block = lambda rows: jax.ShapeDtypeStruct((rows, 1024), BF16)
    outs = [block(SUM_ROWS)] * BLOCKS + [block(256)] * BLOCKS + [jax.ShapeDtypeStruct((4, 384, 1024), BF16)]
    anywhere = pl.BlockSpec(memory_space=pl.ANY)
    blocks = lambda rows: pltpu.VMEM((BLOCKS, rows, 1024), BF16)
    column, wide = pltpu.VMEM((ROWS, 1), F32), pltpu.VMEM((ROWS, 1024), BF16)
    sems = [pltpu.SemaphoreType.DMA((count,)) for count in (8, 8, 2, 8, 8, 8, 8, 1)]
    results = pl.pallas_call(
        functools.partial(expert_body, before is None, len(weights) == 1),
        out_shape=outs,
        in_specs=[pl.BlockSpec(memory_space=pltpu.SMEM)] + [anywhere] * len(operands),
        out_specs=[anywhere] * len(outs),
        scratch_shapes=[
            blocks(PAY_ROWS), blocks(256), pltpu.VMEM((4, 256, 1024), BF16), pltpu.VMEM((4, 128, 1024), BF16),
            blocks(SUM_ROWS), blocks(256),
            pltpu.VMEM((4, 384, 1024), BF16), wide, pltpu.VMEM((ROWS, 1024), F32), column,
            pltpu.VMEM((HALF, 8, 256), F32), wide, wide, column,
            pltpu.VMEM((1024, 1024), F32), pltpu.VMEM((512, 1024), F32),
        ] + sems,
        compiler_params=pltpu.CompilerParams(vmem_limit_bytes=60 * 1024 * 1024),
        cost_estimate=pl.CostEstimate(
            flops=1000, bytes_accessed=1000, transcendentals=0
        ),
        name="expert",
    )(number, *operands)
    return results[: 2 * BLOCKS], results[2 * BLOCKS]


LANES = 128
GAIN_ATTN = 32
GAIN_FFN = 33
SEQUENCE = 256


def group_of(e, r):
    return pl.ds(pl.multiple_of((e ^ r) * LANES, LANES), LANES)


def turn_halves(value):
    lane = lax.broadcasted_iota(jnp.int32, value.shape, 1) % HEAD_SIZE
    width = value.shape[1]
    return jnp.where(
        lane < HEAD_SIZE // 2,
        -pltpu.roll(value, width - HEAD_SIZE // 2, 1),
        pltpu.roll(value, HEAD_SIZE // 2, 1),
    )


def wide_table(table, width):
    return jnp.concatenate([table] * (width // LANES), axis=1)


def inverse_rms(value):
    return lax.rsqrt(jnp.mean(value * value, axis=1, keepdims=True) + norm_eps)


def attention_probs(queries, keys, allowed):
    scores = jnp.where(allowed, dot_f32(queries, keys, CONTRACT_LAST) * attn_scale, -1e30)
    exps = jnp.exp(scores - jnp.max(scores, axis=1, keepdims=True))
    return exps / jnp.sum(exps, axis=1, keepdims=True)


def allowed_of(column_ref, row_ref):
    shape = (2 * SEQUENCE, SEQUENCE)
    query = lax.broadcasted_iota(jnp.int32, shape, 0) % SEQUENCE
    key = lax.broadcasted_iota(jnp.int32, shape, 1)
    column = column_ref[...]
    same = jnp.concatenate([column, column], axis=0) == row_ref[...]
    return (key <= query) & same


def heads_of(block, first, count):
    return jnp.concatenate(
        [block[:, HEAD_SIZE * (first + i) : HEAD_SIZE * (first + i + 1)] for i in range(count)], axis=0
    )


def stacked(refs, a, b):
    return jnp.concatenate([ref[:, a:b] for ref in refs], axis=0)


def gain_row(refs, index):
    return stacked(refs, 1024, 1152).astype(F32).T[index : index + 1, :]


def attend_body(e_ref, x_ref, column_ref, row_ref, cos_ref, sin_ref, *refs):
    lefts, rights = (refs[0:4], refs[4:8]), (refs[8:12], refs[12:16])
    normed_ref, q_ref, k_ref, v_ref, mixed_ref, small_ref = refs[16:]
    e = e_ref[0]
    resid = embed_scale * x_ref[...].astype(F32)
    inverse = inverse_rms(resid)
    for part in range(2):
        gain = gain_row(lefts[part], GAIN_ATTN)
        for q in range(4):
            group = group_of(e, 2 * q + part)
            block = embed_scale * x_ref[:, group].astype(F32)
            scaled = block * inverse * gain[:, LANES * q : LANES * (q + 1)]
            at = 512 * part + LANES * q
            normed_ref[:, at : at + LANES] = scaled.astype(BF16)
            small_ref[group, :] = lefts[part][q][:, 1024:1152]
    own = normed_ref[:, :512]
    far = normed_ref[:, 512:]
    project = lambda sides, a, b: dot_f32(own, stacked(sides[0], a, b), CONTRACT_PLAIN) + dot_f32(
        far, stacked(sides[1], a, b), CONTRACT_PLAIN
    )
    rotate = lambda u: u * wide_table(cos_ref[...], u.shape[1]) + turn_halves(u) * wide_table(
        sin_ref[...], u.shape[1]
    )
    q_ref[...] = rotate(project(lefts, 0, 1024)).astype(BF16)
    k_ref[...] = rotate(project(rights, 0, 512)).astype(BF16)
    v_ref[...] = project(rights, 512, 1024).astype(BF16)
    allowed = allowed_of(column_ref, row_ref)

    def pair(step, _):
        wide = pl.ds(pl.multiple_of(step * 256, 256), 256)
        narrow = pl.ds(pl.multiple_of(step * LANES, LANES), LANES)
        q_block, k_block, v_block = q_ref[:, wide], k_ref[:, narrow], v_ref[:, narrow]
        outs = []
        for i in range(2):
            probs = attention_probs(heads_of(q_block, 2 * i, 2), heads_of(k_block, i, 1), allowed)
            rows = dot_f32(probs.astype(BF16), heads_of(v_block, i, 1), CONTRACT_PLAIN)
            outs += [rows[:SEQUENCE], rows[SEQUENCE:]]
        mixed_ref[:, wide] = jnp.concatenate(outs, axis=1).astype(BF16)
        return 0

    lax.fori_loop(0, 4, pair, 0)


def route_body(e_ref, x_ref, mixed_ref, small_ref, code_ref, *refs):
    w_refs, (pay_ref, gates_ref, middle_ref) = (refs[0:4], refs[4:8]), refs[8:]
    e = e_ref[0]
    total = jnp.zeros((SEQUENCE, 1024), F32)
    for part in range(2):
        features = jnp.concatenate([mixed_ref[:, group_of(e, 2 * q + part)] for q in range(4)], axis=1)
        total = total + dot_f32(features, stacked(w_refs[part], 0, 1024), CONTRACT_PLAIN)
    middle = embed_scale * x_ref[...].astype(F32) + resid_scale * total
    middle_ref[...] = middle
    gain = small_ref[...].astype(F32).T[GAIN_FFN : GAIN_FFN + 1, :]
    normed2 = (middle * inverse_rms(middle) * gain).astype(BF16)
    pay_ref[0:256, :] = normed2
    logits = dot_f32(normed2, small_ref[...], CONTRACT_PLAIN)
    code = code_ref[...]
    member = code >= 0.0
    masked = jnp.where(member, logits, -1e30)
    raised = jnp.where(member, jnp.exp(masked - jnp.max(masked, axis=1, keepdims=True)), 0.0)
    gates = raised / jnp.sum(raised, axis=1, keepdims=True)
    gates_ref[...] = gates
    rows = lambda value: value.T[:EXPERTS, :]
    turned = rows(gates)
    high = turned.astype(BF16).astype(F32)
    middle_part = (turned - high).astype(BF16).astype(F32)
    low = turned - high - middle_part
    pay_ref[256:288, :] = jnp.concatenate([rows(code), high, middle_part, low], axis=1).astype(BF16)


def turn_body(e_ref, sum_ref, add_ref, grad_ref, middle_ref, gates_ref, small_ref, normed2_ref, mixed_ref,
              *refs):
    w_refs, (own_ref, far_ref, mixed_grad_ref, middle_grad_ref, side_ref) = (refs[0:4], refs[4:8]), refs[8:]
    e = e_ref[0]
    upstream = sum_ref[0:256, :].astype(F32) + add_ref[0:256, :].astype(F32)
    table = sum_ref[256:272, :].astype(F32) + add_ref[256:272, :].astype(F32)
    dots = jnp.concatenate([table[:, :256], table[:, 256:512]], axis=0) + jnp.concatenate(
        [table[:, 512:768], table[:, 768:]], axis=0
    )
    dots = jnp.concatenate([dots, jnp.zeros((LANES - EXPERTS, SEQUENCE), F32)], axis=0).T
    gates = gates_ref[...]
    logit_grads = (gates * (dots - jnp.sum(gates * dots, axis=1, keepdims=True))).astype(BF16)
    small = small_ref[...]
    upstream = upstream + dot_f32(logit_grads, small, CONTRACT_LAST)
    middle = middle_ref[...]
    inverse = inverse_rms(middle)
    unit = middle * inverse
    gain = small.astype(F32).T[GAIN_FFN : GAIN_FFN + 1, :]
    gain_grad = jnp.sum(upstream * unit, axis=0, keepdims=True)
    scaled = upstream * gain
    middle_grad = grad_ref[...].astype(F32) + inverse * (
        scaled - unit * jnp.mean(scaled * unit, axis=1, keepdims=True)
    )
    middle_grad_ref[...] = middle_grad
    attn_grad = (resid_scale * middle_grad).astype(BF16)
    line = lax.broadcasted_iota(jnp.int32, (LANES, 1024), 0)
    side_ref[...] = dot_f32(normed2_ref[0:256, :], logit_grads, CONTRACT_FIRST) + jnp.where(
        line == GAIN_FFN, gain_grad, 0.0
    ).T
    for part, out_ref in ((0, own_ref), (1, far_ref)):
        features = jnp.concatenate([mixed_ref[:, group_of(e, 2 * q + part)] for q in range(4)], axis=1)
        out_ref[:, :1024] = dot_f32(features, attn_grad, CONTRACT_FIRST).astype(BF16)
        back = dot_f32(attn_grad, stacked(w_refs[part], 0, 1024), CONTRACT_LAST).astype(BF16)
        for q in range(4):
            mixed_grad_ref[:, group_of(e, 2 * q + part)] = back[:, LANES * q : LANES * (q + 1)]
            at = slice(LANES * q, LANES * (q + 1))
            out_ref[at, 1024:] = side_ref[group_of(e, 2 * q + part), :].astype(BF16)


def attend_back_body(e_ref, x_ref, column_ref, row_ref, cos_ref, sin_ref, q_ref, k_ref, v_ref, grad_ref,
                     normed_ref, middle_grad_ref, *refs):
    lefts, rights = (refs[0:4], refs[4:8]), (refs[8:12], refs[12:16])
    left_refs, right_refs = refs[16:18], refs[18:20]
    embed_ref, raw_ref, scaled_ref = refs[20:]
    e = e_ref[0]
    allowed = allowed_of(column_ref, row_ref)
    unrotate = lambda u: (
        u * wide_table(cos_ref[...], u.shape[1]) - turn_halves(u) * wide_table(sin_ref[...], u.shape[1])
    ).astype(BF16)

    def pair(step, _):
        wide = pl.ds(pl.multiple_of(step * 256, 256), 256)
        narrow = lambda base: pl.ds(pl.multiple_of(base + step * LANES, LANES), LANES)
        q_block, d_block = q_ref[:, wide], grad_ref[:, wide]
        k_block, v_block = k_ref[:, narrow(0)], v_ref[:, narrow(0)]
        q_outs, k_outs, v_outs = [], [], []
        for i in range(2):
            queries, keys = heads_of(q_block, 2 * i, 2), heads_of(k_block, i, 1)
            upstream = heads_of(d_block, 2 * i, 2)
            probs = attention_probs(queries, keys, allowed)
            prob_grads = dot_f32(upstream, heads_of(v_block, i, 1), CONTRACT_LAST)
            centre = jnp.sum(probs * prob_grads, axis=1, keepdims=True)
            score_grads = (probs * (prob_grads - centre)).astype(BF16)
            rows = dot_f32(score_grads, keys, CONTRACT_PLAIN) * attn_scale
            q_outs += [rows[:SEQUENCE], rows[SEQUENCE:]]
            k_outs.append(dot_f32(score_grads, queries, CONTRACT_FIRST) * attn_scale)
            v_outs.append(dot_f32(probs.astype(BF16), upstream, CONTRACT_FIRST))
        raw_ref[:, wide] = unrotate(jnp.concatenate(q_outs, axis=1))
        raw_ref[:, narrow(1024)] = unrotate(jnp.concatenate(k_outs, axis=1))
        raw_ref[:, narrow(1536)] = jnp.concatenate(v_outs, axis=1).astype(BF16)
        return 0

    lax.fori_loop(0, 4, pair, 0)
    resid = embed_scale * x_ref[...].astype(F32)
    inverse = inverse_rms(resid)
    for part in range(2):
        half = normed_ref[:, 512 * part : 512 * part + 512]
        for c in range(2):
            at = slice(512 * c, 512 * c + 512)
            left_refs[part][:, at] = dot_f32(half, raw_ref[:, at], CONTRACT_FIRST).astype(BF16)
            right_refs[part][:, at] = dot_f32(
                half, raw_ref[:, 1024 + 512 * c : 1536 + 512 * c], CONTRACT_FIRST
            ).astype(BF16)
        back = dot_f32(raw_ref[:, :1024], stacked(lefts[part], 0, 1024), CONTRACT_LAST) + dot_f32(
            raw_ref[:, 1024:], stacked(rights[part], 0, 1024), CONTRACT_LAST
        )
        gain = gain_row(lefts[part], GAIN_ATTN)
        gain_grads = []
        for q in range(4):
            at = slice(LANES * q, LANES * (q + 1))
            group = group_of(e, 2 * q + part)
            unit = embed_scale * x_ref[:, group].astype(F32) * inverse
            gain_grads.append(jnp.sum(back[:, at] * unit, axis=0, keepdims=True))
            scaled_ref[:, group] = back[:, at] * gain[:, at]
        line = lax.broadcasted_iota(jnp.int32, (LANES, 512), 0)
        side = jnp.where(line == GAIN_ATTN, jnp.concatenate(gain_grads, axis=1), 0.0).T
        left_refs[part][:, 1024:] = side.astype(BF16)
    unit = resid * inverse
    scaled = scaled_ref[...]
    resid_grad = middle_grad_ref[...] + inverse * (
        scaled - unit * jnp.mean(scaled * unit, axis=1, keepdims=True)
    )
    embed_ref[...] = (embed_scale * resid_grad).astype(BF16)


def local_kernel(body, name, outs, scratch, number, *operands):
    vmem = pl.BlockSpec(memory_space=pltpu.VMEM)
    return pl.pallas_call(
        body,
        out_shape=[jax.ShapeDtypeStruct(shape, dtype) for shape, dtype in outs],
        in_specs=[pl.BlockSpec(memory_space=pltpu.SMEM)] + [vmem] * len(operands),
        out_specs=[vmem] * len(outs),
        scratch_shapes=[pltpu.VMEM(shape, dtype) for shape, dtype in scratch],
        compiler_params=pltpu.CompilerParams(vmem_limit_bytes=56 * 1024 * 1024),
        cost_estimate=pl.CostEstimate(flops=1000, bytes_accessed=1000, transcendentals=0),
        name=name,
    )(number, *operands)


def together(*values):
    return lax.optimization_barrier(values)


def core_sum(own, far):
    return (own.astype(F32) + over_expert(far, 1).astype(F32)).astype(BF16)


def xor_order(pieces, at):
    stacked = jnp.stack(pieces)
    return jnp.concatenate(
        [lax.dynamic_index_in_dim(stacked, at ^ i, 0, keepdims=False) for i in range(len(pieces))]
    )


def exchange(slices):
    return lax.all_to_all(slices, "shard", split_axis=0, concat_axis=0, tiled=True)


def expert_slices(weights, part):
    return jnp.stack([weights[OWN * (d % PAIR) + part] for d in range(4)])


def over_x(value):
    return over_expert(value, 2)


def over_y(value):
    return over_expert(value, 4)


def spread(value, first, second):
    near = {first: first(value), second: second(value)}
    return [value, near[over_x], near[over_y], second(near[first])]


def bf_sum(*values):
    return sum(value.astype(F32) for value in values).astype(BF16)


def pack_body(query_ref, key_ref, value_ref, router_ref, attn_ref, ffn_ref, out_ref, pack_ref):
    pack_ref[:, 0:1024] = query_ref[...].astype(BF16)
    row = lax.broadcasted_iota(jnp.int32, (32, 32), 0)
    diagonal = row == lax.broadcasted_iota(jnp.int32, (32, 32), 1)
    upright = lambda ref: jnp.sum(jnp.where(diagonal, ref[...], 0.0), axis=1, keepdims=True)
    zeros = jnp.zeros((32, LANES - EXPERTS - 2), F32)
    small = jnp.concatenate([router_ref[...], upright(attn_ref), upright(ffn_ref), zeros], axis=1)
    pack_ref[:, 1024:1152] = small.astype(BF16)
    pack_ref[:, 1152:1664] = key_ref[...].astype(BF16)
    pack_ref[:, 1664:2176] = value_ref[...].astype(BF16)
    pack_ref[:, 2176:] = out_ref[...].astype(BF16)


def plane_body(z_ref, *refs):
    z = z_ref[0]
    for group, (a, b) in enumerate(((0, 1152), (1152, 2176), (2176, 3328))):
        mine, one, other = refs[3 * group : 3 * group + 3]
        for k in range(4):
            rows = pl.ds(pl.multiple_of((z ^ k) * 32, 32), 32)
            total = mine[rows, :].astype(F32) + one[rows, :].astype(F32) + other[rows, :].astype(F32)
            refs[9 + k][:, a:b] = total.astype(BF16)


def settle_body(z_ref, *refs):
    sources, outs = refs[:4], refs[4:]
    total = lambda a, b: sum(ref[:, a:b].astype(F32) for ref in sources)
    bounds = ((0, 1024), (1152, 1664), (1664, 2176), (2176, 3200))
    for out_ref, (a, b) in zip(outs, bounds):
        out_ref[...] = total(a, b)
    row = lax.broadcasted_iota(jnp.int32, (32, 32), 0)
    diagonal = row == lax.broadcasted_iota(jnp.int32, (32, 32), 1)
    flat = lambda column: jnp.sum(jnp.where(diagonal, column, 0.0), axis=0, keepdims=True)
    late, early = total(1024, 1152), total(3200, 3328)
    outs[4][...] = early[:, :EXPERTS]
    outs[5][...] = flat(late[:, GAIN_ATTN : GAIN_ATTN + 1])
    outs[6][...] = flat(early[:, GAIN_FFN : GAIN_FFN + 1])


def owner_body(first_part, one_ref, two_ref, *refs):
    in_ref, out_ref = refs if first_part else refs[2:]
    total = one_ref[...].astype(F32) + two_ref[...].astype(F32)
    in_ref[...] = total[:, :256]
    out_ref[...] = total[:, 256:]


def owner_sum(part, slices, before=()):
    block = lambda rows, at: pl.BlockSpec((1, rows, 1024), lambda d: (at(d), 0, 0))
    place = lambda d: 2 * d + part
    return pl.pallas_call(
        functools.partial(owner_body, not before),
        out_shape=[jax.ShapeDtypeStruct((4, rows, 1024), F32) for rows in (256, 128)],
        grid=(2,),
        in_specs=[block(384, lambda d: d), block(384, lambda d: d + 2)]
        + [pl.BlockSpec(memory_space=pl.ANY)] * len(before),
        out_specs=[block(256, place), block(128, place)],
        input_output_aliases={2: 0, 3: 1} if before else {},
        name="owner_sum",
    )(slices, slices, *before)


def plane_fold(total, first, second):
    part = lambda q: total[128 * q : 128 * (q + 1)]
    one, two = (1, 2) if first is over_x else (2, 1)
    passing, mine = first(part(3)), first(part(one))
    return [part(0), mine, second(bf_sum(part(two), passing))]


def pack_call(*operands):
    return pl.pallas_call(
        pack_body,
        out_shape=jax.ShapeDtypeStruct((32, 3200), BF16),
        in_specs=[pl.BlockSpec(memory_space=pltpu.VMEM)] * len(operands),
        out_specs=pl.BlockSpec(memory_space=pltpu.VMEM),
        name="pack",
    )(*operands)


def per_device_fast(
    embedded,
    document_numbers,
    expert_ids,
    attn_gain,
    ffn_gain,
    w_query,
    key_projection,
    value_projection,
    w_out,
    w_router,
    expert_in,
    expert_out,
    cotangent,
):
    e = lax.axis_index("expert")
    z = lax.axis_index("shard")
    place = e.reshape(1)
    pack = pack_call(
        w_query, key_projection, value_projection, w_router, attn_gain[None, :], ffn_gain[None, :], w_out
    )
    pack, grad_early = together(pack, cotangent)
    plane = xor_order([pack] + [over_shard(pack, k) for k in (1, 2, 3)], z)
    out_pair = over_shard(grad_early, 1)
    out_x, out_y = over_x(grad_early), over_y(grad_early)
    slices = [expert_slices(w, 0) for w in (expert_in, expert_out)]
    second = jnp.concatenate([expert_slices(w, 1) for w in (expert_in, expert_out)], axis=1)
    plane, out_x, out_y, slices[0] = together(plane, out_x, out_y, slices[0])
    left = spread(plane[:, :1152], over_x, over_y)
    right = spread(plane[:, 1152:2176], over_y, over_x)
    slices[0], out_pair, left[1], right[2] = together(slices[0], out_pair, left[1], right[2])
    in0 = exchange(slices[0])
    swap = lambda values: [over_expert(value, 1) for value in values]
    left_far, right_far = swap(left), swap(right)
    left[3], right[3], plane, out_pair, out_x = together(left[3], right[3], plane, out_pair, out_x)
    out_w = [plane[:, 2176:]] + [over_expert(plane[:, 2176:], bits) for bits in (2, 4, 6)]
    out_blocks = [cotangent, out_x, out_y, over_y(out_x), out_pair, over_x(out_pair), over_y(out_pair)]

    segments = document_numbers[0]
    column, row = segments[:, None], segments[None, :]
    cosine, sine = (jnp.concatenate([table] * 4, axis=1) for table in rope_tables(segments))
    lanes = jnp.arange(LANES, dtype=jnp.int32)
    member = jnp.any(expert_ids[:, :, None] == lanes, axis=1)
    index = jnp.arange(SEQUENCE, dtype=jnp.int32)
    below = (index[None, :] < index[:, None]).astype(BF16)
    rank = jnp.dot(below, member.astype(BF16), preferred_element_type=F32)
    code = jnp.where(member, rank, -1.0)

    wide, half = (SEQUENCE, 1024), (SEQUENCE, 512)
    weights = left + left_far + right + right_far
    normed, queries, keys, values, mixed, small_all = local_kernel(
        attend_body, "attend",
        [(wide, BF16), (wide, BF16), (half, BF16), (half, BF16), (wide, BF16), ((1024, LANES), BF16)], [],
        place, embedded, column, row, cosine, sine, *weights,
    )
    *out_w, mixed = together(*out_w, mixed)
    out_w = out_w + swap(out_w)
    payload, gates, middle = local_kernel(
        route_body, "route", [((288, 1024), BF16), ((SEQUENCE, LANES), F32), (wide, F32)], [],
        place, embedded, mixed, small_all, code, *out_w,
    )
    pay_pair = over_shard(payload, 1)
    pay_x, pay_y = over_x(payload), over_y(payload)
    pay_x, pay_y, pay_pair, *out_blocks = together(pay_x, pay_y, pay_pair, *out_blocks)
    slices[1], in0, pay_pair = together(slices[1], in0, pay_pair)
    out0 = exchange(slices[1])
    out_blocks.append(over_x(out_blocks[6]))
    tok_own = [payload, pay_x, pay_y, over_y(pay_x)]
    tok_pair = [pay_pair, over_x(pay_pair), over_y(pay_pair)]
    *tok_pair, out_blocks[7], out0, second = together(*tok_pair, out_blocks[7], out0, second)
    tok_pair.append(over_x(tok_pair[2]))
    weights0 = [in0, out0]
    weights1 = [exchange(second)]
    weights0_far = swap(weights0)
    tokens = tok_own + tok_pair
    first = (e * 4 + z % PAIR * OWN).reshape(1)
    first_far = ((e ^ 1) * 4 + z % PAIR * OWN).reshape(1)
    sums, grad_b = expert_call(first_far, tokens, out_blocks, weights0_far)
    sums, grad_a = expert_call(first, tokens, out_blocks, weights0, sums)
    expert_grad0 = core_sum(grad_a, grad_b)
    expert_grad0, *weights1 = together(expert_grad0, *weights1)
    slices0 = exchange(expert_grad0)
    weights1_far = swap(weights1)
    sums, grad_d = expert_call(first_far + 1, tokens, out_blocks, weights1_far, sums)
    sums, grad_c = expert_call(first + 1, tokens, out_blocks, weights1, sums)
    rows, moes = sums[:BLOCKS], sums[BLOCKS:]
    expert_grad1 = core_sum(grad_c, grad_d)
    own, pair = rows[:4], rows[4:]
    pair_pass, own_pass = over_x(pair[3]), over_y(own[3])
    pair_mine = over_x(pair[1])
    pair_pass, expert_grad1, slices0 = together(pair_pass, expert_grad1, slices0)
    pair_other = over_y(bf_sum(pair[2], pair_pass))
    mine, pair_pass = together(own[2], pair_pass)
    own_mine = over_y(mine)
    own_other = over_x(bf_sum(own[1], own_pass))
    row_pair = bf_sum(pair[0], pair_mine, pair_other)
    returned = over_shard(row_pair, 1)
    row_pair, *moes = together(row_pair, *moes)
    moe_pass, moe_own_pass = over_x(moes[7]), over_y(moes[3])
    moe_mine, moe_own_mine = over_x(moes[5]), over_y(moes[2])
    owned = owner_sum(0, slices0)
    own_other, *owned = together(own_other, *owned)
    row_own = bf_sum(own[0], own_mine, own_other)
    returned, expert_grad1, slices0 = together(returned, expert_grad1, slices0)
    slices1 = exchange(expert_grad1)
    early_own, early_far, mixed_grad, middle_grad = local_kernel(
        turn_body, "turn", [((512, 1152), BF16), ((512, 1152), BF16), (wide, BF16), (wide, F32)],
        [((1024, LANES), F32)], place, row_own, returned, cotangent, middle, gates,
        small_all, payload, mixed, *out_w,
    )
    middle_grad, moe_mine, moe_own_mine = together(middle_grad, moe_mine, moe_own_mine)
    moe_rest, moe_own_rest = over_y(bf_sum(moes[6], moe_pass)), over_x(bf_sum(moes[1], moe_own_pass))
    left_own, left_far, right_own, right_far, grad_embedded = local_kernel(
        attend_back_body, "attend_back", [((512, 1152), BF16)] * 2 + [((512, 1024), BF16)] * 2 + [(wide, BF16)],
        [((SEQUENCE, 2048), BF16), (wide, F32)], place, embedded, column, row, cosine, sine,
        queries, keys, values, mixed_grad, normed, middle_grad, *weights,
    )
    left_far, right_far, moe_rest, moe_own_rest = together(left_far, right_far, moe_rest, moe_own_rest)
    moe_pair = bf_sum(moes[4], moe_mine, moe_rest)
    moe_own = bf_sum(moes[0], moe_own_mine, moe_own_rest)
    moe_other = over_shard(moe_pair, 1)
    addends = plane_fold(core_sum(left_own, left_far), over_x, over_y)
    addends += plane_fold(core_sum(right_own, right_far), over_y, over_x)
    addends += plane_fold(core_sum(early_own, early_far), over_y, over_x)
    addends[0], slices1 = together(addends[0], slices1)
    planes = local_kernel(plane_body, "plane", [((32, 3328), BF16)] * 4, [], z.reshape(1), *addends)
    planes = [planes[0]] + [over_shard(planes[k], k) for k in (1, 2, 3)]
    shapes = [(32, 1024), (32, 512), (32, 512), (32, 1024), (32, EXPERTS), (1, 32), (1, 32)]
    late_query, late_key, late_value, early_out, router, gain_attn, gain_ffn = local_kernel(
        settle_body, "settle", [(shape, F32) for shape in shapes], [], z.reshape(1), *planes
    )
    grad_expert_in, grad_expert_out = owner_sum(1, slices1, owned)
    moe = moe_own.astype(F32) + moe_other.astype(F32)
    output = (middle + resid_scale * moe).astype(BF16)
    return (
        output,
        grad_embedded,
        gain_attn[0],
        gain_ffn[0],
        late_query,
        late_key,
        late_value,
        early_out,
        router,
        grad_expert_in,
        grad_expert_out,
    )


def solution(mesh):
    owners, shards = mesh.shape["expert"], mesh.shape["shard"]
    fast = owners == 8 and shards == 4
    both = ("expert", "shard")
    rows = P(both, None)
    weights = P("expert", "shard", None)
    return jax.shard_map(
        per_device_fast if fast else per_device_general,
        mesh=mesh,
        in_specs=(rows,) * 3 + (P(both),) * 2 + (rows,) * 5 + (weights,) * 2 + (rows,),
        out_specs=(rows,) * 2 + (P(both),) * 2 + (rows,) * 5 + (weights,) * 2,
        check_vma=False,
    )
```

```python
import functools

import jax
import jax.numpy as jnp
from jax import lax
from jax.experimental import pallas as pl
from jax.experimental.pallas import tpu as pltpu
from jax.sharding import PartitionSpec as P

MODEL_WIDTH = 1024
QUERY_HEADS = 16
KEY_VALUE_HEADS = 8
HEAD_SIZE = 64
FF = 512
EXPERTS = 32
TOPK = 8
CAP = 128


embed_scale = 12.0
attn_scale = 0.015625
resid_scale = 0.22
norm_eps = 1e-06
rope_base = 10000.0


def rope_tables(segments):
    sequence_length = segments.shape[0]
    key_index = jnp.arange(sequence_length, dtype=jnp.int32)
    change = jnp.concatenate([jnp.ones((1,), jnp.bool_), segments[1:] != segments[:-1]])
    begins = lax.cummax(jnp.where(change, key_index, 0), axis=0)
    places = (key_index - begins).astype(jnp.float32)
    freqs = rope_base ** (-2.0 * jnp.arange(HEAD_SIZE // 2, dtype=jnp.float32) / HEAD_SIZE)
    angles = places[:, None] * freqs[None, :]
    return (jnp.cos(angles), jnp.sin(angles))


def apply_rotation(value_heads, cosine_table, sine_table):
    halfway = value_heads.shape[-1] // 2
    first_half = value_heads[..., :halfway]
    second_half = value_heads[..., halfway:]
    cos_part = cosine_table[:, None, :]
    sin_part = sine_table[:, None, :]
    return jnp.concatenate(
        [
            first_half * cos_part - second_half * sin_part,
            second_half * cos_part + first_half * sin_part,
        ],
        axis=-1,
    )


def reverse_rotation(grads, cosine_table, sine_table):
    halfway = grads.shape[-1] // 2
    first_half = grads[..., :halfway]
    second_half = grads[..., halfway:]
    cos_part = cosine_table[:, None, :]
    sin_part = sine_table[:, None, :]
    return jnp.concatenate(
        [
            first_half * cos_part + second_half * sin_part,
            second_half * cos_part - first_half * sin_part,
        ],
        axis=-1,
    )


def norm_forward(value_heads):
    inverse = lax.rsqrt(jnp.mean(value_heads * value_heads, axis=1, keepdims=True) + norm_eps)
    return (value_heads * inverse, inverse)


def norm_backward(upstream, unit_values, inverse, gain):
    scaled = upstream * gain
    grad_values = inverse * (
        scaled - unit_values * jnp.mean(scaled * unit_values, axis=1, keepdims=True)
    )
    return (grad_values, jnp.sum(upstream * unit_values, axis=0))


def slot_tables(expert_ids):
    flat_ids = expert_ids.reshape(-1)
    count_all = flat_ids.shape[0]
    matches = (flat_ids[:, None] == jnp.arange(EXPERTS, dtype=jnp.int32)[None, :]).astype(jnp.int32)
    before = jnp.cumsum(matches, axis=0) - 1
    ranking = jnp.sum(before * matches, axis=1)
    target = flat_ids * CAP + ranking
    source = (
        jnp.zeros((EXPERTS * CAP,), jnp.int32)
        .at[target]
        .set(jnp.arange(count_all, dtype=jnp.int32))
    )
    filled = (
        jnp.zeros((EXPERTS * CAP,), jnp.int32).at[target].set(jnp.ones((count_all,), jnp.int32))
    )
    return (target, source, filled)


def silu_parts(gate_up):
    gate_part = gate_up[..., :FF]
    up_part = gate_up[..., FF:]
    sigmoid_gate = jax.nn.sigmoid(gate_part)
    hidden = (gate_part * sigmoid_gate * up_part).astype(jnp.bfloat16)
    return (gate_part, up_part, sigmoid_gate, hidden)


def per_device_general(
    embedded,
    document_numbers,
    expert_ids,
    attn_gain,
    ffn_gain,
    w_query,
    key_projection,
    value_projection,
    w_out,
    w_router,
    expert_in,
    expert_out,
    cotangent,
):
    mixer = (
        lax.all_gather(attn_gain.astype(jnp.bfloat16), ("expert", "shard"), axis=0, tiled=True),
        lax.all_gather(ffn_gain.astype(jnp.bfloat16), ("expert", "shard"), axis=0, tiled=True),
        lax.all_gather(w_query.astype(jnp.bfloat16), ("expert", "shard"), axis=0, tiled=True),
        lax.all_gather(
            key_projection.astype(jnp.bfloat16), ("expert", "shard"), axis=0, tiled=True
        ),
        lax.all_gather(
            value_projection.astype(jnp.bfloat16), ("expert", "shard"), axis=0, tiled=True
        ),
        lax.all_gather(w_out.astype(jnp.bfloat16), ("expert", "shard"), axis=0, tiled=True),
        lax.all_gather(w_router.astype(jnp.bfloat16), ("expert", "shard"), axis=0, tiled=True),
    )
    gain_attn, gain_ffn, query_w, key_w, value_w, out_w, router_w = mixer
    full_in, full_out = (
        lax.all_gather(expert_in, "shard", axis=1, tiled=True),
        lax.all_gather(expert_out, "shard", axis=1, tiled=True),
    )
    sequence_length = embedded.shape[0]
    query_groups = QUERY_HEADS // KEY_VALUE_HEADS
    owners = lax.axis_size("expert")
    local_count = EXPERTS // owners
    received = owners * CAP
    resid = embed_scale * embedded.astype(jnp.float32)
    unit_attn, inverse_attn = norm_forward(resid)
    normed = (unit_attn * gain_attn.astype(jnp.float32)).astype(jnp.bfloat16)
    unrotated_query = jnp.dot(normed, query_w, preferred_element_type=jnp.float32)
    unrotated_key = jnp.dot(normed, key_w, preferred_element_type=jnp.float32)
    projected_value = jnp.dot(normed, value_w, preferred_element_type=jnp.float32)
    segments = document_numbers[0]
    cosine_table, sine_table = rope_tables(segments)
    query_heads = (
        apply_rotation(
            unrotated_query.reshape(sequence_length, QUERY_HEADS, HEAD_SIZE),
            cosine_table,
            sine_table,
        )
        .astype(jnp.bfloat16)
        .reshape(sequence_length, KEY_VALUE_HEADS, query_groups, HEAD_SIZE)
    )
    key_heads = apply_rotation(
        unrotated_key.reshape(sequence_length, KEY_VALUE_HEADS, HEAD_SIZE), cosine_table, sine_table
    ).astype(jnp.bfloat16)
    value_heads = projected_value.astype(jnp.bfloat16).reshape(
        sequence_length, KEY_VALUE_HEADS, HEAD_SIZE
    )
    block_rows = min(512, sequence_length)
    starts = jnp.arange(sequence_length // block_rows, dtype=jnp.int32) * block_rows
    key_index = jnp.arange(sequence_length, dtype=jnp.int32)

    def block_scores(first_row):
        row_index = first_row + jnp.arange(block_rows, dtype=jnp.int32)
        raw_scores = (
            jnp.einsum("qhgd,khd->hgqk", query_heads, key_heads, preferred_element_type=jnp.float32)
            * attn_scale
        )
        allowed = (key_index[None, :] <= row_index[:, None]) & (
            segments[None, :] == segments[:, None]
        )
        return (jnp.where(allowed, raw_scores, -1e30), query_heads)

    def attend_block(first_row):
        scores, query_rows = block_scores(first_row)
        row_max = jnp.max(scores, axis=-1, keepdims=True)
        exps = jnp.exp(scores - row_max)
        totals = jnp.sum(exps, axis=-1, keepdims=True)
        weights = (exps / totals).astype(jnp.bfloat16)
        mixed_rows = jnp.einsum(
            "hgqk,khd->qhgd", weights, value_heads, preferred_element_type=jnp.float32
        )
        return (mixed_rows.astype(jnp.bfloat16), (row_max + jnp.log(totals))[..., 0])

    mixed_blocks, log_totals = lax.map(attend_block, starts)
    mixed_heads_output = mixed_blocks.reshape(sequence_length, QUERY_HEADS * HEAD_SIZE)
    middle = resid + resid_scale * jnp.dot(
        mixed_heads_output, out_w, preferred_element_type=jnp.float32
    )
    unit_ffn, inverse_ffn = norm_forward(middle)
    normed2 = (unit_ffn * gain_ffn.astype(jnp.float32)).astype(jnp.bfloat16)
    logits = jnp.dot(normed2, router_w, preferred_element_type=jnp.float32)
    pick_table = expert_ids[:, :, None] == jnp.arange(EXPERTS, dtype=jnp.int32)[None, None, :]
    chosen = jnp.sum(jnp.where(pick_table, logits[:, None, :], 0.0), axis=2)
    exps_chosen = jnp.exp(chosen - jnp.max(chosen, axis=1, keepdims=True))
    gates = exps_chosen / jnp.sum(exps_chosen, axis=1, keepdims=True)
    target, source, filled = slot_tables(expert_ids)
    live_slots = filled[:, None] == 1
    zero_bf = jnp.zeros((), jnp.bfloat16)
    send_rows = jnp.where(live_slots, normed2[source // TOPK], zero_bf).reshape(
        owners, local_count, CAP, MODEL_WIDTH
    )
    arrived = lax.all_to_all(send_rows, "expert", split_axis=0, concat_axis=2, tiled=True).reshape(
        local_count, received, MODEL_WIDTH
    )
    gate_up = jnp.einsum("erd,edf->erf", arrived, full_in, preferred_element_type=jnp.float32)
    gate_part, up_part, sigmoid_gate, hidden = silu_parts(gate_up)
    produced = jnp.einsum(
        "erf,efd->erd", hidden, full_out, preferred_element_type=jnp.float32
    ).astype(jnp.bfloat16)
    returned = lax.all_to_all(
        produced.reshape(1, local_count, received, MODEL_WIDTH),
        "expert",
        split_axis=2,
        concat_axis=0,
        tiled=True,
    ).reshape(EXPERTS * CAP, MODEL_WIDTH)
    slot_values = returned[target].reshape(sequence_length, TOPK, MODEL_WIDTH)
    moe = jnp.einsum("tk,tkd->td", gates, slot_values.astype(jnp.float32))
    output = (middle + resid_scale * moe).astype(jnp.bfloat16)
    grad_output = cotangent.astype(jnp.float32)
    grad_mix = resid_scale * grad_output
    gate_grads = jnp.einsum("tkd,td->tk", slot_values.astype(jnp.float32), grad_mix)
    slot_grads = (
        (gates[:, :, None] * grad_mix[:, None, :])
        .astype(jnp.bfloat16)
        .reshape(sequence_length * TOPK, MODEL_WIDTH)
    )
    grad_send = jnp.where(live_slots, slot_grads[source], zero_bf).reshape(
        owners, local_count, CAP, MODEL_WIDTH
    )
    grad_arrived = lax.all_to_all(
        grad_send, "expert", split_axis=0, concat_axis=2, tiled=True
    ).reshape(local_count, received, MODEL_WIDTH)
    owner_rows = lax.all_to_all(
        send_rows, "expert", split_axis=0, concat_axis=2, tiled=True
    ).reshape(local_count, received, MODEL_WIDTH)
    owner_gate_up = jnp.einsum(
        "erd,edf->erf", owner_rows, full_in, preferred_element_type=jnp.float32
    )
    owner_gate, owner_up, owner_sigmoid, owner_hidden = silu_parts(owner_gate_up)
    hidden_grad = jnp.einsum(
        "erd,efd->erf", grad_arrived, full_out, preferred_element_type=jnp.float32
    )
    gate_grad_part = (
        hidden_grad * owner_up * owner_sigmoid * (1.0 + owner_gate * (1.0 - owner_sigmoid))
    )
    up_grad_part = hidden_grad * owner_gate * owner_sigmoid
    gate_up_grad = jnp.concatenate([gate_grad_part, up_grad_part], axis=-1).astype(jnp.bfloat16)
    grad_full_out = jnp.einsum(
        "erf,erd->efd", owner_hidden, grad_arrived, preferred_element_type=jnp.float32
    )
    grad_full_in = jnp.einsum(
        "erd,erf->edf", owner_rows, gate_up_grad, preferred_element_type=jnp.float32
    )
    row_grads = jnp.einsum(
        "erf,edf->erd", gate_up_grad, full_in, preferred_element_type=jnp.float32
    ).astype(jnp.bfloat16)
    grad_returned = lax.all_to_all(
        row_grads.reshape(1, local_count, received, MODEL_WIDTH),
        "expert",
        split_axis=2,
        concat_axis=0,
        tiled=True,
    ).reshape(EXPERTS * CAP, MODEL_WIDTH)
    grad_expert_in, grad_expert_out = (
        lax.psum_scatter(
            grad_full_in.astype(jnp.bfloat16), "shard", scatter_dimension=1, tiled=True
        ).astype(jnp.float32),
        lax.psum_scatter(
            grad_full_out.astype(jnp.bfloat16), "shard", scatter_dimension=1, tiled=True
        ).astype(jnp.float32),
    )
    mixer_back = (
        lax.all_gather(attn_gain.astype(jnp.bfloat16), ("expert", "shard"), axis=0, tiled=True),
        lax.all_gather(ffn_gain.astype(jnp.bfloat16), ("expert", "shard"), axis=0, tiled=True),
        lax.all_gather(w_query.astype(jnp.bfloat16), ("expert", "shard"), axis=0, tiled=True),
        lax.all_gather(
            key_projection.astype(jnp.bfloat16), ("expert", "shard"), axis=0, tiled=True
        ),
        lax.all_gather(
            value_projection.astype(jnp.bfloat16), ("expert", "shard"), axis=0, tiled=True
        ),
        lax.all_gather(w_out.astype(jnp.bfloat16), ("expert", "shard"), axis=0, tiled=True),
        lax.all_gather(w_router.astype(jnp.bfloat16), ("expert", "shard"), axis=0, tiled=True),
    )
    back_gain_attn, back_gain_ffn, back_query, back_key, back_value, back_out, back_router = (
        mixer_back
    )
    chosen_grad = gates * (gate_grads - jnp.sum(gates * gate_grads, axis=1, keepdims=True))
    logit_grads = jnp.sum(jnp.where(pick_table, chosen_grad[:, :, None], 0.0), axis=1).astype(
        jnp.bfloat16
    )
    grad_router_full = jnp.einsum(
        "td,te->de", normed2, logit_grads, preferred_element_type=jnp.float32
    )
    normed2_grad = jnp.sum(
        grad_returned[target].reshape(sequence_length, TOPK, MODEL_WIDTH), axis=1, dtype=jnp.float32
    )
    normed2_grad = normed2_grad + jnp.einsum(
        "te,de->td", logit_grads, back_router, preferred_element_type=jnp.float32
    )
    middle_norm_grad, grad_gain_ffn = norm_backward(
        normed2_grad, unit_ffn, inverse_ffn, back_gain_ffn.astype(jnp.float32)
    )
    middle_grad = grad_output + middle_norm_grad
    attn_grad = (resid_scale * middle_grad).astype(jnp.bfloat16)
    grad_out_full = jnp.einsum(
        "tf,td->fd", mixed_heads_output, attn_grad, preferred_element_type=jnp.float32
    )
    mixed_output_gradient = jnp.einsum(
        "td,fd->tf", attn_grad, back_out, preferred_element_type=jnp.float32
    ).astype(jnp.bfloat16)
    mixed_gradient_by_head = mixed_output_gradient.reshape(
        sequence_length, KEY_VALUE_HEADS, query_groups, HEAD_SIZE
    )

    def attend_back(carries, packed):
        key_acc, value_acc = carries
        first_row, log_rows = packed
        scores, query_rows = block_scores(first_row)
        probs = jnp.exp(scores - log_rows[..., None])
        prob_grads = jnp.einsum(
            "qhgd,khd->hgqk",
            mixed_gradient_by_head,
            value_heads,
            preferred_element_type=jnp.float32,
        )
        score_grads = (
            probs * (prob_grads - jnp.sum(probs * prob_grads, axis=-1, keepdims=True))
        ).astype(jnp.bfloat16)
        query_grads = (
            jnp.einsum("hgqk,khd->qhgd", score_grads, key_heads, preferred_element_type=jnp.float32)
            * attn_scale
        )
        key_acc = (
            key_acc
            + jnp.einsum(
                "hgqk,qhgd->khd", score_grads, query_rows, preferred_element_type=jnp.float32
            )
            * attn_scale
        )
        value_acc = value_acc + jnp.einsum(
            "hgqk,qhgd->khd",
            probs.astype(jnp.bfloat16),
            mixed_gradient_by_head,
            preferred_element_type=jnp.float32,
        )
        return ((key_acc, value_acc), query_grads)

    empty_head_rows = jnp.zeros((sequence_length, KEY_VALUE_HEADS, HEAD_SIZE), jnp.float32)
    (summed_key_gradient, summed_value_gradient), query_grad_blocks = lax.scan(
        attend_back, (empty_head_rows, empty_head_rows), (starts, log_totals)
    )
    query_raw_grad = (
        reverse_rotation(
            query_grad_blocks.reshape(sequence_length, QUERY_HEADS, HEAD_SIZE),
            cosine_table,
            sine_table,
        )
        .astype(jnp.bfloat16)
        .reshape(sequence_length, QUERY_HEADS * HEAD_SIZE)
    )
    key_raw_grad = (
        reverse_rotation(summed_key_gradient, cosine_table, sine_table)
        .astype(jnp.bfloat16)
        .reshape(sequence_length, KEY_VALUE_HEADS * HEAD_SIZE)
    )
    projected_value_gradient = summed_value_gradient.astype(jnp.bfloat16).reshape(
        sequence_length, KEY_VALUE_HEADS * HEAD_SIZE
    )
    grad_query_full = jnp.einsum(
        "td,tf->df", normed, query_raw_grad, preferred_element_type=jnp.float32
    )
    grad_key_full = jnp.einsum(
        "td,tf->df", normed, key_raw_grad, preferred_element_type=jnp.float32
    )
    grad_value_full = jnp.einsum(
        "td,tf->df", normed, projected_value_gradient, preferred_element_type=jnp.float32
    )
    normed_grad = jnp.einsum(
        "tf,df->td", query_raw_grad, back_query, preferred_element_type=jnp.float32
    )
    normed_grad = normed_grad + jnp.einsum(
        "tf,df->td", key_raw_grad, back_key, preferred_element_type=jnp.float32
    )
    normed_grad = normed_grad + jnp.einsum(
        "tf,df->td", projected_value_gradient, back_value, preferred_element_type=jnp.float32
    )
    resid_norm_grad, grad_gain_attn = norm_backward(
        normed_grad, unit_attn, inverse_attn, back_gain_attn.astype(jnp.float32)
    )
    resid_grad = middle_grad + resid_norm_grad
    grad_embedded = (embed_scale * resid_grad).astype(jnp.bfloat16)
    summed = (
        lax.psum_scatter(grad_gain_attn, ("expert", "shard"), scatter_dimension=0, tiled=True),
        lax.psum_scatter(grad_gain_ffn, ("expert", "shard"), scatter_dimension=0, tiled=True),
        lax.psum_scatter(grad_query_full, ("expert", "shard"), scatter_dimension=0, tiled=True),
        lax.psum_scatter(grad_key_full, ("expert", "shard"), scatter_dimension=0, tiled=True),
        lax.psum_scatter(grad_value_full, ("expert", "shard"), scatter_dimension=0, tiled=True),
        lax.psum_scatter(grad_out_full, ("expert", "shard"), scatter_dimension=0, tiled=True),
        lax.psum_scatter(grad_router_full, ("expert", "shard"), scatter_dimension=0, tiled=True),
    )
    return (
        output,
        grad_embedded,
        summed[0],
        summed[1],
        summed[2],
        summed[3],
        summed[4],
        summed[5],
        summed[6],
        grad_expert_in,
        grad_expert_out,
    )


BF16 = jnp.bfloat16
F32 = jnp.float32
PAIR = 2
OWN = 2


def over_expert(value, bits):
    return lax.ppermute(value, "expert", [(i, i ^ bits) for i in range(8)])


def over_shard(value, bits):
    return lax.ppermute(value, "shard", [(i, i ^ bits) for i in range(4)])


def dot_f32(left, right, dims):
    return lax.dot_general(left, right, dims, preferred_element_type=F32)


CONTRACT_LAST = (((1,), (1,)), ((), ()))
CONTRACT_FIRST = (((0,), (0,)), ((), ()))
CONTRACT_PLAIN = (((1,), (0,)), ((), ()))
BLOCKS = 8
HALF = 4
ROWS = HALF * CAP
PAY_ROWS = 288
SUM_ROWS = 272


def expert_body(first_part, packed, number_ref, *refs):
    refs = list(refs)
    take = lambda count: [refs.pop(0) for _ in range(count)]
    tok_refs, out_refs = take(BLOCKS), take(BLOCKS)
    if packed:
        (w_ref,) = take(1)
        w_in_ref, w_out_ref = w_ref.at[:, 0:256, :], w_ref.at[:, 256:384, :]
    else:
        w_in_ref, w_out_ref = take(2)
    row_before, moe_before = ([], []) if first_part else (take(BLOCKS), take(BLOCKS))
    row_outs, moe_outs = take(BLOCKS), take(BLOCKS)
    (grad_ref,) = take(1)
    (tok_s, out_s, w_in_s, w_out_s, row_s, moe_s, grad_s, x_s, g_s, gate_s, table_s, back_s, mix_s, dot_s,
     in_acc, out_acc, tok_sem, out_sem, w_sem, row_sem, moe_sem, row_out_sem, moe_out_sem, grad_sem) = refs
    number = number_ref[0]
    copy = pltpu.make_async_copy
    for j in range(BLOCKS):
        copy(tok_refs[j], tok_s.at[j], tok_sem.at[j]).start()
        copy(out_refs[j], out_s.at[j], out_sem.at[j]).start()
        if j == HALF - 1:
            copy(w_in_ref, w_in_s, w_sem.at[0]).start()
            copy(w_out_ref, w_out_s, w_sem.at[1]).start()
    if not first_part:
        for j in range(BLOCKS):
            copy(row_before[j], row_s.at[j], row_sem.at[j]).start()
            copy(moe_before[j], moe_s.at[j], moe_sem.at[j]).start()

    def mask_of(i):
        slot = lax.broadcasted_iota(jnp.int32, (CAP, 256), 0).astype(F32)
        return slot == table_s[i, 0:1, :]

    def half_step(half, _):
        for i in range(HALF):
            j = half * HALF + i
            copy(tok_s.at[j], tok_s.at[j], tok_sem.at[j]).wait()
            copy(out_s.at[j], out_s.at[j], out_sem.at[j]).wait()
            aux = tok_s[j, 256:PAY_ROWS, :].astype(F32)
            line = lax.broadcasted_iota(jnp.int32, (EXPERTS, 1024), 0)
            line = jnp.sum(jnp.where(line == number, aux, 0.0), axis=0, keepdims=True)
            table_s[i, 0:1, :] = line[:, :256]
            gate = line[:, 256:512] + line[:, 512:768] + line[:, 768:]
            mask = mask_of(i)
            pick = jnp.where(mask, 1.0, 0.0).astype(BF16)
            at = slice(i * CAP, (i + 1) * CAP)
            x_s[at, :] = dot_f32(pick, tok_s[j, 0:256, :], CONTRACT_PLAIN).astype(BF16)
            g_s[at, :] = resid_scale * dot_f32(pick, out_s[j], CONTRACT_PLAIN)
            gate_s[at, :] = jnp.sum(jnp.where(mask, gate, 0.0), axis=1, keepdims=True)

        @pl.when(half == 0)
        def _():
            copy(w_in_ref, w_in_s, w_sem.at[0]).wait()
            copy(w_out_ref, w_out_s, w_sem.at[1]).wait()

        w_in = w_in_s[...].reshape(1024, 1024)
        w_out = w_out_s[...].reshape(512, 1024)
        x = x_s[...]
        gate_up = dot_f32(x, w_in, CONTRACT_PLAIN)
        gate_part, up_part = gate_up[:, :FF], gate_up[:, FF:]
        sigmoid = jax.nn.sigmoid(gate_part)
        hidden = (gate_part * sigmoid * up_part).astype(BF16)
        produced = dot_f32(hidden, w_out, CONTRACT_PLAIN).astype(BF16).astype(F32)
        slot_gate = gate_s[...]
        scaled = g_s[...]
        slot_grad = (slot_gate * scaled).astype(BF16)
        dot_s[...] = jnp.sum(produced * scaled, axis=1, keepdims=True)
        mix_s[...] = (slot_gate * produced).astype(BF16)
        hidden_grad = dot_f32(slot_grad, w_out, CONTRACT_LAST)
        gate_grad = hidden_grad * up_part * sigmoid * (1.0 + gate_part * (1.0 - sigmoid))
        up_grad = hidden_grad * gate_part * sigmoid
        gate_up_grad = jnp.concatenate([gate_grad.astype(BF16), up_grad.astype(BF16)], axis=1)
        back_s[...] = dot_f32(gate_up_grad, w_in, CONTRACT_LAST).astype(BF16)
        in_part = dot_f32(x, gate_up_grad, CONTRACT_FIRST)
        out_part = dot_f32(hidden, slot_grad, CONTRACT_FIRST)

        @pl.when(half == 0)
        def _():
            in_acc[...] = in_part
            out_acc[...] = out_part

        @pl.when(half == 1)
        def _():
            for d in range(4):
                wide, narrow = slice(d * 256, (d + 1) * 256), slice(d * 128, (d + 1) * 128)
                grad_s[d, 0:256, :] = (in_acc[wide, :] + in_part[wide, :]).astype(BF16)
                grad_s[d, 256:384, :] = (out_acc[narrow, :] + out_part[narrow, :]).astype(BF16)
            copy(grad_s, grad_ref, grad_sem.at[0]).start()

        for i in range(HALF):
            j = half * HALF + i
            at = slice(i * CAP, (i + 1) * CAP)
            mask = mask_of(i)
            pick = jnp.where(mask, 1.0, 0.0).astype(BF16)
            rows = dot_f32(pick, back_s[at, :], CONTRACT_FIRST)
            mixed = dot_f32(pick, mix_s[at, :], CONTRACT_FIRST)
            dots = jnp.sum(jnp.where(mask, dot_s[at, :], 0.0), axis=0, keepdims=True)
            high = dots.astype(BF16).astype(F32)
            low = dots - high
            wide = jnp.concatenate([high, high, low, low], axis=1)
            line = lax.broadcasted_iota(jnp.int32, (16, 1024), 0)
            lane = lax.broadcasted_iota(jnp.int32, (16, 1024), 1) // 256
            here = (line == number % 16) & (lane % 2 == number // 16)
            side = jnp.where(here, jnp.broadcast_to(wide, (16, 1024)), 0.0)
            if not first_part:
                copy(row_s.at[j], row_s.at[j], row_sem.at[j]).wait()
                copy(moe_s.at[j], moe_s.at[j], moe_sem.at[j]).wait()
                rows = rows + row_s[j, 0:256, :].astype(F32)
                mixed = mixed + moe_s[j].astype(F32)
                side = side + row_s[j, 256:SUM_ROWS, :].astype(F32)
            row_s[j, 0:256, :] = rows.astype(BF16)
            row_s[j, 256:SUM_ROWS, :] = side.astype(BF16)
            moe_s[j] = mixed.astype(BF16)
            for part in range(2):

                @pl.when(half == part)
                def _():
                    k = part * HALF + i
                    copy(row_s.at[k], row_outs[k], row_out_sem.at[k]).start()
                    copy(moe_s.at[k], moe_outs[k], moe_out_sem.at[k]).start()

        return 0

    lax.fori_loop(0, 2, half_step, 0)
    copy(grad_s, grad_ref, grad_sem.at[0]).wait()
    for j in range(BLOCKS):
        copy(row_s.at[j], row_outs[j], row_out_sem.at[j]).wait()
        copy(moe_s.at[j], moe_outs[j], moe_out_sem.at[j]).wait()


def expert_call(number, tokens, grads, weights, before=None):
    operands = list(tokens) + list(grads) + list(weights) + ([] if before is None else list(before))
    block = lambda rows: jax.ShapeDtypeStruct((rows, 1024), BF16)
    outs = [block(SUM_ROWS)] * BLOCKS + [block(256)] * BLOCKS + [jax.ShapeDtypeStruct((4, 384, 1024), BF16)]
    anywhere = pl.BlockSpec(memory_space=pl.ANY)
    blocks = lambda rows: pltpu.VMEM((BLOCKS, rows, 1024), BF16)
    column, wide = pltpu.VMEM((ROWS, 1), F32), pltpu.VMEM((ROWS, 1024), BF16)
    sems = [pltpu.SemaphoreType.DMA((count,)) for count in (8, 8, 2, 8, 8, 8, 8, 1)]
    results = pl.pallas_call(
        functools.partial(expert_body, before is None, len(weights) == 1),
        out_shape=outs,
        in_specs=[pl.BlockSpec(memory_space=pltpu.SMEM)] + [anywhere] * len(operands),
        out_specs=[anywhere] * len(outs),
        scratch_shapes=[
            blocks(PAY_ROWS), blocks(256), pltpu.VMEM((4, 256, 1024), BF16), pltpu.VMEM((4, 128, 1024), BF16),
            blocks(SUM_ROWS), blocks(256),
            pltpu.VMEM((4, 384, 1024), BF16), wide, pltpu.VMEM((ROWS, 1024), F32), column,
            pltpu.VMEM((HALF, 8, 256), F32), wide, wide, column,
            pltpu.VMEM((1024, 1024), F32), pltpu.VMEM((512, 1024), F32),
        ] + sems,
        compiler_params=pltpu.CompilerParams(vmem_limit_bytes=60 * 1024 * 1024),
        cost_estimate=pl.CostEstimate(
            flops=1000, bytes_accessed=1000, transcendentals=0
        ),
        name="expert",
    )(number, *operands)
    return results[: 2 * BLOCKS], results[2 * BLOCKS]


LANES = 128
GAIN_ATTN = 32
GAIN_FFN = 33
SEQUENCE = 256


def group_of(e, r):
    return pl.ds(pl.multiple_of((e ^ r) * LANES, LANES), LANES)


def turn_halves(value):
    lane = lax.broadcasted_iota(jnp.int32, value.shape, 1) % HEAD_SIZE
    width = value.shape[1]
    return jnp.where(
        lane < HEAD_SIZE // 2,
        -pltpu.roll(value, width - HEAD_SIZE // 2, 1),
        pltpu.roll(value, HEAD_SIZE // 2, 1),
    )


def wide_table(table, width):
    return jnp.concatenate([table] * (width // LANES), axis=1)


def inverse_rms(value):
    return lax.rsqrt(jnp.mean(value * value, axis=1, keepdims=True) + norm_eps)


def attention_probs(queries, keys, allowed):
    scores = jnp.where(allowed, dot_f32(queries, keys, CONTRACT_LAST) * attn_scale, -1e30)
    exps = jnp.exp(scores - jnp.max(scores, axis=1, keepdims=True))
    return exps / jnp.sum(exps, axis=1, keepdims=True)


def allowed_of(column_ref, row_ref):
    shape = (2 * SEQUENCE, SEQUENCE)
    query = lax.broadcasted_iota(jnp.int32, shape, 0) % SEQUENCE
    key = lax.broadcasted_iota(jnp.int32, shape, 1)
    column = column_ref[...]
    same = jnp.concatenate([column, column], axis=0) == row_ref[...]
    return (key <= query) & same


def heads_of(block, first, count):
    return jnp.concatenate(
        [block[:, HEAD_SIZE * (first + i) : HEAD_SIZE * (first + i + 1)] for i in range(count)], axis=0
    )


def stacked(refs, a, b):
    return jnp.concatenate([ref[:, a:b] for ref in refs], axis=0)


def gain_row(refs, index):
    return stacked(refs, 1024, 1152).astype(F32).T[index : index + 1, :]


def attend_body(e_ref, x_ref, column_ref, row_ref, cos_ref, sin_ref, *refs):
    lefts, rights = (refs[0:4], refs[4:8]), (refs[8:12], refs[12:16])
    normed_ref, q_ref, k_ref, v_ref, mixed_ref, small_ref = refs[16:]
    e = e_ref[0]
    resid = embed_scale * x_ref[...].astype(F32)
    inverse = inverse_rms(resid)
    for part in range(2):
        gain = gain_row(lefts[part], GAIN_ATTN)
        for q in range(4):
            group = group_of(e, 2 * q + part)
            block = embed_scale * x_ref[:, group].astype(F32)
            scaled = block * inverse * gain[:, LANES * q : LANES * (q + 1)]
            at = 512 * part + LANES * q
            normed_ref[:, at : at + LANES] = scaled.astype(BF16)
            small_ref[group, :] = lefts[part][q][:, 1024:1152]
    own = normed_ref[:, :512]
    far = normed_ref[:, 512:]
    project = lambda sides, a, b: dot_f32(own, stacked(sides[0], a, b), CONTRACT_PLAIN) + dot_f32(
        far, stacked(sides[1], a, b), CONTRACT_PLAIN
    )
    rotate = lambda u: u * wide_table(cos_ref[...], u.shape[1]) + turn_halves(u) * wide_table(
        sin_ref[...], u.shape[1]
    )
    q_ref[...] = rotate(project(lefts, 0, 1024)).astype(BF16)
    k_ref[...] = rotate(project(rights, 0, 512)).astype(BF16)
    v_ref[...] = project(rights, 512, 1024).astype(BF16)
    allowed = allowed_of(column_ref, row_ref)

    def pair(step, _):
        wide = pl.ds(pl.multiple_of(step * 256, 256), 256)
        narrow = pl.ds(pl.multiple_of(step * LANES, LANES), LANES)
        q_block, k_block, v_block = q_ref[:, wide], k_ref[:, narrow], v_ref[:, narrow]
        outs = []
        for i in range(2):
            probs = attention_probs(heads_of(q_block, 2 * i, 2), heads_of(k_block, i, 1), allowed)
            rows = dot_f32(probs.astype(BF16), heads_of(v_block, i, 1), CONTRACT_PLAIN)
            outs += [rows[:SEQUENCE], rows[SEQUENCE:]]
        mixed_ref[:, wide] = jnp.concatenate(outs, axis=1).astype(BF16)
        return 0

    lax.fori_loop(0, 4, pair, 0)


def route_body(e_ref, x_ref, mixed_ref, small_ref, code_ref, *refs):
    w_refs, (pay_ref, gates_ref, middle_ref) = (refs[0:4], refs[4:8]), refs[8:]
    e = e_ref[0]
    total = jnp.zeros((SEQUENCE, 1024), F32)
    for part in range(2):
        features = jnp.concatenate([mixed_ref[:, group_of(e, 2 * q + part)] for q in range(4)], axis=1)
        total = total + dot_f32(features, stacked(w_refs[part], 0, 1024), CONTRACT_PLAIN)
    middle = embed_scale * x_ref[...].astype(F32) + resid_scale * total
    middle_ref[...] = middle
    gain = small_ref[...].astype(F32).T[GAIN_FFN : GAIN_FFN + 1, :]
    normed2 = (middle * inverse_rms(middle) * gain).astype(BF16)
    pay_ref[0:256, :] = normed2
    logits = dot_f32(normed2, small_ref[...], CONTRACT_PLAIN)
    code = code_ref[...]
    member = code >= 0.0
    masked = jnp.where(member, logits, -1e30)
    raised = jnp.where(member, jnp.exp(masked - jnp.max(masked, axis=1, keepdims=True)), 0.0)
    gates = raised / jnp.sum(raised, axis=1, keepdims=True)
    gates_ref[...] = gates
    rows = lambda value: value.T[:EXPERTS, :]
    turned = rows(gates)
    high = turned.astype(BF16).astype(F32)
    middle_part = (turned - high).astype(BF16).astype(F32)
    low = turned - high - middle_part
    pay_ref[256:288, :] = jnp.concatenate([rows(code), high, middle_part, low], axis=1).astype(BF16)


def turn_body(e_ref, sum_ref, mine_ref, other_ref, add_ref, grad_ref, middle_ref, gates_ref, small_ref, normed2_ref, mixed_ref,
              *refs):
    w_refs, (own_ref, far_ref, mixed_grad_ref, middle_grad_ref, side_ref) = (refs[0:4], refs[4:8]), refs[8:]
    e = e_ref[0]
    addends = (sum_ref, mine_ref, other_ref, add_ref)
    upstream = sum(ref[0:256, :].astype(F32) for ref in addends)
    table = sum(ref[256:272, :].astype(F32) for ref in addends)
    dots = jnp.concatenate([table[:, :256], table[:, 256:512]], axis=0) + jnp.concatenate(
        [table[:, 512:768], table[:, 768:]], axis=0
    )
    dots = jnp.concatenate([dots, jnp.zeros((LANES - EXPERTS, SEQUENCE), F32)], axis=0).T
    gates = gates_ref[...]
    logit_grads = (gates * (dots - jnp.sum(gates * dots, axis=1, keepdims=True))).astype(BF16)
    small = small_ref[...]
    upstream = upstream + dot_f32(logit_grads, small, CONTRACT_LAST)
    middle = middle_ref[...]
    inverse = inverse_rms(middle)
    unit = middle * inverse
    gain = small.astype(F32).T[GAIN_FFN : GAIN_FFN + 1, :]
    gain_grad = jnp.sum(upstream * unit, axis=0, keepdims=True)
    scaled = upstream * gain
    middle_grad = grad_ref[...].astype(F32) + inverse * (
        scaled - unit * jnp.mean(scaled * unit, axis=1, keepdims=True)
    )
    middle_grad_ref[...] = middle_grad
    attn_grad = (resid_scale * middle_grad).astype(BF16)
    line = lax.broadcasted_iota(jnp.int32, (LANES, 1024), 0)
    side_ref[...] = dot_f32(normed2_ref[0:256, :], logit_grads, CONTRACT_FIRST) + jnp.where(
        line == GAIN_FFN, gain_grad, 0.0
    ).T
    for part, out_ref in ((0, own_ref), (1, far_ref)):
        features = jnp.concatenate([mixed_ref[:, group_of(e, 2 * q + part)] for q in range(4)], axis=1)
        out_ref[:, :1024] = dot_f32(features, attn_grad, CONTRACT_FIRST).astype(BF16)
        back = dot_f32(attn_grad, stacked(w_refs[part], 0, 1024), CONTRACT_LAST).astype(BF16)
        for q in range(4):
            mixed_grad_ref[:, group_of(e, 2 * q + part)] = back[:, LANES * q : LANES * (q + 1)]
            at = slice(LANES * q, LANES * (q + 1))
            out_ref[at, 1024:] = side_ref[group_of(e, 2 * q + part), :].astype(BF16)


def attend_back_body(e_ref, x_ref, column_ref, row_ref, cos_ref, sin_ref, q_ref, k_ref, v_ref, grad_ref,
                     normed_ref, middle_grad_ref, *refs):
    lefts, rights = (refs[0:4], refs[4:8]), (refs[8:12], refs[12:16])
    left_refs, right_refs = refs[16:18], refs[18:20]
    embed_ref, raw_ref, scaled_ref = refs[20:]
    e = e_ref[0]
    allowed = allowed_of(column_ref, row_ref)
    unrotate = lambda u: (
        u * wide_table(cos_ref[...], u.shape[1]) - turn_halves(u) * wide_table(sin_ref[...], u.shape[1])
    ).astype(BF16)

    def pair(step, _):
        wide = pl.ds(pl.multiple_of(step * 256, 256), 256)
        narrow = lambda base: pl.ds(pl.multiple_of(base + step * LANES, LANES), LANES)
        q_block, d_block = q_ref[:, wide], grad_ref[:, wide]
        k_block, v_block = k_ref[:, narrow(0)], v_ref[:, narrow(0)]
        q_outs, k_outs, v_outs = [], [], []
        for i in range(2):
            queries, keys = heads_of(q_block, 2 * i, 2), heads_of(k_block, i, 1)
            upstream = heads_of(d_block, 2 * i, 2)
            probs = attention_probs(queries, keys, allowed)
            prob_grads = dot_f32(upstream, heads_of(v_block, i, 1), CONTRACT_LAST)
            centre = jnp.sum(probs * prob_grads, axis=1, keepdims=True)
            score_grads = (probs * (prob_grads - centre)).astype(BF16)
            rows = dot_f32(score_grads, keys, CONTRACT_PLAIN) * attn_scale
            q_outs += [rows[:SEQUENCE], rows[SEQUENCE:]]
            k_outs.append(dot_f32(score_grads, queries, CONTRACT_FIRST) * attn_scale)
            v_outs.append(dot_f32(probs.astype(BF16), upstream, CONTRACT_FIRST))
        raw_ref[:, wide] = unrotate(jnp.concatenate(q_outs, axis=1))
        raw_ref[:, narrow(1024)] = unrotate(jnp.concatenate(k_outs, axis=1))
        raw_ref[:, narrow(1536)] = jnp.concatenate(v_outs, axis=1).astype(BF16)
        return 0

    lax.fori_loop(0, 4, pair, 0)
    resid = embed_scale * x_ref[...].astype(F32)
    inverse = inverse_rms(resid)
    for part in range(2):
        half = normed_ref[:, 512 * part : 512 * part + 512]
        for c in range(2):
            at = slice(512 * c, 512 * c + 512)
            left_refs[part][:, at] = dot_f32(half, raw_ref[:, at], CONTRACT_FIRST).astype(BF16)
            right_refs[part][:, at] = dot_f32(
                half, raw_ref[:, 1024 + 512 * c : 1536 + 512 * c], CONTRACT_FIRST
            ).astype(BF16)
        back = dot_f32(raw_ref[:, :1024], stacked(lefts[part], 0, 1024), CONTRACT_LAST) + dot_f32(
            raw_ref[:, 1024:], stacked(rights[part], 0, 1024), CONTRACT_LAST
        )
        gain = gain_row(lefts[part], GAIN_ATTN)
        gain_grads = []
        for q in range(4):
            at = slice(LANES * q, LANES * (q + 1))
            group = group_of(e, 2 * q + part)
            unit = embed_scale * x_ref[:, group].astype(F32) * inverse
            gain_grads.append(jnp.sum(back[:, at] * unit, axis=0, keepdims=True))
            scaled_ref[:, group] = back[:, at] * gain[:, at]
        line = lax.broadcasted_iota(jnp.int32, (LANES, 512), 0)
        side = jnp.where(line == GAIN_ATTN, jnp.concatenate(gain_grads, axis=1), 0.0).T
        left_refs[part][:, 1024:] = side.astype(BF16)
    unit = resid * inverse
    scaled = scaled_ref[...]
    resid_grad = middle_grad_ref[...] + inverse * (
        scaled - unit * jnp.mean(scaled * unit, axis=1, keepdims=True)
    )
    embed_ref[...] = (embed_scale * resid_grad).astype(BF16)


def local_kernel(body, name, outs, scratch, number, *operands):
    vmem = pl.BlockSpec(memory_space=pltpu.VMEM)
    return pl.pallas_call(
        body,
        out_shape=[jax.ShapeDtypeStruct(shape, dtype) for shape, dtype in outs],
        in_specs=[pl.BlockSpec(memory_space=pltpu.SMEM)] + [vmem] * len(operands),
        out_specs=[vmem] * len(outs),
        scratch_shapes=[pltpu.VMEM(shape, dtype) for shape, dtype in scratch],
        compiler_params=pltpu.CompilerParams(vmem_limit_bytes=56 * 1024 * 1024),
        cost_estimate=pl.CostEstimate(flops=1000, bytes_accessed=1000, transcendentals=0),
        name=name,
    )(number, *operands)


def together(*values):
    return lax.optimization_barrier(values)


def core_sum(own, far):
    return (own.astype(F32) + over_expert(far, 1).astype(F32)).astype(BF16)


def xor_order(pieces, at):
    stacked = jnp.stack(pieces)
    return jnp.concatenate(
        [lax.dynamic_index_in_dim(stacked, at ^ i, 0, keepdims=False) for i in range(len(pieces))]
    )


def exchange(slices):
    return lax.all_to_all(slices, "shard", split_axis=0, concat_axis=0, tiled=True)


def expert_slices(weights, part):
    return jnp.stack([weights[OWN * (d % PAIR) + part] for d in range(4)])


def over_x(value):
    return over_expert(value, 2)


def over_y(value):
    return over_expert(value, 4)


def spread(value, first, second):
    near = {first: first(value), second: second(value)}
    return [value, near[over_x], near[over_y], second(near[first])]


def bf_sum(*values):
    return sum(value.astype(F32) for value in values).astype(BF16)


def pack_body(query_ref, key_ref, value_ref, router_ref, attn_ref, ffn_ref, out_ref, pack_ref):
    pack_ref[:, 0:1024] = query_ref[...].astype(BF16)
    row = lax.broadcasted_iota(jnp.int32, (32, 32), 0)
    diagonal = row == lax.broadcasted_iota(jnp.int32, (32, 32), 1)
    upright = lambda ref: jnp.sum(jnp.where(diagonal, ref[...], 0.0), axis=1, keepdims=True)
    zeros = jnp.zeros((32, LANES - EXPERTS - 2), F32)
    small = jnp.concatenate([router_ref[...], upright(attn_ref), upright(ffn_ref), zeros], axis=1)
    pack_ref[:, 1024:1152] = small.astype(BF16)
    pack_ref[:, 1152:1664] = key_ref[...].astype(BF16)
    pack_ref[:, 1664:2176] = value_ref[...].astype(BF16)
    pack_ref[:, 2176:] = out_ref[...].astype(BF16)


def plane_body(z_ref, *refs):
    z = z_ref[0]
    for group, (a, b) in enumerate(((0, 1152), (1152, 2176), (2176, 3328))):
        mine, one, other = refs[3 * group : 3 * group + 3]
        for k in range(4):
            rows = pl.ds(pl.multiple_of((z ^ k) * 32, 32), 32)
            total = mine[rows, :].astype(F32) + one[rows, :].astype(F32) + other[rows, :].astype(F32)
            refs[9 + k][:, a:b] = total.astype(BF16)


def settle_body(z_ref, *refs):
    sources, outs = refs[:4], refs[4:]
    total = lambda a, b: sum(ref[:, a:b].astype(F32) for ref in sources)
    bounds = ((0, 1024), (1152, 1664), (1664, 2176), (2176, 3200))
    for out_ref, (a, b) in zip(outs, bounds):
        out_ref[...] = total(a, b)
    row = lax.broadcasted_iota(jnp.int32, (32, 32), 0)
    diagonal = row == lax.broadcasted_iota(jnp.int32, (32, 32), 1)
    flat = lambda column: jnp.sum(jnp.where(diagonal, column, 0.0), axis=0, keepdims=True)
    late, early = total(1024, 1152), total(3200, 3328)
    outs[4][...] = early[:, :EXPERTS]
    outs[5][...] = flat(late[:, GAIN_ATTN : GAIN_ATTN + 1])
    outs[6][...] = flat(early[:, GAIN_FFN : GAIN_FFN + 1])


def owner_body(first_part, one_ref, two_ref, *refs):
    in_ref, out_ref = refs if first_part else refs[2:]
    total = one_ref[...].astype(F32) + two_ref[...].astype(F32)
    in_ref[...] = total[:, :256]
    out_ref[...] = total[:, 256:]


def owner_sum(part, slices, before=()):
    block = lambda rows, at: pl.BlockSpec((1, rows, 1024), lambda d: (at(d), 0, 0))
    place = lambda d: 2 * d + part
    return pl.pallas_call(
        functools.partial(owner_body, not before),
        out_shape=[jax.ShapeDtypeStruct((4, rows, 1024), F32) for rows in (256, 128)],
        grid=(2,),
        in_specs=[block(384, lambda d: d), block(384, lambda d: d + 2)]
        + [pl.BlockSpec(memory_space=pl.ANY)] * len(before),
        out_specs=[block(256, place), block(128, place)],
        input_output_aliases={2: 0, 3: 1} if before else {},
        name="owner_sum",
    )(slices, slices, *before)


def plane_fold(total, first, second):
    part = lambda q: total[128 * q : 128 * (q + 1)]
    one, two = (1, 2) if first is over_x else (2, 1)
    passing, mine = first(part(3)), first(part(one))
    return [part(0), mine, second(bf_sum(part(two), passing))]


def pack_call(*operands):
    return pl.pallas_call(
        pack_body,
        out_shape=jax.ShapeDtypeStruct((32, 3200), BF16),
        in_specs=[pl.BlockSpec(memory_space=pltpu.VMEM)] * len(operands),
        out_specs=pl.BlockSpec(memory_space=pltpu.VMEM),
        name="pack",
    )(*operands)


def per_device_fast(
    embedded,
    document_numbers,
    expert_ids,
    attn_gain,
    ffn_gain,
    w_query,
    key_projection,
    value_projection,
    w_out,
    w_router,
    expert_in,
    expert_out,
    cotangent,
):
    e = lax.axis_index("expert")
    z = lax.axis_index("shard")
    place = e.reshape(1)
    pack = pack_call(
        w_query, key_projection, value_projection, w_router, attn_gain[None, :], ffn_gain[None, :], w_out
    )
    pack, grad_early = together(pack, cotangent)
    plane = xor_order([pack] + [over_shard(pack, k) for k in (1, 2, 3)], z)
    out_pair = over_shard(grad_early, 1)
    out_x, out_y = over_x(grad_early), over_y(grad_early)
    slices = [
        jnp.concatenate([expert_slices(w, part) for w in (expert_in, expert_out)], axis=1)
        for part in range(OWN)
    ]
    plane, out_x, out_y, slices[0] = together(plane, out_x, out_y, slices[0])
    left = spread(plane[:, :1152], over_x, over_y)
    right = spread(plane[:, 1152:2176], over_y, over_x)
    slices[0], out_pair, left[1], right[2] = together(slices[0], out_pair, left[1], right[2])
    weights0 = exchange(slices[0])
    swap = lambda values: [over_expert(value, 1) for value in values]
    left_far, right_far = swap(left), swap(right)
    left[3], right[3], plane, out_pair, out_x = together(left[3], right[3], plane, out_pair, out_x)
    out_w = [plane[:, 2176:]] + [over_expert(plane[:, 2176:], bits) for bits in (2, 4, 6)]
    out_blocks = [cotangent, out_x, out_y, over_y(out_x), out_pair, over_x(out_pair), over_y(out_pair)]

    segments = document_numbers[0]
    column, row = segments[:, None], segments[None, :]
    cosine, sine = (jnp.concatenate([table] * 4, axis=1) for table in rope_tables(segments))
    lanes = jnp.arange(LANES, dtype=jnp.int32)
    member = jnp.any(expert_ids[:, :, None] == lanes, axis=1)
    index = jnp.arange(SEQUENCE, dtype=jnp.int32)
    below = (index[None, :] < index[:, None]).astype(BF16)
    rank = jnp.dot(below, member.astype(BF16), preferred_element_type=F32)
    code = jnp.where(member, rank, -1.0)

    wide, half = (SEQUENCE, 1024), (SEQUENCE, 512)
    weights = left + left_far + right + right_far
    normed, queries, keys, values, mixed, small_all = local_kernel(
        attend_body, "attend",
        [(wide, BF16), (wide, BF16), (half, BF16), (half, BF16), (wide, BF16), ((1024, LANES), BF16)], [],
        place, embedded, column, row, cosine, sine, *weights,
    )
    *out_w, mixed = together(*out_w, mixed)
    out_w = out_w + swap(out_w)
    payload, gates, middle = local_kernel(
        route_body, "route", [((288, 1024), BF16), ((SEQUENCE, LANES), F32), (wide, F32)], [],
        place, embedded, mixed, small_all, code, *out_w,
    )
    pay_pair = over_shard(payload, 1)
    pay_x, pay_y = over_x(payload), over_y(payload)
    pay_x, pay_y, pay_pair, *out_blocks = together(pay_x, pay_y, pay_pair, *out_blocks)
    slices[1], weights0, pay_pair = together(slices[1], weights0, pay_pair)
    weights1 = [exchange(slices[1])]
    out_blocks.append(over_x(out_blocks[6]))
    tok_own = [payload, pay_x, pay_y, over_y(pay_x)]
    tok_pair = [pay_pair, over_x(pay_pair), over_y(pay_pair)]
    tok_pair[2], out_blocks[7] = together(tok_pair[2], out_blocks[7])
    tok_pair.append(over_x(tok_pair[2]))
    weights0 = [weights0]
    weights0_far = swap(weights0)
    tokens = tok_own + tok_pair
    first = (e * 4 + z % PAIR * OWN).reshape(1)
    first_far = ((e ^ 1) * 4 + z % PAIR * OWN).reshape(1)
    sums, grad_b = expert_call(first_far, tokens, out_blocks, weights0_far)
    sums, grad_a = expert_call(first, tokens, out_blocks, weights0, sums)
    expert_grad0 = core_sum(grad_a, grad_b)
    expert_grad0, *weights1 = together(expert_grad0, *weights1)
    slices0 = exchange(expert_grad0)
    weights1_far = swap(weights1)
    sums, grad_d = expert_call(first_far + 1, tokens, out_blocks, weights1_far, sums)
    sums, grad_c = expert_call(first + 1, tokens, out_blocks, weights1, sums)
    rows, moes = sums[:BLOCKS], sums[BLOCKS:]
    expert_grad1 = core_sum(grad_c, grad_d)
    own, pair = rows[:4], rows[4:]
    pair_pass, own_pass = over_x(pair[3]), over_y(own[3])
    pair_mine = over_x(pair[1])
    pair_pass, expert_grad1, slices0 = together(pair_pass, expert_grad1, slices0)
    pair_other = over_y(bf_sum(pair[2], pair_pass))
    mine, pair_pass = together(own[2], pair_pass)
    own_mine = over_y(mine)
    own_other = over_x(bf_sum(own[1], own_pass))
    row_pair = bf_sum(pair[0], pair_mine, pair_other)
    returned = over_shard(row_pair, 1)
    row_pair, *moes = together(row_pair, *moes)
    moe_pass, moe_own_pass = over_x(moes[7]), over_y(moes[3])
    moe_mine, moe_own_mine = over_x(moes[5]), over_y(moes[2])
    owned = owner_sum(0, slices0)
    own_other, *owned = together(own_other, *owned)
    own_other, expert_grad1 = together(own_other, expert_grad1)
    slices1 = exchange(expert_grad1)
    early_own, early_far, mixed_grad, middle_grad = local_kernel(
        turn_body, "turn", [((512, 1152), BF16), ((512, 1152), BF16), (wide, BF16), (wide, F32)],
        [((1024, LANES), F32)], place, own[0], own_mine, own_other, returned, cotangent, middle, gates,
        small_all, payload, mixed, *out_w,
    )
    moe_rest, moe_own_rest = over_y(bf_sum(moes[6], moe_pass)), over_x(bf_sum(moes[1], moe_own_pass))
    left_own, left_far, right_own, right_far, grad_embedded = local_kernel(
        attend_back_body, "attend_back", [((512, 1152), BF16)] * 2 + [((512, 1024), BF16)] * 2 + [(wide, BF16)],
        [((SEQUENCE, 2048), BF16), (wide, F32)], place, embedded, column, row, cosine, sine,
        queries, keys, values, mixed_grad, normed, middle_grad, *weights,
    )
    left_far, right_far, moe_rest, moe_own_rest, moe_mine, moe_own_mine = together(
        left_far, right_far, moe_rest, moe_own_rest, moe_mine, moe_own_mine
    )
    moe_pair = bf_sum(moes[4], moe_mine, moe_rest)
    moe_own = bf_sum(moes[0], moe_own_mine, moe_own_rest)
    moe_other = over_shard(moe_pair, 1)
    addends = plane_fold(core_sum(left_own, left_far), over_x, over_y)
    addends += plane_fold(core_sum(right_own, right_far), over_y, over_x)
    addends += plane_fold(core_sum(early_own, early_far), over_y, over_x)
    planes = local_kernel(plane_body, "plane", [((32, 3328), BF16)] * 4, [], z.reshape(1), *addends)
    planes = list(planes)
    planes[3], slices1 = together(planes[3], slices1)
    planes = [planes[0]] + [over_shard(planes[k], k) for k in (1, 2, 3)]
    shapes = [(32, 1024), (32, 512), (32, 512), (32, 1024), (32, EXPERTS), (1, 32), (1, 32)]
    late_query, late_key, late_value, early_out, router, gain_attn, gain_ffn = local_kernel(
        settle_body, "settle", [(shape, F32) for shape in shapes], [], z.reshape(1), *planes
    )
    grad_expert_in, grad_expert_out = owner_sum(1, slices1, owned)
    moe = moe_own.astype(F32) + moe_other.astype(F32)
    output = (middle + resid_scale * moe).astype(BF16)
    return (
        output,
        grad_embedded,
        gain_attn[0],
        gain_ffn[0],
        late_query,
        late_key,
        late_value,
        early_out,
        router,
        grad_expert_in,
        grad_expert_out,
    )


def solution(mesh):
    owners, shards = mesh.shape["expert"], mesh.shape["shard"]
    fast = owners == 8 and shards == 4
    both = ("expert", "shard")
    rows = P(both, None)
    weights = P("expert", "shard", None)
    return jax.shard_map(
        per_device_fast if fast else per_device_general,
        mesh=mesh,
        in_specs=(rows,) * 3 + (P(both),) * 2 + (rows,) * 5 + (weights,) * 2 + (rows,),
        out_specs=(rows,) * 2 + (P(both),) * 2 + (rows,) * 5 + (weights,) * 2,
        check_vma=False,
    )
```

```python
import functools

import jax
import jax.numpy as jnp
from jax import lax
from jax.experimental import pallas as pl
from jax.experimental.pallas import tpu as pltpu
from jax.sharding import PartitionSpec as P

MODEL_WIDTH = 1024
QUERY_HEADS = 16
KEY_VALUE_HEADS = 8
HEAD_SIZE = 64
FF = 512
EXPERTS = 32
TOPK = 8
CAP = 128


embed_scale = 12.0
attn_scale = 0.015625
resid_scale = 0.22
norm_eps = 1e-06
rope_base = 10000.0


def rope_tables(segments):
    sequence_length = segments.shape[0]
    key_index = jnp.arange(sequence_length, dtype=jnp.int32)
    change = jnp.concatenate([jnp.ones((1,), jnp.bool_), segments[1:] != segments[:-1]])
    begins = lax.cummax(jnp.where(change, key_index, 0), axis=0)
    places = (key_index - begins).astype(jnp.float32)
    freqs = rope_base ** (-2.0 * jnp.arange(HEAD_SIZE // 2, dtype=jnp.float32) / HEAD_SIZE)
    angles = places[:, None] * freqs[None, :]
    return (jnp.cos(angles), jnp.sin(angles))


def apply_rotation(value_heads, cosine_table, sine_table):
    halfway = value_heads.shape[-1] // 2
    first_half = value_heads[..., :halfway]
    second_half = value_heads[..., halfway:]
    cos_part = cosine_table[:, None, :]
    sin_part = sine_table[:, None, :]
    return jnp.concatenate(
        [
            first_half * cos_part - second_half * sin_part,
            second_half * cos_part + first_half * sin_part,
        ],
        axis=-1,
    )


def reverse_rotation(grads, cosine_table, sine_table):
    halfway = grads.shape[-1] // 2
    first_half = grads[..., :halfway]
    second_half = grads[..., halfway:]
    cos_part = cosine_table[:, None, :]
    sin_part = sine_table[:, None, :]
    return jnp.concatenate(
        [
            first_half * cos_part + second_half * sin_part,
            second_half * cos_part - first_half * sin_part,
        ],
        axis=-1,
    )


def norm_forward(value_heads):
    inverse = lax.rsqrt(jnp.mean(value_heads * value_heads, axis=1, keepdims=True) + norm_eps)
    return (value_heads * inverse, inverse)


def norm_backward(upstream, unit_values, inverse, gain):
    scaled = upstream * gain
    grad_values = inverse * (
        scaled - unit_values * jnp.mean(scaled * unit_values, axis=1, keepdims=True)
    )
    return (grad_values, jnp.sum(upstream * unit_values, axis=0))


def slot_tables(expert_ids):
    flat_ids = expert_ids.reshape(-1)
    count_all = flat_ids.shape[0]
    matches = (flat_ids[:, None] == jnp.arange(EXPERTS, dtype=jnp.int32)[None, :]).astype(jnp.int32)
    before = jnp.cumsum(matches, axis=0) - 1
    ranking = jnp.sum(before * matches, axis=1)
    target = flat_ids * CAP + ranking
    source = (
        jnp.zeros((EXPERTS * CAP,), jnp.int32)
        .at[target]
        .set(jnp.arange(count_all, dtype=jnp.int32))
    )
    filled = (
        jnp.zeros((EXPERTS * CAP,), jnp.int32).at[target].set(jnp.ones((count_all,), jnp.int32))
    )
    return (target, source, filled)


def silu_parts(gate_up):
    gate_part = gate_up[..., :FF]
    up_part = gate_up[..., FF:]
    sigmoid_gate = jax.nn.sigmoid(gate_part)
    hidden = (gate_part * sigmoid_gate * up_part).astype(jnp.bfloat16)
    return (gate_part, up_part, sigmoid_gate, hidden)


def per_device_general(
    embedded,
    document_numbers,
    expert_ids,
    attn_gain,
    ffn_gain,
    w_query,
    key_projection,
    value_projection,
    w_out,
    w_router,
    expert_in,
    expert_out,
    cotangent,
):
    mixer = (
        lax.all_gather(attn_gain.astype(jnp.bfloat16), ("expert", "shard"), axis=0, tiled=True),
        lax.all_gather(ffn_gain.astype(jnp.bfloat16), ("expert", "shard"), axis=0, tiled=True),
        lax.all_gather(w_query.astype(jnp.bfloat16), ("expert", "shard"), axis=0, tiled=True),
        lax.all_gather(
            key_projection.astype(jnp.bfloat16), ("expert", "shard"), axis=0, tiled=True
        ),
        lax.all_gather(
            value_projection.astype(jnp.bfloat16), ("expert", "shard"), axis=0, tiled=True
        ),
        lax.all_gather(w_out.astype(jnp.bfloat16), ("expert", "shard"), axis=0, tiled=True),
        lax.all_gather(w_router.astype(jnp.bfloat16), ("expert", "shard"), axis=0, tiled=True),
    )
    gain_attn, gain_ffn, query_w, key_w, value_w, out_w, router_w = mixer
    full_in, full_out = (
        lax.all_gather(expert_in, "shard", axis=1, tiled=True),
        lax.all_gather(expert_out, "shard", axis=1, tiled=True),
    )
    sequence_length = embedded.shape[0]
    query_groups = QUERY_HEADS // KEY_VALUE_HEADS
    owners = lax.axis_size("expert")
    local_count = EXPERTS // owners
    received = owners * CAP
    resid = embed_scale * embedded.astype(jnp.float32)
    unit_attn, inverse_attn = norm_forward(resid)
    normed = (unit_attn * gain_attn.astype(jnp.float32)).astype(jnp.bfloat16)
    unrotated_query = jnp.dot(normed, query_w, preferred_element_type=jnp.float32)
    unrotated_key = jnp.dot(normed, key_w, preferred_element_type=jnp.float32)
    projected_value = jnp.dot(normed, value_w, preferred_element_type=jnp.float32)
    segments = document_numbers[0]
    cosine_table, sine_table = rope_tables(segments)
    query_heads = (
        apply_rotation(
            unrotated_query.reshape(sequence_length, QUERY_HEADS, HEAD_SIZE),
            cosine_table,
            sine_table,
        )
        .astype(jnp.bfloat16)
        .reshape(sequence_length, KEY_VALUE_HEADS, query_groups, HEAD_SIZE)
    )
    key_heads = apply_rotation(
        unrotated_key.reshape(sequence_length, KEY_VALUE_HEADS, HEAD_SIZE), cosine_table, sine_table
    ).astype(jnp.bfloat16)
    value_heads = projected_value.astype(jnp.bfloat16).reshape(
        sequence_length, KEY_VALUE_HEADS, HEAD_SIZE
    )
    block_rows = min(512, sequence_length)
    starts = jnp.arange(sequence_length // block_rows, dtype=jnp.int32) * block_rows
    key_index = jnp.arange(sequence_length, dtype=jnp.int32)

    def block_scores(first_row):
        row_index = first_row + jnp.arange(block_rows, dtype=jnp.int32)
        raw_scores = (
            jnp.einsum("qhgd,khd->hgqk", query_heads, key_heads, preferred_element_type=jnp.float32)
            * attn_scale
        )
        allowed = (key_index[None, :] <= row_index[:, None]) & (
            segments[None, :] == segments[:, None]
        )
        return (jnp.where(allowed, raw_scores, -1e30), query_heads)

    def attend_block(first_row):
        scores, query_rows = block_scores(first_row)
        row_max = jnp.max(scores, axis=-1, keepdims=True)
        exps = jnp.exp(scores - row_max)
        totals = jnp.sum(exps, axis=-1, keepdims=True)
        weights = (exps / totals).astype(jnp.bfloat16)
        mixed_rows = jnp.einsum(
            "hgqk,khd->qhgd", weights, value_heads, preferred_element_type=jnp.float32
        )
        return (mixed_rows.astype(jnp.bfloat16), (row_max + jnp.log(totals))[..., 0])

    mixed_blocks, log_totals = lax.map(attend_block, starts)
    mixed_heads_output = mixed_blocks.reshape(sequence_length, QUERY_HEADS * HEAD_SIZE)
    middle = resid + resid_scale * jnp.dot(
        mixed_heads_output, out_w, preferred_element_type=jnp.float32
    )
    unit_ffn, inverse_ffn = norm_forward(middle)
    normed2 = (unit_ffn * gain_ffn.astype(jnp.float32)).astype(jnp.bfloat16)
    logits = jnp.dot(normed2, router_w, preferred_element_type=jnp.float32)
    pick_table = expert_ids[:, :, None] == jnp.arange(EXPERTS, dtype=jnp.int32)[None, None, :]
    chosen = jnp.sum(jnp.where(pick_table, logits[:, None, :], 0.0), axis=2)
    exps_chosen = jnp.exp(chosen - jnp.max(chosen, axis=1, keepdims=True))
    gates = exps_chosen / jnp.sum(exps_chosen, axis=1, keepdims=True)
    target, source, filled = slot_tables(expert_ids)
    live_slots = filled[:, None] == 1
    zero_bf = jnp.zeros((), jnp.bfloat16)
    send_rows = jnp.where(live_slots, normed2[source // TOPK], zero_bf).reshape(
        owners, local_count, CAP, MODEL_WIDTH
    )
    arrived = lax.all_to_all(send_rows, "expert", split_axis=0, concat_axis=2, tiled=True).reshape(
        local_count, received, MODEL_WIDTH
    )
    gate_up = jnp.einsum("erd,edf->erf", arrived, full_in, preferred_element_type=jnp.float32)
    gate_part, up_part, sigmoid_gate, hidden = silu_parts(gate_up)
    produced = jnp.einsum(
        "erf,efd->erd", hidden, full_out, preferred_element_type=jnp.float32
    ).astype(jnp.bfloat16)
    returned = lax.all_to_all(
        produced.reshape(1, local_count, received, MODEL_WIDTH),
        "expert",
        split_axis=2,
        concat_axis=0,
        tiled=True,
    ).reshape(EXPERTS * CAP, MODEL_WIDTH)
    slot_values = returned[target].reshape(sequence_length, TOPK, MODEL_WIDTH)
    moe = jnp.einsum("tk,tkd->td", gates, slot_values.astype(jnp.float32))
    output = (middle + resid_scale * moe).astype(jnp.bfloat16)
    grad_output = cotangent.astype(jnp.float32)
    grad_mix = resid_scale * grad_output
    gate_grads = jnp.einsum("tkd,td->tk", slot_values.astype(jnp.float32), grad_mix)
    slot_grads = (
        (gates[:, :, None] * grad_mix[:, None, :])
        .astype(jnp.bfloat16)
        .reshape(sequence_length * TOPK, MODEL_WIDTH)
    )
    grad_send = jnp.where(live_slots, slot_grads[source], zero_bf).reshape(
        owners, local_count, CAP, MODEL_WIDTH
    )
    grad_arrived = lax.all_to_all(
        grad_send, "expert", split_axis=0, concat_axis=2, tiled=True
    ).reshape(local_count, received, MODEL_WIDTH)
    owner_rows = lax.all_to_all(
        send_rows, "expert", split_axis=0, concat_axis=2, tiled=True
    ).reshape(local_count, received, MODEL_WIDTH)
    owner_gate_up = jnp.einsum(
        "erd,edf->erf", owner_rows, full_in, preferred_element_type=jnp.float32
    )
    owner_gate, owner_up, owner_sigmoid, owner_hidden = silu_parts(owner_gate_up)
    hidden_grad = jnp.einsum(
        "erd,efd->erf", grad_arrived, full_out, preferred_element_type=jnp.float32
    )
    gate_grad_part = (
        hidden_grad * owner_up * owner_sigmoid * (1.0 + owner_gate * (1.0 - owner_sigmoid))
    )
    up_grad_part = hidden_grad * owner_gate * owner_sigmoid
    gate_up_grad = jnp.concatenate([gate_grad_part, up_grad_part], axis=-1).astype(jnp.bfloat16)
    grad_full_out = jnp.einsum(
        "erf,erd->efd", owner_hidden, grad_arrived, preferred_element_type=jnp.float32
    )
    grad_full_in = jnp.einsum(
        "erd,erf->edf", owner_rows, gate_up_grad, preferred_element_type=jnp.float32
    )
    row_grads = jnp.einsum(
        "erf,edf->erd", gate_up_grad, full_in, preferred_element_type=jnp.float32
    ).astype(jnp.bfloat16)
    grad_returned = lax.all_to_all(
        row_grads.reshape(1, local_count, received, MODEL_WIDTH),
        "expert",
        split_axis=2,
        concat_axis=0,
        tiled=True,
    ).reshape(EXPERTS * CAP, MODEL_WIDTH)
    grad_expert_in, grad_expert_out = (
        lax.psum_scatter(
            grad_full_in.astype(jnp.bfloat16), "shard", scatter_dimension=1, tiled=True
        ).astype(jnp.float32),
        lax.psum_scatter(
            grad_full_out.astype(jnp.bfloat16), "shard", scatter_dimension=1, tiled=True
        ).astype(jnp.float32),
    )
    mixer_back = (
        lax.all_gather(attn_gain.astype(jnp.bfloat16), ("expert", "shard"), axis=0, tiled=True),
        lax.all_gather(ffn_gain.astype(jnp.bfloat16), ("expert", "shard"), axis=0, tiled=True),
        lax.all_gather(w_query.astype(jnp.bfloat16), ("expert", "shard"), axis=0, tiled=True),
        lax.all_gather(
            key_projection.astype(jnp.bfloat16), ("expert", "shard"), axis=0, tiled=True
        ),
        lax.all_gather(
            value_projection.astype(jnp.bfloat16), ("expert", "shard"), axis=0, tiled=True
        ),
        lax.all_gather(w_out.astype(jnp.bfloat16), ("expert", "shard"), axis=0, tiled=True),
        lax.all_gather(w_router.astype(jnp.bfloat16), ("expert", "shard"), axis=0, tiled=True),
    )
    back_gain_attn, back_gain_ffn, back_query, back_key, back_value, back_out, back_router = (
        mixer_back
    )
    chosen_grad = gates * (gate_grads - jnp.sum(gates * gate_grads, axis=1, keepdims=True))
    logit_grads = jnp.sum(jnp.where(pick_table, chosen_grad[:, :, None], 0.0), axis=1).astype(
        jnp.bfloat16
    )
    grad_router_full = jnp.einsum(
        "td,te->de", normed2, logit_grads, preferred_element_type=jnp.float32
    )
    normed2_grad = jnp.sum(
        grad_returned[target].reshape(sequence_length, TOPK, MODEL_WIDTH), axis=1, dtype=jnp.float32
    )
    normed2_grad = normed2_grad + jnp.einsum(
        "te,de->td", logit_grads, back_router, preferred_element_type=jnp.float32
    )
    middle_norm_grad, grad_gain_ffn = norm_backward(
        normed2_grad, unit_ffn, inverse_ffn, back_gain_ffn.astype(jnp.float32)
    )
    middle_grad = grad_output + middle_norm_grad
    attn_grad = (resid_scale * middle_grad).astype(jnp.bfloat16)
    grad_out_full = jnp.einsum(
        "tf,td->fd", mixed_heads_output, attn_grad, preferred_element_type=jnp.float32
    )
    mixed_output_gradient = jnp.einsum(
        "td,fd->tf", attn_grad, back_out, preferred_element_type=jnp.float32
    ).astype(jnp.bfloat16)
    mixed_gradient_by_head = mixed_output_gradient.reshape(
        sequence_length, KEY_VALUE_HEADS, query_groups, HEAD_SIZE
    )

    def attend_back(carries, packed):
        key_acc, value_acc = carries
        first_row, log_rows = packed
        scores, query_rows = block_scores(first_row)
        probs = jnp.exp(scores - log_rows[..., None])
        prob_grads = jnp.einsum(
            "qhgd,khd->hgqk",
            mixed_gradient_by_head,
            value_heads,
            preferred_element_type=jnp.float32,
        )
        score_grads = (
            probs * (prob_grads - jnp.sum(probs * prob_grads, axis=-1, keepdims=True))
        ).astype(jnp.bfloat16)
        query_grads = (
            jnp.einsum("hgqk,khd->qhgd", score_grads, key_heads, preferred_element_type=jnp.float32)
            * attn_scale
        )
        key_acc = (
            key_acc
            + jnp.einsum(
                "hgqk,qhgd->khd", score_grads, query_rows, preferred_element_type=jnp.float32
            )
            * attn_scale
        )
        value_acc = value_acc + jnp.einsum(
            "hgqk,qhgd->khd",
            probs.astype(jnp.bfloat16),
            mixed_gradient_by_head,
            preferred_element_type=jnp.float32,
        )
        return ((key_acc, value_acc), query_grads)

    empty_head_rows = jnp.zeros((sequence_length, KEY_VALUE_HEADS, HEAD_SIZE), jnp.float32)
    (summed_key_gradient, summed_value_gradient), query_grad_blocks = lax.scan(
        attend_back, (empty_head_rows, empty_head_rows), (starts, log_totals)
    )
    query_raw_grad = (
        reverse_rotation(
            query_grad_blocks.reshape(sequence_length, QUERY_HEADS, HEAD_SIZE),
            cosine_table,
            sine_table,
        )
        .astype(jnp.bfloat16)
        .reshape(sequence_length, QUERY_HEADS * HEAD_SIZE)
    )
    key_raw_grad = (
        reverse_rotation(summed_key_gradient, cosine_table, sine_table)
        .astype(jnp.bfloat16)
        .reshape(sequence_length, KEY_VALUE_HEADS * HEAD_SIZE)
    )
    projected_value_gradient = summed_value_gradient.astype(jnp.bfloat16).reshape(
        sequence_length, KEY_VALUE_HEADS * HEAD_SIZE
    )
    grad_query_full = jnp.einsum(
        "td,tf->df", normed, query_raw_grad, preferred_element_type=jnp.float32
    )
    grad_key_full = jnp.einsum(
        "td,tf->df", normed, key_raw_grad, preferred_element_type=jnp.float32
    )
    grad_value_full = jnp.einsum(
        "td,tf->df", normed, projected_value_gradient, preferred_element_type=jnp.float32
    )
    normed_grad = jnp.einsum(
        "tf,df->td", query_raw_grad, back_query, preferred_element_type=jnp.float32
    )
    normed_grad = normed_grad + jnp.einsum(
        "tf,df->td", key_raw_grad, back_key, preferred_element_type=jnp.float32
    )
    normed_grad = normed_grad + jnp.einsum(
        "tf,df->td", projected_value_gradient, back_value, preferred_element_type=jnp.float32
    )
    resid_norm_grad, grad_gain_attn = norm_backward(
        normed_grad, unit_attn, inverse_attn, back_gain_attn.astype(jnp.float32)
    )
    resid_grad = middle_grad + resid_norm_grad
    grad_embedded = (embed_scale * resid_grad).astype(jnp.bfloat16)
    summed = (
        lax.psum_scatter(grad_gain_attn, ("expert", "shard"), scatter_dimension=0, tiled=True),
        lax.psum_scatter(grad_gain_ffn, ("expert", "shard"), scatter_dimension=0, tiled=True),
        lax.psum_scatter(grad_query_full, ("expert", "shard"), scatter_dimension=0, tiled=True),
        lax.psum_scatter(grad_key_full, ("expert", "shard"), scatter_dimension=0, tiled=True),
        lax.psum_scatter(grad_value_full, ("expert", "shard"), scatter_dimension=0, tiled=True),
        lax.psum_scatter(grad_out_full, ("expert", "shard"), scatter_dimension=0, tiled=True),
        lax.psum_scatter(grad_router_full, ("expert", "shard"), scatter_dimension=0, tiled=True),
    )
    return (
        output,
        grad_embedded,
        summed[0],
        summed[1],
        summed[2],
        summed[3],
        summed[4],
        summed[5],
        summed[6],
        grad_expert_in,
        grad_expert_out,
    )


BF16 = jnp.bfloat16
F32 = jnp.float32
PAIR = 2
OWN = 2


def over_expert(value, bits):
    return lax.ppermute(value, "expert", [(i, i ^ bits) for i in range(8)])


def over_shard(value, bits):
    return lax.ppermute(value, "shard", [(i, i ^ bits) for i in range(4)])


def dot_f32(left, right, dims):
    return lax.dot_general(left, right, dims, preferred_element_type=F32)


CONTRACT_LAST = (((1,), (1,)), ((), ()))
CONTRACT_FIRST = (((0,), (0,)), ((), ()))
CONTRACT_PLAIN = (((1,), (0,)), ((), ()))
BLOCKS = 8
HALF = 4
ROWS = HALF * CAP
PAY_ROWS = 288
SUM_ROWS = 272


def expert_body(first_part, packed, number_ref, *refs):
    refs = list(refs)
    take = lambda count: [refs.pop(0) for _ in range(count)]
    tok_refs, out_refs = take(BLOCKS), take(BLOCKS)
    if packed:
        (w_ref,) = take(1)
        w_in_ref, w_out_ref = w_ref.at[:, 0:256, :], w_ref.at[:, 256:384, :]
    else:
        w_in_ref, w_out_ref = take(2)
    row_before, moe_before = ([], []) if first_part else (take(BLOCKS), take(BLOCKS))
    row_outs, moe_outs = take(BLOCKS), take(BLOCKS)
    (grad_ref,) = take(1)
    (tok_s, out_s, w_in_s, w_out_s, row_s, moe_s, grad_s, x_s, g_s, gate_s, table_s, back_s, mix_s, dot_s,
     in_acc, out_acc, tok_sem, out_sem, w_sem, row_sem, moe_sem, row_out_sem, moe_out_sem, grad_sem) = refs
    number = number_ref[0]
    copy = pltpu.make_async_copy
    for j in range(BLOCKS):
        copy(tok_refs[j], tok_s.at[j], tok_sem.at[j]).start()
        copy(out_refs[j], out_s.at[j], out_sem.at[j]).start()
        if j == HALF - 1:
            copy(w_in_ref, w_in_s, w_sem.at[0]).start()
            copy(w_out_ref, w_out_s, w_sem.at[1]).start()
    if not first_part:
        for j in range(BLOCKS):
            copy(row_before[j], row_s.at[j], row_sem.at[j]).start()
            copy(moe_before[j], moe_s.at[j], moe_sem.at[j]).start()

    def mask_of(i):
        slot = lax.broadcasted_iota(jnp.int32, (CAP, 256), 0).astype(F32)
        return slot == table_s[i, 0:1, :]

    def half_step(half, _):
        for i in range(HALF):
            j = half * HALF + i
            copy(tok_s.at[j], tok_s.at[j], tok_sem.at[j]).wait()
            copy(out_s.at[j], out_s.at[j], out_sem.at[j]).wait()
            aux = tok_s[j, 256:PAY_ROWS, :].astype(F32)
            line = lax.broadcasted_iota(jnp.int32, (EXPERTS, 1024), 0)
            line = jnp.sum(jnp.where(line == number, aux, 0.0), axis=0, keepdims=True)
            table_s[i, 0:1, :] = line[:, :256]
            gate = line[:, 256:512] + line[:, 512:768] + line[:, 768:]
            mask = mask_of(i)
            pick = jnp.where(mask, 1.0, 0.0).astype(BF16)
            at = slice(i * CAP, (i + 1) * CAP)
            x_s[at, :] = dot_f32(pick, tok_s[j, 0:256, :], CONTRACT_PLAIN).astype(BF16)
            g_s[at, :] = resid_scale * dot_f32(pick, out_s[j], CONTRACT_PLAIN)
            gate_s[at, :] = jnp.sum(jnp.where(mask, gate, 0.0), axis=1, keepdims=True)

        @pl.when(half == 0)
        def _():
            copy(w_in_ref, w_in_s, w_sem.at[0]).wait()
            copy(w_out_ref, w_out_s, w_sem.at[1]).wait()

        w_in = w_in_s[...].reshape(1024, 1024)
        w_out = w_out_s[...].reshape(512, 1024)
        x = x_s[...]
        gate_up = dot_f32(x, w_in, CONTRACT_PLAIN)
        gate_part, up_part = gate_up[:, :FF], gate_up[:, FF:]
        sigmoid = jax.nn.sigmoid(gate_part)
        hidden = (gate_part * sigmoid * up_part).astype(BF16)
        produced = dot_f32(hidden, w_out, CONTRACT_PLAIN).astype(BF16).astype(F32)
        slot_gate = gate_s[...]
        scaled = g_s[...]
        slot_grad = (slot_gate * scaled).astype(BF16)
        dot_s[...] = jnp.sum(produced * scaled, axis=1, keepdims=True)
        mix_s[...] = (slot_gate * produced).astype(BF16)
        hidden_grad = dot_f32(slot_grad, w_out, CONTRACT_LAST)
        gate_grad = hidden_grad * up_part * sigmoid * (1.0 + gate_part * (1.0 - sigmoid))
        up_grad = hidden_grad * gate_part * sigmoid
        gate_up_grad = jnp.concatenate([gate_grad.astype(BF16), up_grad.astype(BF16)], axis=1)
        back_s[...] = dot_f32(gate_up_grad, w_in, CONTRACT_LAST).astype(BF16)
        in_part = dot_f32(x, gate_up_grad, CONTRACT_FIRST)
        out_part = dot_f32(hidden, slot_grad, CONTRACT_FIRST)

        @pl.when(half == 0)
        def _():
            in_acc[...] = in_part
            out_acc[...] = out_part

        @pl.when(half == 1)
        def _():
            for d in range(4):
                wide, narrow = slice(d * 256, (d + 1) * 256), slice(d * 128, (d + 1) * 128)
                grad_s[d, 0:256, :] = (in_acc[wide, :] + in_part[wide, :]).astype(BF16)
                grad_s[d, 256:384, :] = (out_acc[narrow, :] + out_part[narrow, :]).astype(BF16)
            copy(grad_s, grad_ref, grad_sem.at[0]).start()

        for i in range(HALF):
            j = half * HALF + i
            at = slice(i * CAP, (i + 1) * CAP)
            mask = mask_of(i)
            pick = jnp.where(mask, 1.0, 0.0).astype(BF16)
            rows = dot_f32(pick, back_s[at, :], CONTRACT_FIRST)
            mixed = dot_f32(pick, mix_s[at, :], CONTRACT_FIRST)
            dots = jnp.sum(jnp.where(mask, dot_s[at, :], 0.0), axis=0, keepdims=True)
            high = dots.astype(BF16).astype(F32)
            low = dots - high
            wide = jnp.concatenate([high, high, low, low], axis=1)
            line = lax.broadcasted_iota(jnp.int32, (16, 1024), 0)
            lane = lax.broadcasted_iota(jnp.int32, (16, 1024), 1) // 256
            here = (line == number % 16) & (lane % 2 == number // 16)
            side = jnp.where(here, jnp.broadcast_to(wide, (16, 1024)), 0.0)
            if not first_part:
                copy(row_s.at[j], row_s.at[j], row_sem.at[j]).wait()
                copy(moe_s.at[j], moe_s.at[j], moe_sem.at[j]).wait()
                rows = rows + row_s[j, 0:256, :].astype(F32)
                mixed = mixed + moe_s[j].astype(F32)
                side = side + row_s[j, 256:SUM_ROWS, :].astype(F32)
            row_s[j, 0:256, :] = rows.astype(BF16)
            row_s[j, 256:SUM_ROWS, :] = side.astype(BF16)
            moe_s[j] = mixed.astype(BF16)
            for part in range(2):

                @pl.when(half == part)
                def _():
                    k = part * HALF + i
                    copy(row_s.at[k], row_outs[k], row_out_sem.at[k]).start()
                    copy(moe_s.at[k], moe_outs[k], moe_out_sem.at[k]).start()

        return 0

    lax.fori_loop(0, 2, half_step, 0)
    copy(grad_s, grad_ref, grad_sem.at[0]).wait()
    for j in range(BLOCKS):
        copy(row_s.at[j], row_outs[j], row_out_sem.at[j]).wait()
        copy(moe_s.at[j], moe_outs[j], moe_out_sem.at[j]).wait()


def expert_call(number, tokens, grads, weights, before=None):
    operands = list(tokens) + list(grads) + list(weights) + ([] if before is None else list(before))
    block = lambda rows: jax.ShapeDtypeStruct((rows, 1024), BF16)
    outs = [block(SUM_ROWS)] * BLOCKS + [block(256)] * BLOCKS + [jax.ShapeDtypeStruct((4, 384, 1024), BF16)]
    anywhere = pl.BlockSpec(memory_space=pl.ANY)
    blocks = lambda rows: pltpu.VMEM((BLOCKS, rows, 1024), BF16)
    column, wide = pltpu.VMEM((ROWS, 1), F32), pltpu.VMEM((ROWS, 1024), BF16)
    sems = [pltpu.SemaphoreType.DMA((count,)) for count in (8, 8, 2, 8, 8, 8, 8, 1)]
    results = pl.pallas_call(
        functools.partial(expert_body, before is None, len(weights) == 1),
        out_shape=outs,
        in_specs=[pl.BlockSpec(memory_space=pltpu.SMEM)] + [anywhere] * len(operands),
        out_specs=[anywhere] * len(outs),
        scratch_shapes=[
            blocks(PAY_ROWS), blocks(256), pltpu.VMEM((4, 256, 1024), BF16), pltpu.VMEM((4, 128, 1024), BF16),
            blocks(SUM_ROWS), blocks(256),
            pltpu.VMEM((4, 384, 1024), BF16), wide, pltpu.VMEM((ROWS, 1024), F32), column,
            pltpu.VMEM((HALF, 8, 256), F32), wide, wide, column,
            pltpu.VMEM((1024, 1024), F32), pltpu.VMEM((512, 1024), F32),
        ] + sems,
        compiler_params=pltpu.CompilerParams(vmem_limit_bytes=60 * 1024 * 1024),
        cost_estimate=pl.CostEstimate(
            flops=1000, bytes_accessed=1000, transcendentals=0
        ),
        name="expert",
    )(number, *operands)
    return results[: 2 * BLOCKS], results[2 * BLOCKS]


LANES = 128
GAIN_ATTN = 32
GAIN_FFN = 33
SEQUENCE = 256


def group_of(e, r):
    return pl.ds(pl.multiple_of((e ^ r) * LANES, LANES), LANES)


def turn_halves(value):
    lane = lax.broadcasted_iota(jnp.int32, value.shape, 1) % HEAD_SIZE
    width = value.shape[1]
    return jnp.where(
        lane < HEAD_SIZE // 2,
        -pltpu.roll(value, width - HEAD_SIZE // 2, 1),
        pltpu.roll(value, HEAD_SIZE // 2, 1),
    )


def wide_table(table, width):
    return jnp.concatenate([table] * (width // LANES), axis=1)


def inverse_rms(value):
    return lax.rsqrt(jnp.mean(value * value, axis=1, keepdims=True) + norm_eps)


def attention_probs(queries, keys, allowed):
    scores = jnp.where(allowed, dot_f32(queries, keys, CONTRACT_LAST) * attn_scale, -1e30)
    exps = jnp.exp(scores - jnp.max(scores, axis=1, keepdims=True))
    return exps / jnp.sum(exps, axis=1, keepdims=True)


def allowed_of(column_ref, row_ref):
    shape = (2 * SEQUENCE, SEQUENCE)
    query = lax.broadcasted_iota(jnp.int32, shape, 0) % SEQUENCE
    key = lax.broadcasted_iota(jnp.int32, shape, 1)
    column = column_ref[...]
    same = jnp.concatenate([column, column], axis=0) == row_ref[...]
    return (key <= query) & same


def heads_of(block, first, count):
    return jnp.concatenate(
        [block[:, HEAD_SIZE * (first + i) : HEAD_SIZE * (first + i + 1)] for i in range(count)], axis=0
    )


def stacked(refs, a, b):
    return jnp.concatenate([ref[:, a:b] for ref in refs], axis=0)


def gain_row(refs, index):
    return stacked(refs, 1024, 1152).astype(F32).T[index : index + 1, :]


def attend_body(e_ref, x_ref, column_ref, row_ref, cos_ref, sin_ref, *refs):
    lefts, rights = (refs[0:4], refs[4:8]), (refs[8:12], refs[12:16])
    normed_ref, q_ref, k_ref, v_ref, mixed_ref, small_ref = refs[16:]
    e = e_ref[0]
    resid = embed_scale * x_ref[...].astype(F32)
    inverse = inverse_rms(resid)
    for part in range(2):
        gain = gain_row(lefts[part], GAIN_ATTN)
        for q in range(4):
            group = group_of(e, 2 * q + part)
            block = embed_scale * x_ref[:, group].astype(F32)
            scaled = block * inverse * gain[:, LANES * q : LANES * (q + 1)]
            at = 512 * part + LANES * q
            normed_ref[:, at : at + LANES] = scaled.astype(BF16)
            small_ref[group, :] = lefts[part][q][:, 1024:1152]
    own = normed_ref[:, :512]
    far = normed_ref[:, 512:]
    project = lambda sides, a, b: dot_f32(own, stacked(sides[0], a, b), CONTRACT_PLAIN) + dot_f32(
        far, stacked(sides[1], a, b), CONTRACT_PLAIN
    )
    rotate = lambda u: u * wide_table(cos_ref[...], u.shape[1]) + turn_halves(u) * wide_table(
        sin_ref[...], u.shape[1]
    )
    q_ref[...] = rotate(project(lefts, 0, 1024)).astype(BF16)
    k_ref[...] = rotate(project(rights, 0, 512)).astype(BF16)
    v_ref[...] = project(rights, 512, 1024).astype(BF16)
    allowed = allowed_of(column_ref, row_ref)

    def pair(step, _):
        wide = pl.ds(pl.multiple_of(step * 256, 256), 256)
        narrow = pl.ds(pl.multiple_of(step * LANES, LANES), LANES)
        q_block, k_block, v_block = q_ref[:, wide], k_ref[:, narrow], v_ref[:, narrow]
        outs = []
        for i in range(2):
            probs = attention_probs(heads_of(q_block, 2 * i, 2), heads_of(k_block, i, 1), allowed)
            rows = dot_f32(probs.astype(BF16), heads_of(v_block, i, 1), CONTRACT_PLAIN)
            outs += [rows[:SEQUENCE], rows[SEQUENCE:]]
        mixed_ref[:, wide] = jnp.concatenate(outs, axis=1).astype(BF16)
        return 0

    lax.fori_loop(0, 4, pair, 0)


def route_body(e_ref, x_ref, mixed_ref, small_ref, code_ref, *refs):
    w_refs, (pay_ref, gates_ref, middle_ref) = (refs[0:4], refs[4:8]), refs[8:]
    e = e_ref[0]
    total = jnp.zeros((SEQUENCE, 1024), F32)
    for part in range(2):
        features = jnp.concatenate([mixed_ref[:, group_of(e, 2 * q + part)] for q in range(4)], axis=1)
        total = total + dot_f32(features, stacked(w_refs[part], 0, 1024), CONTRACT_PLAIN)
    middle = embed_scale * x_ref[...].astype(F32) + resid_scale * total
    middle_ref[...] = middle
    gain = small_ref[...].astype(F32).T[GAIN_FFN : GAIN_FFN + 1, :]
    normed2 = (middle * inverse_rms(middle) * gain).astype(BF16)
    pay_ref[0:256, :] = normed2
    logits = dot_f32(normed2, small_ref[...], CONTRACT_PLAIN)
    code = code_ref[...]
    member = code >= 0.0
    masked = jnp.where(member, logits, -1e30)
    raised = jnp.where(member, jnp.exp(masked - jnp.max(masked, axis=1, keepdims=True)), 0.0)
    gates = raised / jnp.sum(raised, axis=1, keepdims=True)
    gates_ref[...] = gates
    rows = lambda value: value.T[:EXPERTS, :]
    turned = rows(gates)
    high = turned.astype(BF16).astype(F32)
    middle_part = (turned - high).astype(BF16).astype(F32)
    low = turned - high - middle_part
    pay_ref[256:288, :] = jnp.concatenate([rows(code), high, middle_part, low], axis=1).astype(BF16)


def turn_body(e_ref, sum_ref, mine_ref, other_ref, add_ref, grad_ref, middle_ref, gates_ref, small_ref, normed2_ref, mixed_ref,
              *refs):
    w_refs, (own_ref, far_ref, mixed_grad_ref, middle_grad_ref, side_ref) = (refs[0:4], refs[4:8]), refs[8:]
    e = e_ref[0]
    addends = (sum_ref, mine_ref, other_ref, add_ref)
    upstream = sum(ref[0:256, :].astype(F32) for ref in addends)
    table = sum(ref[256:272, :].astype(F32) for ref in addends)
    dots = jnp.concatenate([table[:, :256], table[:, 256:512]], axis=0) + jnp.concatenate(
        [table[:, 512:768], table[:, 768:]], axis=0
    )
    dots = jnp.concatenate([dots, jnp.zeros((LANES - EXPERTS, SEQUENCE), F32)], axis=0).T
    gates = gates_ref[...]
    logit_grads = (gates * (dots - jnp.sum(gates * dots, axis=1, keepdims=True))).astype(BF16)
    small = small_ref[...]
    upstream = upstream + dot_f32(logit_grads, small, CONTRACT_LAST)
    middle = middle_ref[...]
    inverse = inverse_rms(middle)
    unit = middle * inverse
    gain = small.astype(F32).T[GAIN_FFN : GAIN_FFN + 1, :]
    gain_grad = jnp.sum(upstream * unit, axis=0, keepdims=True)
    scaled = upstream * gain
    middle_grad = grad_ref[...].astype(F32) + inverse * (
        scaled - unit * jnp.mean(scaled * unit, axis=1, keepdims=True)
    )
    middle_grad_ref[...] = middle_grad
    attn_grad = (resid_scale * middle_grad).astype(BF16)
    line = lax.broadcasted_iota(jnp.int32, (LANES, 1024), 0)
    side_ref[...] = dot_f32(normed2_ref[0:256, :], logit_grads, CONTRACT_FIRST) + jnp.where(
        line == GAIN_FFN, gain_grad, 0.0
    ).T
    for part, out_ref in ((0, own_ref), (1, far_ref)):
        features = jnp.concatenate([mixed_ref[:, group_of(e, 2 * q + part)] for q in range(4)], axis=1)
        out_ref[:, :1024] = dot_f32(features, attn_grad, CONTRACT_FIRST).astype(BF16)
        back = dot_f32(attn_grad, stacked(w_refs[part], 0, 1024), CONTRACT_LAST).astype(BF16)
        for q in range(4):
            mixed_grad_ref[:, group_of(e, 2 * q + part)] = back[:, LANES * q : LANES * (q + 1)]
            at = slice(LANES * q, LANES * (q + 1))
            out_ref[at, 1024:] = side_ref[group_of(e, 2 * q + part), :].astype(BF16)


def attend_back_body(e_ref, x_ref, column_ref, row_ref, cos_ref, sin_ref, q_ref, k_ref, v_ref, grad_ref,
                     normed_ref, middle_grad_ref, *refs):
    lefts, rights = (refs[0:4], refs[4:8]), (refs[8:12], refs[12:16])
    left_refs, right_refs = refs[16:18], refs[18:20]
    embed_ref, raw_ref, scaled_ref = refs[20:]
    e = e_ref[0]
    allowed = allowed_of(column_ref, row_ref)
    unrotate = lambda u: (
        u * wide_table(cos_ref[...], u.shape[1]) - turn_halves(u) * wide_table(sin_ref[...], u.shape[1])
    ).astype(BF16)

    def pair(step, _):
        wide = pl.ds(pl.multiple_of(step * 256, 256), 256)
        narrow = lambda base: pl.ds(pl.multiple_of(base + step * LANES, LANES), LANES)
        q_block, d_block = q_ref[:, wide], grad_ref[:, wide]
        k_block, v_block = k_ref[:, narrow(0)], v_ref[:, narrow(0)]
        q_outs, k_outs, v_outs = [], [], []
        for i in range(2):
            queries, keys = heads_of(q_block, 2 * i, 2), heads_of(k_block, i, 1)
            upstream = heads_of(d_block, 2 * i, 2)
            probs = attention_probs(queries, keys, allowed)
            prob_grads = dot_f32(upstream, heads_of(v_block, i, 1), CONTRACT_LAST)
            centre = jnp.sum(probs * prob_grads, axis=1, keepdims=True)
            score_grads = (probs * (prob_grads - centre)).astype(BF16)
            rows = dot_f32(score_grads, keys, CONTRACT_PLAIN) * attn_scale
            q_outs += [rows[:SEQUENCE], rows[SEQUENCE:]]
            k_outs.append(dot_f32(score_grads, queries, CONTRACT_FIRST) * attn_scale)
            v_outs.append(dot_f32(probs.astype(BF16), upstream, CONTRACT_FIRST))
        raw_ref[:, wide] = unrotate(jnp.concatenate(q_outs, axis=1))
        raw_ref[:, narrow(1024)] = unrotate(jnp.concatenate(k_outs, axis=1))
        raw_ref[:, narrow(1536)] = jnp.concatenate(v_outs, axis=1).astype(BF16)
        return 0

    lax.fori_loop(0, 4, pair, 0)
    resid = embed_scale * x_ref[...].astype(F32)
    inverse = inverse_rms(resid)
    for part in range(2):
        half = normed_ref[:, 512 * part : 512 * part + 512]
        for c in range(2):
            at = slice(512 * c, 512 * c + 512)
            left_refs[part][:, at] = dot_f32(half, raw_ref[:, at], CONTRACT_FIRST).astype(BF16)
            right_refs[part][:, at] = dot_f32(
                half, raw_ref[:, 1024 + 512 * c : 1536 + 512 * c], CONTRACT_FIRST
            ).astype(BF16)
        back = dot_f32(raw_ref[:, :1024], stacked(lefts[part], 0, 1024), CONTRACT_LAST) + dot_f32(
            raw_ref[:, 1024:], stacked(rights[part], 0, 1024), CONTRACT_LAST
        )
        gain = gain_row(lefts[part], GAIN_ATTN)
        gain_grads = []
        for q in range(4):
            at = slice(LANES * q, LANES * (q + 1))
            group = group_of(e, 2 * q + part)
            unit = embed_scale * x_ref[:, group].astype(F32) * inverse
            gain_grads.append(jnp.sum(back[:, at] * unit, axis=0, keepdims=True))
            scaled_ref[:, group] = back[:, at] * gain[:, at]
        line = lax.broadcasted_iota(jnp.int32, (LANES, 512), 0)
        side = jnp.where(line == GAIN_ATTN, jnp.concatenate(gain_grads, axis=1), 0.0).T
        left_refs[part][:, 1024:] = side.astype(BF16)
    unit = resid * inverse
    scaled = scaled_ref[...]
    resid_grad = middle_grad_ref[...] + inverse * (
        scaled - unit * jnp.mean(scaled * unit, axis=1, keepdims=True)
    )
    embed_ref[...] = (embed_scale * resid_grad).astype(BF16)


def local_kernel(body, name, outs, scratch, number, *operands):
    vmem = pl.BlockSpec(memory_space=pltpu.VMEM)
    return pl.pallas_call(
        body,
        out_shape=[jax.ShapeDtypeStruct(shape, dtype) for shape, dtype in outs],
        in_specs=[pl.BlockSpec(memory_space=pltpu.SMEM)] + [vmem] * len(operands),
        out_specs=[vmem] * len(outs),
        scratch_shapes=[pltpu.VMEM(shape, dtype) for shape, dtype in scratch],
        compiler_params=pltpu.CompilerParams(vmem_limit_bytes=56 * 1024 * 1024),
        cost_estimate=pl.CostEstimate(flops=1000, bytes_accessed=1000, transcendentals=0),
        name=name,
    )(number, *operands)


def together(*values):
    return lax.optimization_barrier(values)


def core_sum(own, far):
    return (own.astype(F32) + over_expert(far, 1).astype(F32)).astype(BF16)


def xor_order(pieces, at):
    stacked = jnp.stack(pieces)
    return jnp.concatenate(
        [lax.dynamic_index_in_dim(stacked, at ^ i, 0, keepdims=False) for i in range(len(pieces))]
    )


def exchange(slices):
    return lax.all_to_all(slices, "shard", split_axis=0, concat_axis=0, tiled=True)


def expert_slices(weights, part):
    return jnp.stack([weights[OWN * (d % PAIR) + part] for d in range(4)])


def over_x(value):
    return over_expert(value, 2)


def over_y(value):
    return over_expert(value, 4)


def spread(value, first, second):
    near = {first: first(value), second: second(value)}
    return [value, near[over_x], near[over_y], second(near[first])]


def bf_sum(*values):
    return sum(value.astype(F32) for value in values).astype(BF16)


def pack_body(query_ref, key_ref, value_ref, router_ref, attn_ref, ffn_ref, out_ref, pack_ref):
    pack_ref[:, 0:1024] = query_ref[...].astype(BF16)
    row = lax.broadcasted_iota(jnp.int32, (32, 32), 0)
    diagonal = row == lax.broadcasted_iota(jnp.int32, (32, 32), 1)
    upright = lambda ref: jnp.sum(jnp.where(diagonal, ref[...], 0.0), axis=1, keepdims=True)
    zeros = jnp.zeros((32, LANES - EXPERTS - 2), F32)
    small = jnp.concatenate([router_ref[...], upright(attn_ref), upright(ffn_ref), zeros], axis=1)
    pack_ref[:, 1024:1152] = small.astype(BF16)
    pack_ref[:, 1152:1664] = key_ref[...].astype(BF16)
    pack_ref[:, 1664:2176] = value_ref[...].astype(BF16)
    pack_ref[:, 2176:] = out_ref[...].astype(BF16)


def plane_body(z_ref, *refs):
    z = z_ref[0]
    for group, (a, b) in enumerate(((0, 1152), (1152, 2176), (2176, 3328))):
        mine, one, other = refs[3 * group : 3 * group + 3]
        for k in range(4):
            rows = pl.ds(pl.multiple_of((z ^ k) * 32, 32), 32)
            total = mine[rows, :].astype(F32) + one[rows, :].astype(F32) + other[rows, :].astype(F32)
            refs[9 + k][:, a:b] = total.astype(BF16)


def settle_body(z_ref, *refs):
    sources, outs = refs[:4], refs[4:]
    total = lambda a, b: sum(ref[:, a:b].astype(F32) for ref in sources)
    bounds = ((0, 1024), (1152, 1664), (1664, 2176), (2176, 3200))
    for out_ref, (a, b) in zip(outs, bounds):
        out_ref[...] = total(a, b)
    row = lax.broadcasted_iota(jnp.int32, (32, 32), 0)
    diagonal = row == lax.broadcasted_iota(jnp.int32, (32, 32), 1)
    flat = lambda column: jnp.sum(jnp.where(diagonal, column, 0.0), axis=0, keepdims=True)
    late, early = total(1024, 1152), total(3200, 3328)
    outs[4][...] = early[:, :EXPERTS]
    outs[5][...] = flat(late[:, GAIN_ATTN : GAIN_ATTN + 1])
    outs[6][...] = flat(early[:, GAIN_FFN : GAIN_FFN + 1])


def owner_body(first_part, one_ref, two_ref, *refs):
    in_ref, out_ref = refs if first_part else refs[2:]
    total = one_ref[...].astype(F32) + two_ref[...].astype(F32)
    in_ref[...] = total[:, :256]
    out_ref[...] = total[:, 256:]


def owner_sum(part, slices, before=()):
    block = lambda rows, at: pl.BlockSpec((1, rows, 1024), lambda d: (at(d), 0, 0))
    place = lambda d: 2 * d + part
    return pl.pallas_call(
        functools.partial(owner_body, not before),
        out_shape=[jax.ShapeDtypeStruct((4, rows, 1024), F32) for rows in (256, 128)],
        grid=(2,),
        in_specs=[block(384, lambda d: d), block(384, lambda d: d + 2)]
        + [pl.BlockSpec(memory_space=pl.ANY)] * len(before),
        out_specs=[block(256, place), block(128, place)],
        input_output_aliases={2: 0, 3: 1} if before else {},
        name="owner_sum",
    )(slices, slices, *before)


def plane_fold(total, first, second):
    part = lambda q: total[128 * q : 128 * (q + 1)]
    one, two = (1, 2) if first is over_x else (2, 1)
    passing, mine = first(part(3)), first(part(one))
    return [part(0), mine, second(bf_sum(part(two), passing))]


def pack_call(*operands):
    return pl.pallas_call(
        pack_body,
        out_shape=jax.ShapeDtypeStruct((32, 3200), BF16),
        in_specs=[pl.BlockSpec(memory_space=pltpu.VMEM)] * len(operands),
        out_specs=pl.BlockSpec(memory_space=pltpu.VMEM),
        name="pack",
    )(*operands)


def per_device_fast(
    embedded,
    document_numbers,
    expert_ids,
    attn_gain,
    ffn_gain,
    w_query,
    key_projection,
    value_projection,
    w_out,
    w_router,
    expert_in,
    expert_out,
    cotangent,
):
    e = lax.axis_index("expert")
    z = lax.axis_index("shard")
    place = e.reshape(1)
    pack = pack_call(
        w_query, key_projection, value_projection, w_router, attn_gain[None, :], ffn_gain[None, :], w_out
    )
    pack, grad_early = together(pack, cotangent)
    plane = xor_order([pack] + [over_shard(pack, k) for k in (1, 2, 3)], z)
    out_pair = over_shard(grad_early, 1)
    out_x, out_y = over_x(grad_early), over_y(grad_early)
    slices = [
        jnp.concatenate([expert_slices(w, part) for w in (expert_in, expert_out)], axis=1)
        for part in range(OWN)
    ]
    plane, out_x, out_y, slices[0] = together(plane, out_x, out_y, slices[0])
    left = spread(plane[:, :1152], over_x, over_y)
    right = spread(plane[:, 1152:2176], over_y, over_x)
    slices[0], out_pair, left[1], right[2] = together(slices[0], out_pair, left[1], right[2])
    weights0 = exchange(slices[0])
    swap = lambda values: [over_expert(value, 1) for value in values]
    left_far, right_far = swap(left), swap(right)
    left[3], right[3], plane, out_pair, out_x = together(left[3], right[3], plane, out_pair, out_x)
    out_w = [plane[:, 2176:]] + [over_expert(plane[:, 2176:], bits) for bits in (2, 4, 6)]
    out_blocks = [cotangent, out_x, out_y, over_y(out_x), out_pair, over_x(out_pair), over_y(out_pair)]

    segments = document_numbers[0]
    column, row = segments[:, None], segments[None, :]
    cosine, sine = (jnp.concatenate([table] * 4, axis=1) for table in rope_tables(segments))
    lanes = jnp.arange(LANES, dtype=jnp.int32)
    member = jnp.any(expert_ids[:, :, None] == lanes, axis=1)
    index = jnp.arange(SEQUENCE, dtype=jnp.int32)
    below = (index[None, :] < index[:, None]).astype(BF16)
    rank = jnp.dot(below, member.astype(BF16), preferred_element_type=F32)
    code = jnp.where(member, rank, -1.0)

    wide, half = (SEQUENCE, 1024), (SEQUENCE, 512)
    weights = left + left_far + right + right_far
    normed, queries, keys, values, mixed, small_all = local_kernel(
        attend_body, "attend",
        [(wide, BF16), (wide, BF16), (half, BF16), (half, BF16), (wide, BF16), ((1024, LANES), BF16)], [],
        place, embedded, column, row, cosine, sine, *weights,
    )
    *out_w, mixed = together(*out_w, mixed)
    out_w = out_w + swap(out_w)
    payload, gates, middle = local_kernel(
        route_body, "route", [((288, 1024), BF16), ((SEQUENCE, LANES), F32), (wide, F32)], [],
        place, embedded, mixed, small_all, code, *out_w,
    )
    pay_pair = over_shard(payload, 1)
    pay_x, pay_y = over_x(payload), over_y(payload)
    pay_x, pay_y, pay_pair, *out_blocks = together(pay_x, pay_y, pay_pair, *out_blocks)
    slices[1], weights0, pay_pair = together(slices[1], weights0, pay_pair)
    weights1 = [exchange(slices[1])]
    out_blocks.append(over_x(out_blocks[6]))
    tok_own = [payload, pay_x, pay_y, over_y(pay_x)]
    tok_pair = [pay_pair, over_x(pay_pair), over_y(pay_pair)]
    tok_pair[2], out_blocks[7] = together(tok_pair[2], out_blocks[7])
    tok_pair.append(over_x(tok_pair[2]))
    weights0 = [weights0]
    weights0_far = swap(weights0)
    tokens = tok_own + tok_pair
    first = (e * 4 + z % PAIR * OWN).reshape(1)
    first_far = ((e ^ 1) * 4 + z % PAIR * OWN).reshape(1)
    sums, grad_b = expert_call(first_far, tokens, out_blocks, weights0_far)
    sums, grad_a = expert_call(first, tokens, out_blocks, weights0, sums)
    expert_grad0 = core_sum(grad_a, grad_b)
    expert_grad0, *weights1 = together(expert_grad0, *weights1)
    slices0 = exchange(expert_grad0)
    weights1_far = swap(weights1)
    sums, grad_d = expert_call(first_far + 1, tokens, out_blocks, weights1_far, sums)
    sums, grad_c = expert_call(first + 1, tokens, out_blocks, weights1, sums)
    rows, moes = sums[:BLOCKS], sums[BLOCKS:]
    expert_grad1 = core_sum(grad_c, grad_d)
    own, pair = rows[:4], rows[4:]
    pair_pass, own_pass = over_x(pair[3]), over_y(own[3])
    pair_mine = over_x(pair[1])
    pair_pass, expert_grad1 = together(pair_pass, expert_grad1)
    pair_other = over_y(bf_sum(pair[2], pair_pass))
    mine, pair_pass, slices0 = together(own[2], pair_pass, slices0)
    own_mine = over_y(mine)
    own_other = over_x(bf_sum(own[1], own_pass))
    row_pair = bf_sum(pair[0], pair_mine, pair_other)
    returned = over_shard(row_pair, 1)
    row_pair, *moes = together(row_pair, *moes)
    moe_pass, moe_own_pass = over_x(moes[7]), over_y(moes[3])
    moe_mine, moe_own_mine = over_x(moes[5]), over_y(moes[2])
    owned = owner_sum(0, slices0)
    own_other, *owned = together(own_other, *owned)
    own_other, expert_grad1 = together(own_other, expert_grad1)
    slices1 = exchange(expert_grad1)
    early_own, early_far, mixed_grad, middle_grad = local_kernel(
        turn_body, "turn", [((512, 1152), BF16), ((512, 1152), BF16), (wide, BF16), (wide, F32)],
        [((1024, LANES), F32)], place, own[0], own_mine, own_other, returned, cotangent, middle, gates,
        small_all, payload, mixed, *out_w,
    )
    moe_rest, moe_own_rest = over_y(bf_sum(moes[6], moe_pass)), over_x(bf_sum(moes[1], moe_own_pass))
    left_own, left_far, right_own, right_far, grad_embedded = local_kernel(
        attend_back_body, "attend_back", [((512, 1152), BF16)] * 2 + [((512, 1024), BF16)] * 2 + [(wide, BF16)],
        [((SEQUENCE, 2048), BF16), (wide, F32)], place, embedded, column, row, cosine, sine,
        queries, keys, values, mixed_grad, normed, middle_grad, *weights,
    )
    left_far, right_far, moe_rest, moe_own_rest, moe_mine, moe_own_mine = together(
        left_far, right_far, moe_rest, moe_own_rest, moe_mine, moe_own_mine
    )
    moe_pair = bf_sum(moes[4], moe_mine, moe_rest)
    moe_own = bf_sum(moes[0], moe_own_mine, moe_own_rest)
    moe_other = over_shard(moe_pair, 1)
    addends = plane_fold(core_sum(left_own, left_far), over_x, over_y)
    addends += plane_fold(core_sum(right_own, right_far), over_y, over_x)
    addends += plane_fold(core_sum(early_own, early_far), over_y, over_x)
    planes = local_kernel(plane_body, "plane", [((32, 3328), BF16)] * 4, [], z.reshape(1), *addends)
    planes = list(planes)
    planes[3], slices1 = together(planes[3], slices1)
    planes = [planes[0]] + [over_shard(planes[k], k) for k in (1, 2, 3)]
    shapes = [(32, 1024), (32, 512), (32, 512), (32, 1024), (32, EXPERTS), (1, 32), (1, 32)]
    late_query, late_key, late_value, early_out, router, gain_attn, gain_ffn = local_kernel(
        settle_body, "settle", [(shape, F32) for shape in shapes], [], z.reshape(1), *planes
    )
    grad_expert_in, grad_expert_out = owner_sum(1, slices1, owned)
    moe = moe_own.astype(F32) + moe_other.astype(F32)
    output = (middle + resid_scale * moe).astype(BF16)
    return (
        output,
        grad_embedded,
        gain_attn[0],
        gain_ffn[0],
        late_query,
        late_key,
        late_value,
        early_out,
        router,
        grad_expert_in,
        grad_expert_out,
    )


def solution(mesh):
    owners, shards = mesh.shape["expert"], mesh.shape["shard"]
    fast = owners == 8 and shards == 4
    both = ("expert", "shard")
    rows = P(both, None)
    weights = P("expert", "shard", None)
    return jax.shard_map(
        per_device_fast if fast else per_device_general,
        mesh=mesh,
        in_specs=(rows,) * 3 + (P(both),) * 2 + (rows,) * 5 + (weights,) * 2 + (rows,),
        out_specs=(rows,) * 2 + (P(both),) * 2 + (rows,) * 5 + (weights,) * 2,
        check_vma=False,
    )
```
